32 devices in a mesh: grp: 2 (over y), seq: 4 (over x, core), sub: 4 (over z).
Axes of the slice: x: 2, y: 2, z: 4, core: 2. Of those that a mesh axis runs over, the one named last changes fastest.
Arguments:
- events: bfloat16 [4096, 1024], P(('grp', 'seq', 'sub')), parts along dimension 0, may hold values from -36 to 36
- offsets: int32 [4096], P(('grp', 'seq', 'sub')), parts along dimension 0, may hold values from 0 to 2047
- cotangent: bfloat16 [4096, 1024], P(('grp', 'seq', 'sub')), parts along dimension 0, may hold values from -6 to 6
- query_weight: bfloat16 [1024, 1024], P('sub'), may hold values from -0.1875 to 0.1875
- key_weight: bfloat16 [1024, 1024], P('sub'), may hold values from -0.1875 to 0.1875
- value_weight: bfloat16 [1024, 1024], P('sub'), may hold values from -0.1875 to 0.1875
- omega: bfloat16 [8, 128, 256], replicated, may hold values from -0.5 to 0.5
Outputs:
- grad_events: bfloat16 [4096, 1024], P(('grp', 'seq', 'sub')), parts along dimension 0
The draws below stay inside these ranges and needn't reach their ends.
There are 2 independent parts, one for each index of `grp`. The reference program is written for one: setup_inputs(seed, part) draws one part's arguments, and reference() takes and returns one part's arrays. A program takes and returns all parts, laid end to end along the dimension named above; an argument that names none is the same for every part. Nothing has to cross between parts.
All inputs are finite; a program needn't handle non-finite values.
Results may differ from the reference program's by a relative error of at most 0.012.
Values may be sent and summed in bfloat16 or wider, within the bound.
A program may use at most 64 MiB of HBM per device.

```python
import math
import jax
import jax.numpy as jnp
from jax import lax

D = 1024
H = 8
M = 256
TOK_DEV = 128
HD = 128
TOKENS = 2048
N_SUB = 4


def draw_events(key, part):
    block_count = TOKENS // TOK_DEV
    ranks = jax.random.permutation(jax.random.fold_in(key, 11), block_count).astype(jnp.float32)
    scales = 0.5 * jnp.exp(ranks / max(block_count - 1, 1) * jnp.log(12.0))
    noise_key = jax.random.fold_in(key, 12)
    noise = jnp.clip(jax.random.normal(noise_key, (block_count, TOK_DEV, D), jnp.float32), -6.0, 6.0)
    values = noise * scales[:, None, None]
    return values.reshape(TOKENS, D).astype(jnp.bfloat16)


def plant(array, stream_key, smallest, top_value):
    longest = array.shape.index(max(array.shape))
    spots = []
    for shift in (0, 1):
        where = [jax.random.randint(jax.random.fold_in(stream_key, axis), (), 0, length) for axis, length in enumerate(array.shape)]
        where[longest] = (where[longest] + shift) % array.shape[longest]
        spots.append(tuple(where))
    return array.at[spots[0]].set(smallest).at[spots[1]].set(top_value)


def levels(rng, extent, split, least, high):
    def one(axis_at, blocks):
        draws = jax.random.uniform(jax.random.fold_in(jax.random.fold_in(rng, 6), axis_at), (blocks,), jnp.float32, least / len(split), high / len(split))
        return jnp.repeat(jnp.exp(draws), extent[axis_at] // blocks).reshape((-1,) + (1,) * (len(extent) - axis_at - 1))

    factor_of = one(*split[0])
    for cut in split[1:]:
        factor_of = factor_of * one(*cut)
    return factor_of


def bell_draw(rng, extent, spread, reach, pieces=(), held_as=jnp.bfloat16):
    entries = spread * jax.random.normal(rng, extent, jnp.float32)
    if pieces:
        entries = entries * levels(rng, extent, pieces, -0.22, 0.18)
    return jnp.clip(entries, -reach, reach).astype(held_as)


def setup_inputs(seed: int = 0, part: int = 0) -> dict:
    keys = jax.random.split(jax.random.key(seed), 8)
    own_keys = jax.random.split(jax.random.fold_in(keys[7], part), 8)
    return {
        "events": draw_events(jax.random.fold_in(jax.random.fold_in(keys[7], part), 71), part),
        "offsets": plant(jax.random.randint(own_keys[1], (TOKENS,), 0, 2048), jax.random.fold_in(own_keys[1], 1), 0, 2047).astype(jnp.int32),
        "cotangent": bell_draw(own_keys[2], (TOKENS, D), 1.0, 6.0, ((0, 16),)),
        "query_weight": bell_draw(keys[3], (D, D), D ** -0.5, 0.1875, ((0, 4),)),
        "key_weight": bell_draw(keys[4], (D, D), D ** -0.5, 0.1875, ((0, 4),)),
        "value_weight": bell_draw(keys[5], (D, D), D ** -0.5, 0.1875, ((0, 4),)),
        "omega": bell_draw(keys[6], (H, HD, M), HD ** -0.5, 0.5),
    }


def encode(events, offsets):
    half_width = events.shape[1] // 2
    indices = jnp.arange(half_width, dtype=jnp.float32)
    frequency = jnp.exp(indices * (-2.0 * math.log(10000.0) / events.shape[1]))
    angles = offsets.astype(jnp.float32)[:, None] * frequency[None, :]
    encoding = jnp.concatenate([jnp.sin(angles), jnp.cos(angles)], axis=1)
    return (events.astype(jnp.float32) + encoding).astype(jnp.bfloat16)

def project(inputs, weight):
    return jnp.dot(inputs, weight, preferred_element_type=jnp.float32).astype(jnp.bfloat16)

def reference(events, offsets, cotangent, query_weight, key_weight, value_weight, omega):
    widened_rows = jnp.float32
    inputs = encode(events, offsets)
    queries = project(inputs, query_weight)
    key_act = project(inputs, key_weight)
    value_act = project(inputs, value_weight)
    block_rows = TOK_DEV * N_SUB
    block_count = TOKENS // block_rows
    omega_wide = omega.astype(widened_rows)
    loss_scale = math.sqrt(TOKENS)

    def as_blocks(matrix):
        return matrix.reshape(block_count, block_rows, H, D // H)

    def featurize(acts):
        pre_act = jnp.einsum('thd,hdm->thm', acts.astype(widened_rows), omega_wide)
        return (pre_act, jax.nn.softplus(pre_act).astype(jnp.bfloat16))

    def add_keys(running_state, block_pair):
        key_blk, value_block = block_pair
        _, key_feature_map = featurize(key_blk)
        key_widened = key_feature_map.astype(widened_rows)
        state_digest = running_state[0] + jnp.einsum('reb,rec->ebc', key_widened, value_block.astype(widened_rows))
        return ((state_digest, running_state[1] + lax.optimization_barrier(jnp.sum(key_widened, axis=0))), None)
    starting = (jnp.zeros((H, M, D // H), widened_rows), jnp.zeros((H, M), widened_rows))
    (state_digest, key_total), _ = lax.scan(add_keys, starting, (as_blocks(key_act), as_blocks(value_act)))
    digest_halves = state_digest.astype(jnp.bfloat16)
    total_half = key_total.astype(jnp.bfloat16)

    def query_side(query_blk, upstream_blk):
        query_pre, query_feature_map = featurize(query_blk)
        query_widened = query_feature_map.astype(widened_rows)
        numerator = jnp.einsum('xls,lsk->xlk', query_widened, digest_halves.astype(widened_rows))
        denom = jnp.einsum('thm,hm->th', query_widened, total_half.astype(widened_rows))
        attended = numerator / denom[..., None]
        upstream = upstream_blk.astype(widened_rows) * loss_scale
        scaled_grad = upstream / denom[..., None]
        norm_grad = -lax.optimization_barrier(jnp.sum(scaled_grad * attended, axis=-1))
        return (query_pre, query_feature_map, scaled_grad.astype(jnp.bfloat16), norm_grad, norm_grad.astype(jnp.bfloat16))

    def add_queries(running_state, block_pair):
        _, query_feature_map, scaled_halves, _, norm_half = query_side(block_pair[0], block_pair[1])
        query_widened = query_feature_map.astype(widened_rows)
        gradient_summed = running_state[0] + jnp.einsum('reb,rec->ebc', query_widened, scaled_halves.astype(widened_rows))
        total_sum = running_state[1] + jnp.einsum('thm,th->hm', query_widened, norm_half.astype(widened_rows))
        return ((gradient_summed, total_sum), None)
    query_blocks = as_blocks(queries)
    upstream_blocks = as_blocks(cotangent)
    (summary_grad, overall_gradient), _ = lax.scan(add_queries, starting, (query_blocks, upstream_blocks))
    gradient_halves = summary_grad.astype(jnp.bfloat16).astype(widened_rows)

    def gradients(block_set):
        query_blk, key_blk, value_block, upstream_blk = block_set
        query_pre, _, scaled_halves, norm_grad, _ = query_side(query_blk, upstream_blk)
        key_pre, key_feature_map = featurize(key_blk)
        query_feature_gradient = jnp.einsum('pfy,fly->pfl', scaled_halves.astype(widened_rows), digest_halves.astype(widened_rows))
        query_feature_gradient = query_feature_gradient + norm_grad[..., None] * total_half.astype(widened_rows)[None]
        key_feature_gradient = jnp.einsum('pfy,fly->pfl', value_block.astype(widened_rows), gradient_halves) + overall_gradient[None]
        value_gradient = jnp.einsum('xls,lsk->xlk', key_feature_map.astype(widened_rows), gradient_halves).astype(jnp.bfloat16)
        query_pre_grad = (query_feature_gradient * jax.nn.sigmoid(query_pre)).astype(jnp.bfloat16)
        key_pre_grad = (key_feature_gradient * jax.nn.sigmoid(key_pre)).astype(jnp.bfloat16)
        query_grad = jnp.einsum('thm,hdm->thd', query_pre_grad.astype(widened_rows), omega_wide).astype(jnp.bfloat16)
        key_grad = jnp.einsum('thm,hdm->thd', key_pre_grad.astype(widened_rows), omega_wide).astype(jnp.bfloat16)
        return (query_grad, key_grad, value_gradient)
    query_grad, key_grad, value_gradient = lax.map(gradients, (query_blocks, as_blocks(key_act), as_blocks(value_act), upstream_blocks))
    total = jnp.dot(query_grad.reshape(TOKENS, D), query_weight.T, preferred_element_type=jnp.float32)
    total = total + jnp.dot(key_grad.reshape(TOKENS, D), key_weight.T, preferred_element_type=jnp.float32)
    total = total + jnp.dot(value_gradient.reshape(TOKENS, D), value_weight.T, preferred_element_type=jnp.float32)
    return total.astype(jnp.bfloat16)
```

```python
import functools
import math

import jax
import jax.numpy as jnp
from jax import lax
from jax.experimental import pallas as pl
from jax.experimental.pallas import tpu as pltpu
from jax.sharding import PartitionSpec as P


def encode(events, offsets):
    half_width = events.shape[1] // 2
    indices = jnp.arange(half_width, dtype=jnp.float32)
    frequency = jnp.exp(indices * (-2.0 * math.log(10000.0) / events.shape[1]))
    angles = offsets.astype(jnp.float32)[:, None] * frequency[None, :]
    encoding = jnp.concatenate([jnp.sin(angles), jnp.cos(angles)], axis=1)
    return (events.astype(jnp.float32) + encoding).astype(jnp.bfloat16)


def split_heads(matrix, head_count):
    return matrix.reshape(matrix.shape[0], head_count, matrix.shape[1] // head_count)


def transposed(left, weight):
    return lax.dot_general(
        left, weight, (((1,), (1,)), ((), ())), preferred_element_type=jnp.float32
    )


def local(events, offsets, cotangent, query_weight, key_weight, value_weight, omega):
    widened_rows = jnp.float32
    head_count = omega.shape[0]
    local_rows = events.shape[0]
    model_width = events.shape[1]
    all_tokens = local_rows * lax.axis_size("seq") * lax.axis_size("sub")
    loss_scale = math.sqrt(all_tokens)
    inputs = encode(events, offsets)
    gathered = (
        lax.all_gather(query_weight, "sub", axis=0, tiled=True),
        lax.all_gather(key_weight, "sub", axis=0, tiled=True),
        lax.all_gather(value_weight, "sub", axis=0, tiled=True),
    )
    queries, key_act, value_act = [
        jnp.dot(inputs, weight, preferred_element_type=widened_rows).astype(jnp.bfloat16)
        for weight in gathered
    ]
    query_pre = jnp.einsum(
        "thd,hdm->thm", split_heads(queries, head_count), omega, preferred_element_type=widened_rows
    )
    key_pre = jnp.einsum(
        "thd,hdm->thm", split_heads(key_act, head_count), omega, preferred_element_type=widened_rows
    )
    query_feature_map = jax.nn.softplus(query_pre).astype(jnp.bfloat16)
    key_feature_map = jax.nn.softplus(key_pre).astype(jnp.bfloat16)
    value_per_head = split_heads(value_act, head_count)
    local_digest = jnp.einsum(
        "reb,rec->ebc", key_feature_map, value_per_head, preferred_element_type=widened_rows
    )
    local_total = jnp.sum(key_feature_map, axis=0, dtype=widened_rows)
    state_digest, key_total = lax.psum((local_digest, local_total), ("seq", "sub"))
    digest_halves = state_digest.astype(jnp.bfloat16)
    total_half = key_total.astype(jnp.bfloat16)
    numerator = jnp.einsum(
        "xls,lsk->xlk", query_feature_map, digest_halves, preferred_element_type=widened_rows
    )
    denom = jnp.einsum(
        "thm,hm->th", query_feature_map, total_half, preferred_element_type=widened_rows
    )
    attended = numerator / denom[..., None]
    upstream = split_heads(cotangent, head_count).astype(widened_rows) * loss_scale
    scaled_grad = upstream / denom[..., None]
    norm_grad = -jnp.sum(scaled_grad * attended, axis=-1)
    scaled_halves = scaled_grad.astype(jnp.bfloat16)
    norm_half = norm_grad.astype(jnp.bfloat16)
    local_gradient = jnp.einsum(
        "reb,rec->ebc", query_feature_map, scaled_halves, preferred_element_type=widened_rows
    )
    local_norm = jnp.einsum(
        "thm,th->hm", query_feature_map, norm_half, preferred_element_type=widened_rows
    )
    summary_grad, overall_gradient = lax.psum((local_gradient, local_norm), ("seq", "sub"))
    gradient_halves = summary_grad.astype(jnp.bfloat16)
    query_feature_gradient = jnp.einsum(
        "pfy,fly->pfl", scaled_halves, digest_halves, preferred_element_type=widened_rows
    )
    query_feature_gradient = (
        query_feature_gradient + norm_grad[..., None] * total_half.astype(widened_rows)[None]
    )
    key_feature_gradient = (
        jnp.einsum(
            "pfy,fly->pfl", value_per_head, gradient_halves, preferred_element_type=widened_rows
        )
        + overall_gradient[None]
    )
    value_gradient = jnp.einsum(
        "xls,lsk->xlk", key_feature_map, gradient_halves, preferred_element_type=widened_rows
    ).astype(jnp.bfloat16)
    query_pre_grad = (query_feature_gradient * jax.nn.sigmoid(query_pre)).astype(jnp.bfloat16)
    key_pre_grad = (key_feature_gradient * jax.nn.sigmoid(key_pre)).astype(jnp.bfloat16)
    query_grad = jnp.einsum(
        "thm,hdm->thd", query_pre_grad, omega, preferred_element_type=widened_rows
    ).astype(jnp.bfloat16)
    key_grad = jnp.einsum(
        "thm,hdm->thd", key_pre_grad, omega, preferred_element_type=widened_rows
    ).astype(jnp.bfloat16)
    query_flat = query_grad.reshape(local_rows, model_width)
    key_flat = key_grad.reshape(local_rows, model_width)
    value_flat = value_gradient.reshape(local_rows, model_width)
    summed = transposed(query_flat, gathered[0])
    summed = summed + transposed(key_flat, gathered[1])
    summed = summed + transposed(value_flat, gathered[2])
    return summed.astype(jnp.bfloat16)


F32, BF16 = jnp.float32, jnp.bfloat16
MESH = pl.DeviceIdType.MESH
NN = (((1,), (0,)), ((), ()))
NT = (((1,), (1,)), ((), ()))
TN = (((0,), (0,)), ((), ()))


def mul(left, right, dims):
    return lax.dot_general(left, right, dims, preferred_element_type=F32)


def activations(pre):
    small = jnp.exp(-jnp.abs(pre))
    feature = jnp.maximum(pre, 0.0) + jnp.log1p(small)
    sigmoid = jnp.where(pre >= 0.0, 1.0, small) / (1.0 + small)
    return feature.astype(BF16), sigmoid


def encoded(events, offsets):
    block, width = events.shape
    row = lax.broadcasted_iota(jnp.int32, (block, block), 0)
    lane = lax.broadcasted_iota(jnp.int32, (block, block), 1)
    spread = jnp.broadcast_to(offsets.astype(F32), (block, block))
    column = jnp.sum(jnp.where(row == lane, spread, 0.0), axis=1, keepdims=True)
    indices = lax.broadcasted_iota(jnp.int32, (1, width // 2), 1).astype(F32)
    frequency = jnp.exp(indices * (-2.0 * math.log(10000.0) / width))
    angles = column * frequency
    turns = jnp.floor(angles * (2.0 / math.pi) + 0.5)
    rest = angles - turns * 1.5703125
    rest = rest - turns * 4.837512969970703125e-4
    rest = rest - turns * 7.54978994e-8
    square = rest * rest
    sine = ((-1.9515295891e-4 * square + 8.3321608736e-3) * square - 1.6666654611e-1) * square * rest + rest
    cosine = ((2.443315711809948e-5 * square - 1.388731625493765e-3) * square + 4.166664568298827e-2)
    cosine = cosine * square * square - 0.5 * square + 1.0
    halves = jnp.floor(turns * 0.5)
    odd = turns - 2.0 * halves
    sign = 1.0 - 2.0 * (halves - 2.0 * jnp.floor(halves * 0.5))
    swap = odd > 0.5
    sines = jnp.where(swap, cosine, sine) * sign
    cosines = jnp.where(swap, -sine, cosine) * sign
    wide = events.astype(F32)
    return (
        (wide[:, : width // 2] + sines).astype(BF16),
        (wide[:, width // 2 :] + cosines).astype(BF16),
    )


def kernel(
    n_grp, n_seq, n_sub, loss_scale, cuts, stop,
    ev_ref, off_ref, cot_ref, wq_ref, wk_ref, wv_ref, omega_ref, out_ref,
    ev, off, xall, call, wall, om, act, va, qf, kf, qs, ks, sc, inv, nrm, gr,
    acc, part, rsin, half, tot, totin, mo, mi, ro, ri,
    local_sem, xs, xr, cs, cr, ws, wr, ys, yr, ss, sr, ts, tr, ms, mr, os_, or_,
):
    grp, seq, sub = lax.axis_index("grp"), lax.axis_index("seq"), lax.axis_index("sub")
    chips = n_seq // 2
    chip, core = seq // 2, seq % 2
    mate = 2 * chip + 1 - core
    block, width = ev_ref.shape
    pair, head, features = om.shape
    span = pair * head
    rows = wq_ref.shape[0]
    share = rows // n_grp
    piece = span // n_sub
    slab = width // cuts

    def in_row(index):
        return {"grp": grp, "seq": index, "sub": sub}

    def in_column(index):
        return {"grp": grp, "seq": seq, "sub": index}

    def in_group(index):
        return {"grp": index, "seq": seq, "sub": sub}

    def seat(d, which):
        return 2 * ((chip + d) % chips) + which

    def rows_of(index, size):
        return pl.ds(pl.multiple_of(index * size, size), size)

    unsent, unread = [], []

    def send(src, dst, send_sem, recv_sem, device):
        copy = pltpu.make_async_remote_copy(
            src_ref=src, dst_ref=dst, send_sem=send_sem, recv_sem=recv_sem,
            device_id=device, device_id_type=MESH,
        )
        copy.start()
        unsent.append(copy)
        unread.append(copy)
        return copy

    def arrive(copy):
        copy.wait_recv()
        unread[:] = [other for other in unread if other is not copy]

    def drain():
        for copy in unread:
            copy.wait_recv()
        for copy in unsent:
            copy.wait_send()

    barrier = pltpu.get_barrier_semaphore()
    for d in range(1, n_seq):
        pl.semaphore_signal(barrier, inc=1, device_id=in_row((seq + d) % n_seq), device_id_type=MESH)
    for d in range(1, n_sub):
        pl.semaphore_signal(barrier, inc=1, device_id=in_column((sub + d) % n_sub), device_id_type=MESH)
    for d in range(1, n_grp):
        pl.semaphore_signal(barrier, inc=1, device_id=in_group((grp + d) % n_grp), device_id_type=MESH)

    weights = (wk_ref, wv_ref, wq_ref)
    mine = rows_of(seq, block)
    columns = rows_of(seq, span)

    def local(src, dst, index):
        copy = pltpu.make_async_copy(src, dst, local_sem.at[index])
        copy.start()
        return copy

    first = [local(ev_ref, ev, 0), local(off_ref, off, 1)]
    later = [
        local(w.at[:, columns], wall.at[rows_of(sub, rows), pl.ds(i * span, span)], 2 + i)
        for i, w in enumerate(weights)
    ]
    later.append(local(omega_ref.at[rows_of(seq, pair)], om, 5))
    later.append(local(cot_ref.at[:, columns], call.at[mine], 6))
    for copy in first:
        copy.wait()
    low, high = encoded(ev[...], off[...])
    xall[mine, : width // 2] = low
    xall[mine, width // 2 :] = high
    pl.semaphore_wait(barrier, n_seq + n_sub + n_grp - 3)

    slice_rows = pl.ds(pl.multiple_of(sub * rows + grp * share, share), share)
    wcopies = {}
    xcopies = {}
    for i in range(3):
        for d in range(1, n_sub):
            wcopies[i, d] = send(
                weights[i].at[rows_of(grp, share), columns], wall.at[slice_rows, pl.ds(i * span, span)],
                ws.at[i, d - 1], wr.at[i, d - 1], in_column((sub + d) % n_sub),
            )
        if i == 0:
            for d in range(1, chips):
                xcopies[d] = send(xall.at[mine], xall.at[mine], xs.at[d], xr.at[d], in_row(seat(d, core)))
            xcopies[0] = send(xall.at[mine], xall.at[mine], xs.at[0], xr.at[0], in_row(mate))
    ccopies = []
    for d in range(1, n_seq):
        to = (seq + d) % n_seq
        ccopies.append(send(
            cot_ref.at[:, rows_of(to, span)], call.at[mine], cs.at[d - 1], cr.at[d - 1], in_row(to)
        ))
    for copy in later:
        copy.wait()

    xforward = []
    for d in range(1, chips):
        arrive(xcopies[d])
        source = (seq - 2 * d + n_seq) % n_seq
        at = rows_of(source, block)
        xforward.append(send(xall.at[at], xall.at[at], xs.at[chips + d - 1], xr.at[chips + d - 1], in_row(mate)))

    def gather(i):
        forwards = []
        for d in range(1, n_sub):
            arrive(wcopies[i, d])
            source = (sub + n_sub - d) % n_sub
            at = wall.at[
                pl.ds(pl.multiple_of(source * rows + grp * share, share), share), pl.ds(i * span, span)
            ]
            for e in range(1, n_grp):
                forwards.append(send(
                    at, at, ys.at[i, d - 1, e - 1], yr.at[i, d - 1, e - 1], in_group((grp + e) % n_grp)
                ))
        for copy in forwards:
            arrive(copy)

    def project(i, target):
        target[...] = mul(xall[...], wall[:, i * span : (i + 1) * span], NN).astype(BF16)

    def featurize(feature, sigmoid):
        def step(b, carry):
            at = rows_of(b, block)
            for h in range(pair):
                pre = mul(act[at, h * head : (h + 1) * head], om[h], NN)
                feature[h, at, :], sigmoid[h, at, :] = activations(pre)
            return carry

        lax.fori_loop(0, n_seq, step, 0, unroll=True)

    def start_total(a):
        copies = []
        for d in range(1, n_sub):
            copies.append(send(
                tot.at[a], totin.at[a, d - 1], ts.at[a, d - 1], tr.at[a, d - 1], in_column((sub + d) % n_sub)
            ))
        return copies

    def finish_total(a, copies):
        total = tot[a]
        for d in range(1, n_sub):
            arrive(copies[d - 1])
            total = total + totin[a, d - 1]
        return total

    def start_sum(a):
        part[a] = acc[a].astype(BF16)
        copies = []
        for d in range(1, n_sub):
            to = (sub + d) % n_sub
            copies.append(send(
                part.at[a, rows_of(to, piece)], rsin.at[a, d - 1],
                ss.at[a, 0, d - 1], sr.at[a, 0, d - 1], in_column(to),
            ))
        return copies

    def middle_sum(a, copies):
        own = rows_of(sub, piece)
        summed = acc[a, own, :]
        for d in range(1, n_sub):
            arrive(copies[d - 1])
            summed = summed + rsin[a, d - 1].astype(F32)
        half[a, own, :] = summed.astype(BF16)
        return [
            send(
                half.at[a, own], half.at[a, own],
                ss.at[a, 1, d - 1], sr.at[a, 1, d - 1], in_column((sub + d) % n_sub),
            )
            for d in range(1, n_sub)
        ]

    def body():
        gather(0)
        for copy in xforward:
            arrive(copy)
        arrive(xcopies[0])
        if stop == 1:
            return
        project(0, act)
        featurize(kf, ks)
        tot[...] = jnp.zeros_like(tot)
        for h in range(pair):
            tot[0, pl.ds(h, 1), :] = jnp.sum(kf[h].astype(F32), axis=0, keepdims=True)
        totals = start_total(0)
        if stop == 2:
            return
        gather(1)
        project(1, va)
        for h in range(pair):
            acc[0, pl.ds(h * head, head), :] = mul(va[:, h * head : (h + 1) * head], kf[h], TN)
        first_sum = start_sum(0)
        if stop == 3:
            return
        gather(2)
        project(2, act)
        featurize(qf, qs)
        if stop == 4:
            return
        total_half = finish_total(0, totals).astype(BF16)
        for copy in ccopies:
            arrive(copy)
        for h in range(pair):
            wide = jnp.broadcast_to(total_half[h : h + 1], (head, features))
            lanes = pl.ds(h * head, head)

            def scale(b, carry, h=h, wide=wide, lanes=lanes):
                at = rows_of(b, block)
                inverse = 1.0 / mul(qf[h, at, :], wide, NT)
                inv[h, at, :] = inverse
                sc[at, lanes] = (call[at, lanes].astype(F32) * loss_scale * inverse).astype(BF16)
                return carry

            lax.fori_loop(0, n_seq, scale, 0, unroll=True)
            acc[1, pl.ds(h * head, head), :] = mul(sc[:, lanes], qf[h], TN)
        second_sum = start_sum(1)
        first_back = middle_sum(0, first_sum)
        if stop == 5:
            return
        for copy in first_back:
            arrive(copy)
        for h in range(pair):
            lanes = pl.ds(h * head, head)
            summary = half[0, pl.ds(h * head, head), :]

            def norms(b, carry, h=h, lanes=lanes, summary=summary):
                at = rows_of(b, block)
                inverse = inv[h, at, :]
                attended = mul(qf[h, at, :], summary, NT) * inverse
                scaled = call[at, lanes].astype(F32) * loss_scale * inverse
                nrm[h, at, :] = -jnp.sum(scaled * attended, axis=-1, keepdims=True)
                return carry

            lax.fori_loop(0, n_seq, norms, 0, unroll=True)
            tot[1, pl.ds(h, 1), :] = jnp.sum(
                qf[h].astype(F32) * nrm[h].astype(BF16).astype(F32), axis=0, keepdims=True
            )
        grads = start_total(1)
        second_back = middle_sum(1, second_sum)
        if stop == 6:
            return
        for h in range(pair):
            lanes = pl.ds(h * head, head)
            summary = half[0, pl.ds(h * head, head), :]
            weight = total_half[h : h + 1].astype(F32)

            def query_grads(b, carry, h=h, lanes=lanes, summary=summary, weight=weight):
                at = rows_of(b, block)
                grad = mul(sc[at, lanes], summary, NN) + nrm[h, at, :] * weight
                grad = (grad * qs[h, at, :]).astype(BF16)
                gr[at, pl.ds(2 * span + h * head, head)] = mul(grad, om[h], NT).astype(BF16)
                return carry

            lax.fori_loop(0, n_seq, query_grads, 0, unroll=True)
        total_grad = finish_total(1, grads)
        for copy in second_back:
            arrive(copy)
        if stop == 7:
            return
        for h in range(pair):
            lanes = pl.ds(h * head, head)
            summary = half[1, pl.ds(h * head, head), :]
            extra = total_grad[h : h + 1]

            def key_grads(b, carry, h=h, lanes=lanes, summary=summary, extra=extra):
                at = rows_of(b, block)
                grad = mul(va[at, lanes], summary, NN) + extra
                grad = (grad * ks[h, at, :]).astype(BF16)
                gr[at, pl.ds(h * head, head)] = mul(grad, om[h], NT).astype(BF16)
                gr[at, pl.ds(span + h * head, head)] = mul(kf[h, at, :], summary, NT).astype(BF16)
                return carry

            lax.fori_loop(0, n_seq, key_grads, 0, unroll=True)
        if stop == 8:
            return

        def partial_of(index, c):
            return mul(gr[rows_of(index, block), :], wall[c * slab : (c + 1) * slab, :], NT)

        def to_mate(d):
            copies = []
            for c in range(cuts):
                at = pl.ds(c * slab, slab)
                mo[d, :, at] = partial_of(seat(d, 1 - core), c).astype(BF16)
                copies.append(send(
                    mo.at[d, :, at], mi.at[d, :, at], ms.at[d, c], mr.at[d, c], in_row(mate)
                ))
            return copies

        for_mate = {d: to_mate(d) for d in range(1, chips)}
        outward = {}
        for d in range(1, chips):
            for c in range(cuts):
                at = pl.ds(c * slab, slab)
                own = partial_of(seat(d, core), c)
                arrive(for_mate[d][c])
                ro[d - 1, :, at] = (own + mi[d, :, at].astype(F32)).astype(BF16)
                outward[d, c] = send(
                    ro.at[d - 1, :, at], ri.at[d - 1, :, at], os_.at[d - 1, c], or_.at[d - 1, c],
                    in_row(seat(d, core)),
                )
        for_mate[0] = to_mate(0)
        own = [partial_of(seq, c) for c in range(cuts)]
        for c in range(cuts):
            at = pl.ds(c * slab, slab)
            arrive(for_mate[0][c])
            summed = own[c] + mi[0, :, at].astype(F32)
            for d in range(1, chips):
                arrive(outward[d, c])
                summed = summed + ri[d - 1, :, at].astype(F32)
            out_ref[:, at] = summed.astype(BF16)

    body()
    drain()


def fits(n_grp, n_seq, n_sub, events, offsets, cotangent, query_weight, key_weight, value_weight, omega):
    heads, head, features = omega.shape
    block, width = events.shape
    pair = heads // n_seq
    rows = query_weight.shape[0]
    return (
        n_seq >= 4 and n_seq % 2 == 0 and n_grp > 1 and n_sub > 1 and heads % n_seq == 0 and pair <= 8
        and head % 128 == 0 and features % 128 == 0 and block % 128 == 0 and width % 512 == 0
        and pair * head % (16 * n_sub) == 0 and rows % (16 * n_grp) == 0
        and n_seq * block <= 1024 and pair * features <= 512 and width <= 1024
    )


STOP = 99


def fused(n_grp, n_seq, n_sub, events, offsets, cotangent, query_weight, key_weight, value_weight, omega):
    block, width = events.shape
    heads, head, features = omega.shape
    tokens = n_seq * block
    pair = heads // n_seq
    span = pair * head
    piece = span // n_sub
    chips = n_seq // 2
    cuts = 2
    vm = pltpu.VMEM
    dma = pltpu.SemaphoreType.DMA
    scratch = [
        vm((block, width), BF16),
        vm((1, block), jnp.int32),
        vm((tokens, width), BF16),
        vm((tokens, span), BF16),
        vm((width, 3 * span), BF16),
        vm((pair, head, features), BF16),
        vm((tokens, span), BF16),
        vm((tokens, span), BF16),
        vm((pair, tokens, features), BF16),
        vm((pair, tokens, features), BF16),
        vm((pair, tokens, features), F32),
        vm((pair, tokens, features), F32),
        vm((tokens, span), BF16),
        vm((pair, tokens, head), F32),
        vm((pair, tokens, 1), F32),
        vm((tokens, 3 * span), BF16),
        vm((2, span, features), F32),
        vm((2, span, features), BF16),
        vm((2, n_sub - 1, piece, features), BF16),
        vm((2, span, features), BF16),
        vm((2, 8, features), F32),
        vm((2, n_sub - 1, 8, features), F32),
        vm((chips, block, width), BF16),
        vm((chips, block, width), BF16),
        vm((chips - 1, block, width), BF16),
        vm((chips - 1, block, width), BF16),
        dma((7,)),
        dma((2 * chips - 1,)), dma((2 * chips - 1,)),
        dma((n_seq - 1,)), dma((n_seq - 1,)),
        dma((3, n_sub - 1)), dma((3, n_sub - 1)),
        dma((3, n_sub - 1, n_grp - 1)), dma((3, n_sub - 1, n_grp - 1)),
        dma((2, 2, n_sub - 1)), dma((2, 2, n_sub - 1)),
        dma((2, n_sub - 1)), dma((2, n_sub - 1)),
        dma((chips, cuts)), dma((chips, cuts)),
        dma((chips - 1, cuts)), dma((chips - 1, cuts)),
    ]
    loss_scale = math.sqrt(block * n_seq * n_sub)
    return pl.pallas_call(
        functools.partial(kernel, n_grp, n_seq, n_sub, loss_scale, cuts, STOP),
        out_shape=jax.ShapeDtypeStruct((block, width), BF16),
        in_specs=[pl.BlockSpec(memory_space=pl.ANY)] * 7,
        out_specs=pl.BlockSpec(memory_space=pltpu.VMEM),
        scratch_shapes=scratch,
        compiler_params=pltpu.CompilerParams(
            collective_id=0, has_side_effects=True, vmem_limit_bytes=60 * 1024 * 1024
        ),
    )(events, offsets.reshape(1, block), cotangent, query_weight, key_weight, value_weight, omega)


def solution(mesh):
    in_specs = (
        P(("grp", "seq", "sub"), None),
        P(("grp", "seq", "sub")),
        P(("grp", "seq", "sub"), None),
        P("sub", None),
        P("sub", None),
        P("sub", None),
        P(),
    )
    out_specs = P(("grp", "seq", "sub"), None)
    n_grp, n_seq, n_sub = (mesh.shape[name] for name in ("grp", "seq", "sub"))

    def body(*args):
        if fits(n_grp, n_seq, n_sub, *args):
            return fused(n_grp, n_seq, n_sub, *args)
        return local(*args)

    return jax.shard_map(body, mesh=mesh, in_specs=in_specs, out_specs=out_specs, check_vma=False)
```

```python
import functools
import math

import jax
import jax.numpy as jnp
from jax import lax
from jax.experimental import pallas as pl
from jax.experimental.pallas import tpu as pltpu
from jax.sharding import PartitionSpec as P


def encode(events, offsets):
    half_width = events.shape[1] // 2
    indices = jnp.arange(half_width, dtype=jnp.float32)
    frequency = jnp.exp(indices * (-2.0 * math.log(10000.0) / events.shape[1]))
    angles = offsets.astype(jnp.float32)[:, None] * frequency[None, :]
    encoding = jnp.concatenate([jnp.sin(angles), jnp.cos(angles)], axis=1)
    return (events.astype(jnp.float32) + encoding).astype(jnp.bfloat16)


def split_heads(matrix, head_count):
    return matrix.reshape(matrix.shape[0], head_count, matrix.shape[1] // head_count)


def transposed(left, weight):
    return lax.dot_general(
        left, weight, (((1,), (1,)), ((), ())), preferred_element_type=jnp.float32
    )


def local(events, offsets, cotangent, query_weight, key_weight, value_weight, omega):
    widened_rows = jnp.float32
    head_count = omega.shape[0]
    local_rows = events.shape[0]
    model_width = events.shape[1]
    all_tokens = local_rows * lax.axis_size("seq") * lax.axis_size("sub")
    loss_scale = math.sqrt(all_tokens)
    inputs = encode(events, offsets)
    gathered = (
        lax.all_gather(query_weight, "sub", axis=0, tiled=True),
        lax.all_gather(key_weight, "sub", axis=0, tiled=True),
        lax.all_gather(value_weight, "sub", axis=0, tiled=True),
    )
    queries, key_act, value_act = [
        jnp.dot(inputs, weight, preferred_element_type=widened_rows).astype(jnp.bfloat16)
        for weight in gathered
    ]
    query_pre = jnp.einsum(
        "thd,hdm->thm", split_heads(queries, head_count), omega, preferred_element_type=widened_rows
    )
    key_pre = jnp.einsum(
        "thd,hdm->thm", split_heads(key_act, head_count), omega, preferred_element_type=widened_rows
    )
    query_feature_map = jax.nn.softplus(query_pre).astype(jnp.bfloat16)
    key_feature_map = jax.nn.softplus(key_pre).astype(jnp.bfloat16)
    value_per_head = split_heads(value_act, head_count)
    local_digest = jnp.einsum(
        "reb,rec->ebc", key_feature_map, value_per_head, preferred_element_type=widened_rows
    )
    local_total = jnp.sum(key_feature_map, axis=0, dtype=widened_rows)
    state_digest, key_total = lax.psum((local_digest, local_total), ("seq", "sub"))
    digest_halves = state_digest.astype(jnp.bfloat16)
    total_half = key_total.astype(jnp.bfloat16)
    numerator = jnp.einsum(
        "xls,lsk->xlk", query_feature_map, digest_halves, preferred_element_type=widened_rows
    )
    denom = jnp.einsum(
        "thm,hm->th", query_feature_map, total_half, preferred_element_type=widened_rows
    )
    attended = numerator / denom[..., None]
    upstream = split_heads(cotangent, head_count).astype(widened_rows) * loss_scale
    scaled_grad = upstream / denom[..., None]
    norm_grad = -jnp.sum(scaled_grad * attended, axis=-1)
    scaled_halves = scaled_grad.astype(jnp.bfloat16)
    norm_half = norm_grad.astype(jnp.bfloat16)
    local_gradient = jnp.einsum(
        "reb,rec->ebc", query_feature_map, scaled_halves, preferred_element_type=widened_rows
    )
    local_norm = jnp.einsum(
        "thm,th->hm", query_feature_map, norm_half, preferred_element_type=widened_rows
    )
    summary_grad, overall_gradient = lax.psum((local_gradient, local_norm), ("seq", "sub"))
    gradient_halves = summary_grad.astype(jnp.bfloat16)
    query_feature_gradient = jnp.einsum(
        "pfy,fly->pfl", scaled_halves, digest_halves, preferred_element_type=widened_rows
    )
    query_feature_gradient = (
        query_feature_gradient + norm_grad[..., None] * total_half.astype(widened_rows)[None]
    )
    key_feature_gradient = (
        jnp.einsum(
            "pfy,fly->pfl", value_per_head, gradient_halves, preferred_element_type=widened_rows
        )
        + overall_gradient[None]
    )
    value_gradient = jnp.einsum(
        "xls,lsk->xlk", key_feature_map, gradient_halves, preferred_element_type=widened_rows
    ).astype(jnp.bfloat16)
    query_pre_grad = (query_feature_gradient * jax.nn.sigmoid(query_pre)).astype(jnp.bfloat16)
    key_pre_grad = (key_feature_gradient * jax.nn.sigmoid(key_pre)).astype(jnp.bfloat16)
    query_grad = jnp.einsum(
        "thm,hdm->thd", query_pre_grad, omega, preferred_element_type=widened_rows
    ).astype(jnp.bfloat16)
    key_grad = jnp.einsum(
        "thm,hdm->thd", key_pre_grad, omega, preferred_element_type=widened_rows
    ).astype(jnp.bfloat16)
    query_flat = query_grad.reshape(local_rows, model_width)
    key_flat = key_grad.reshape(local_rows, model_width)
    value_flat = value_gradient.reshape(local_rows, model_width)
    summed = transposed(query_flat, gathered[0])
    summed = summed + transposed(key_flat, gathered[1])
    summed = summed + transposed(value_flat, gathered[2])
    return summed.astype(jnp.bfloat16)


F32, BF16 = jnp.float32, jnp.bfloat16
MESH = pl.DeviceIdType.MESH
NN = (((1,), (0,)), ((), ()))
NT = (((1,), (1,)), ((), ()))
TN = (((0,), (0,)), ((), ()))


def mul(left, right, dims):
    return lax.dot_general(left, right, dims, preferred_element_type=F32)


def activations(pre):
    small = jnp.exp(-jnp.abs(pre))
    feature = jnp.maximum(pre, 0.0) + jnp.log1p(small)
    sigmoid = jnp.where(pre >= 0.0, 1.0, small) / (1.0 + small)
    return feature.astype(BF16), sigmoid


def encoded(events, offsets):
    block, width = events.shape
    row = lax.broadcasted_iota(jnp.int32, (block, block), 0)
    lane = lax.broadcasted_iota(jnp.int32, (block, block), 1)
    spread = jnp.broadcast_to(offsets.astype(F32), (block, block))
    column = jnp.sum(jnp.where(row == lane, spread, 0.0), axis=1, keepdims=True)
    indices = lax.broadcasted_iota(jnp.int32, (1, width // 2), 1).astype(F32)
    frequency = jnp.exp(indices * (-2.0 * math.log(10000.0) / width))
    angles = column * frequency
    turns = jnp.floor(angles * (2.0 / math.pi) + 0.5)
    rest = angles - turns * 1.5703125
    rest = rest - turns * 4.837512969970703125e-4
    rest = rest - turns * 7.54978994e-8
    square = rest * rest
    sine = ((-1.9515295891e-4 * square + 8.3321608736e-3) * square - 1.6666654611e-1) * square * rest + rest
    cosine = ((2.443315711809948e-5 * square - 1.388731625493765e-3) * square + 4.166664568298827e-2)
    cosine = cosine * square * square - 0.5 * square + 1.0
    halves = jnp.floor(turns * 0.5)
    odd = turns - 2.0 * halves
    sign = 1.0 - 2.0 * (halves - 2.0 * jnp.floor(halves * 0.5))
    swap = odd > 0.5
    sines = jnp.where(swap, cosine, sine) * sign
    cosines = jnp.where(swap, -sine, cosine) * sign
    wide = events.astype(F32)
    return (
        (wide[:, : width // 2] + sines).astype(BF16),
        (wide[:, width // 2 :] + cosines).astype(BF16),
    )


def kernel(
    n_grp, n_seq, n_sub, loss_scale, cuts, stop,
    ev_ref, off_ref, cot_ref, wq_ref, wk_ref, wv_ref, omega_ref, out_ref,
    ev, off, xall, call, wall, om, act, va, qf, kf, qs, ks, sc, inv, nrm, gr,
    acc, part, rsin, half, tot, totin, keep, mo, mi, ro, ri,
    local_sem, xs, xr, cs, cr, ws, wr, hs, ys, yr, ss, sr, ts, tr, ms, mr, os_, or_,
):
    grp, seq, sub = lax.axis_index("grp"), lax.axis_index("seq"), lax.axis_index("sub")
    chips = n_seq // 2
    chip, core = seq // 2, seq % 2
    mate = 2 * chip + 1 - core
    block, width = ev_ref.shape
    pair, head, features = om.shape
    span = pair * head
    rows = wq_ref.shape[0]
    share = rows // n_grp
    piece = head // n_sub
    slab = width // cuts
    edge, middle, far = range(n_sub - 1)

    def in_row(index):
        return {"grp": grp, "seq": index, "sub": sub}

    def in_column(index):
        return {"grp": grp, "seq": seq, "sub": index}

    def in_group(index):
        return {"grp": index, "seq": seq, "sub": sub}

    def seat(d, which):
        return 2 * ((chip + d) % chips) + which

    def rows_of(index, size):
        return pl.ds(pl.multiple_of(index * size, size), size)

    def nearest(k):
        found = 0
        for s in range(n_sub):
            others = sorted((abs(s - t), -abs(2 * t - n_sub + 1), t) for t in range(n_sub) if t != s)
            found = found + jnp.where(sub == s, others[k][2], 0)
        return found

    near = [nearest(k) for k in range(n_sub - 1)]
    unsent, unread, pending = [], [], {}

    def remote(src, dst, send_sem, recv_sem, device):
        return pltpu.make_async_remote_copy(
            src_ref=src, dst_ref=dst, send_sem=send_sem, recv_sem=recv_sem,
            device_id=device, device_id_type=MESH,
        )

    def send(src, dst, send_sem, recv_sem, device):
        copy = remote(src, dst, send_sem, recv_sem, device)
        copy.start()
        unsent.append((copy, None))
        unread.append(copy)
        return copy

    def send_some(condition, src, dst, send_sem, recv_sem, device):
        copy = remote(src, dst, send_sem, recv_sem, device)
        if condition is None:
            copy.start()
        else:
            pl.when(condition)(copy.start)
        unsent.append((copy, condition))

    def arrive(copy):
        copy.wait_recv()
        unread[:] = [other for other in unread if other is not copy]

    def drain():
        for key in list(pending):
            settle(*key)
        for copy in unread:
            copy.wait_recv()
        for copy, condition in unsent:
            if condition is None:
                copy.wait_send()
            else:
                pl.when(condition)(copy.wait_send)

    barrier = pltpu.get_barrier_semaphore()
    for d in range(1, n_seq):
        pl.semaphore_signal(barrier, inc=1, device_id=in_row((seq + d) % n_seq), device_id_type=MESH)
    for d in range(1, n_sub):
        pl.semaphore_signal(barrier, inc=1, device_id=in_column((sub + d) % n_sub), device_id_type=MESH)
    for d in range(1, n_grp):
        pl.semaphore_signal(barrier, inc=1, device_id=in_group((grp + d) % n_grp), device_id_type=MESH)

    weights = (wk_ref, wv_ref, wq_ref)
    mine = rows_of(seq, block)
    columns = rows_of(seq, span)

    def local(src, dst, index):
        copy = pltpu.make_async_copy(src, dst, local_sem.at[index])
        copy.start()
        return copy

    first = [local(ev_ref, ev, 0), local(off_ref, off, 1)]
    later = [
        local(w.at[:, columns], wall.at[rows_of(sub, rows), pl.ds(i * span, span)], 2 + i)
        for i, w in enumerate(weights)
    ]
    later.append(local(omega_ref.at[rows_of(seq, pair)], om, 5))
    later.append(local(cot_ref.at[:, columns], call.at[mine], 6))
    pl.semaphore_wait(barrier, n_seq + n_sub + n_grp - 3)

    def slot(source, i):
        return wall.at[
            pl.ds(pl.multiple_of(source * rows + grp * share, share), share), pl.ds(i * span, span)
        ]

    inner = (sub > 0) & (sub < n_sub - 1)
    outer = jnp.logical_not(inner)

    def slice_copy(i, k):
        return remote(
            weights[i].at[rows_of(grp, share), columns], slot(sub, i),
            ws.at[i, k], wr.at[i, sub], in_column(near[k]),
        )

    @pl.when(inner)
    def _():
        slice_copy(0, far).start()
        slice_copy(0, middle).start()
        slice_copy(0, edge).start()
        for i in (1, 2):
            slice_copy(i, far).start()
            slice_copy(i, middle).start()

    @pl.when(outer)
    def _():
        for i in range(3):
            slice_copy(i, middle).start()
            slice_copy(i, edge).start()

    for i in range(3):
        unsent.append((slice_copy(i, far), inner))
        unsent.append((slice_copy(i, middle), None))
        unsent.append((slice_copy(i, edge), None))

    for copy in first:
        copy.wait()
    low, high = encoded(ev[...], off[...])
    xall[mine, : width // 2] = low
    xall[mine, width // 2 :] = high
    xcopies = {}
    for d in range(1, chips):
        xcopies[d] = send(xall.at[mine], xall.at[mine], xs.at[d], xr.at[d], in_row(seat(d, core)))
    xcopies[0] = send(xall.at[mine], xall.at[mine], xs.at[0], xr.at[0], in_row(mate))
    ccopies = []
    for d in range(1, n_seq):
        to = (seq + d) % n_seq
        ccopies.append(send(
            cot_ref.at[:, rows_of(to, span)], call.at[mine], cs.at[d - 1], cr.at[d - 1], in_row(to)
        ))
    xforward = []

    def forward_inputs():
        for d in range(1, chips):
            arrive(xcopies[d])
            at = rows_of((seq - 2 * d + n_seq) % n_seq, block)
            xforward.append(send(xall.at[at], xall.at[at], xs.at[chips + d - 1], xr.at[chips + d - 1], in_row(mate)))

    def relay_copy(i):
        at = slot(near[far], i)
        return remote(at, at, hs.at[i], wr.at[i, near[far]], in_column(near[edge]))

    def group_copies(i, k):
        at = slot(near[k], i)
        return [
            remote(at, at, ys.at[i, k, e - 1], yr.at[i, k, e - 1], in_group((grp + e) % n_grp))
            for e in range(1, n_grp)
        ]

    for i in range(3):
        unsent.append((relay_copy(i), inner))
        for k in range(n_sub - 1):
            unsent.extend((copy, None) for copy in group_copies(i, k))

    def landed(i, k):
        at = slot(near[k], i)
        remote(at, at, ws.at[i, k], wr.at[i, near[k]], in_column(near[k])).wait_recv()

    def share_out(i, k):
        for copy in group_copies(i, k):
            copy.start()

    def pass_on(i, k):
        landed(i, k)
        share_out(i, k)

    def steps(inside, outside):
        pl.when(inner)(inside)
        pl.when(outer)(outside)

    def group_done(i):
        for k in range(n_sub - 1):
            for copy in group_copies(i, k):
                copy.wait_recv()

    def first_inner():
        landed(0, far)
        relay_copy(0).start()
        slice_copy(1, edge).start()
        share_out(0, far)
        pass_on(0, edge)
        landed(1, far)
        relay_copy(1).start()
        slice_copy(2, edge).start()
        pass_on(0, middle)
        share_out(1, far)
        pass_on(1, edge)

    def first_outer():
        pass_on(0, edge)
        pass_on(0, middle)
        pass_on(0, far)
        pass_on(1, edge)

    def second_inner():
        landed(2, far)
        relay_copy(2).start()
        pass_on(1, middle)
        pass_on(2, edge)
        share_out(2, far)

    def second_outer():
        pass_on(1, middle)
        pass_on(1, far)
        pass_on(2, edge)

    def third_inner():
        pass_on(2, middle)

    def third_outer():
        pass_on(2, middle)
        pass_on(2, far)

    def project(i, target):
        target[...] = mul(xall[...], wall[:, i * span : (i + 1) * span], NN).astype(BF16)

    def featurize(feature, sigmoid):
        def step(b, carry):
            at = rows_of(b, block)
            for h in range(pair):
                pre = mul(act[at, h * head : (h + 1) * head], om[h], NN)
                feature[h, at, :], sigmoid[h, at, :] = activations(pre)
            return carry

        lax.fori_loop(0, n_seq, step, 0, unroll=True)

    def start_total(a):
        copies = []
        for d in range(1, n_sub):
            copies.append(send(
                tot.at[a], totin.at[a, d - 1], ts.at[a, d - 1], tr.at[a, d - 1], in_column((sub + d) % n_sub)
            ))
        return copies

    def finish_total(a, copies):
        total = tot[a]
        for d in range(1, n_sub):
            arrive(copies[d - 1])
            total = total + totin[a, d - 1]
        return total

    def start_sum(a, h):
        at = rows_of(h, head)
        part[a, at] = acc[a, at].astype(BF16)
        for k in reversed(range(n_sub - 1)):
            to = near[k]
            send_some(
                None, part.at[a, pl.ds(pl.multiple_of(h * head + to * piece, piece), piece)],
                rsin.at[a, h, sub], ss.at[a, 0, h, k], sr.at[a, 0, h, sub], in_column(to),
            )
        pending[a, 0, h] = [rsin.at[a, h, source] for source in near]

    def middle_sum(a, h):
        own = pl.ds(pl.multiple_of(h * head + sub * piece, piece), piece)
        settle(a, 0, h)
        summed = acc[a, own, :]
        for source in near:
            summed = summed + rsin[a, h, source].astype(F32)
        half[a, own, :] = summed.astype(BF16)
        for k in reversed(range(n_sub - 1)):
            send_some(
                None, half.at[a, own], half.at[a, own],
                ss.at[a, 1, h, k], sr.at[a, 1, h, sub], in_column(near[k]),
            )
        pending[a, 1, h] = [
            half.at[a, pl.ds(pl.multiple_of(h * head + source * piece, piece), piece)] for source in near
        ]

    def settle(a, stage, h):
        for k, dst in enumerate(pending.pop((a, stage, h))):
            remote(dst, dst, ss.at[a, stage, h, k], sr.at[a, stage, h, near[k]], in_column(near[k])).wait_recv()

    def body():
        steps(first_inner, first_outer)
        forward_inputs()
        for copy in later:
            copy.wait()
        group_done(0)
        for copy in xforward:
            arrive(copy)
        arrive(xcopies[0])
        project(0, act)
        featurize(kf, ks)
        tot[...] = jnp.zeros_like(tot)
        for h in range(pair):
            tot[0, pl.ds(h, 1), :] = jnp.sum(kf[h].astype(F32), axis=0, keepdims=True)
        totals = start_total(0)
        steps(second_inner, second_outer)
        group_done(1)
        if stop == 2:
            return
        project(1, va)
        for h in range(pair):
            acc[0, pl.ds(h * head, head), :] = mul(va[:, h * head : (h + 1) * head], kf[h], TN)
            start_sum(0, h)
        steps(third_inner, third_outer)
        group_done(2)
        if stop == 3:
            return
        project(2, act)
        featurize(qf, qs)
        if stop == 4:
            return
        for h in range(pair):
            middle_sum(0, h)
        total_half = finish_total(0, totals).astype(BF16)
        for copy in ccopies:
            arrive(copy)
        for h in range(pair):
            wide = jnp.broadcast_to(total_half[h : h + 1], (head, features))
            lanes = pl.ds(h * head, head)

            def scale(b, carry, h=h, wide=wide, lanes=lanes):
                at = rows_of(b, block)
                inverse = 1.0 / mul(qf[h, at, :], wide, NT)
                inv[h, at, :] = inverse
                sc[at, lanes] = (call[at, lanes].astype(F32) * loss_scale * inverse).astype(BF16)
                return carry

            lax.fori_loop(0, n_seq, scale, 0, unroll=True)
            acc[1, pl.ds(h * head, head), :] = mul(sc[:, lanes], qf[h], TN)
            start_sum(1, h)
        if stop == 5:
            return
        for h in range(pair):
            settle(0, 1, h)
            lanes = pl.ds(h * head, head)
            summary = half[0, pl.ds(h * head, head), :]

            def norms(b, carry, h=h, lanes=lanes, summary=summary):
                at = rows_of(b, block)
                inverse = inv[h, at, :]
                attended = mul(qf[h, at, :], summary, NT) * inverse
                scaled = call[at, lanes].astype(F32) * loss_scale * inverse
                nrm[h, at, :] = -jnp.sum(scaled * attended, axis=-1, keepdims=True)
                return carry

            lax.fori_loop(0, n_seq, norms, 0, unroll=True)
            tot[1, pl.ds(h, 1), :] = jnp.sum(
                qf[h].astype(F32) * nrm[h].astype(BF16).astype(F32), axis=0, keepdims=True
            )
        grads = start_total(1)
        for h in range(pair):
            middle_sum(1, h)
        if stop == 6:
            return
        for h in range(pair):
            lanes = pl.ds(h * head, head)
            summary = half[0, pl.ds(h * head, head), :]
            weight = total_half[h : h + 1].astype(F32)

            def query_grads(b, carry, h=h, lanes=lanes, summary=summary, weight=weight):
                at = rows_of(b, block)
                grad = mul(sc[at, lanes], summary, NN) + nrm[h, at, :] * weight
                grad = (grad * qs[h, at, :]).astype(BF16)
                gr[at, pl.ds(2 * span + h * head, head)] = mul(grad, om[h], NT).astype(BF16)
                return carry

            lax.fori_loop(0, n_seq, query_grads, 0, unroll=True)
        total_grad = finish_total(1, grads)

        def chip_rows(d):
            return pl.ds(pl.multiple_of((chip + d) % chips * 2 * block, 2 * block), 2 * block)

        def key_grads(d, h):
            at = chip_rows(d)
            lanes = pl.ds(h * head, head)
            summary = half[1, pl.ds(h * head, head), :]
            grad = mul(va[at, lanes], summary, NN) + total_grad[h : h + 1]
            grad = (grad * ks[h, at, :]).astype(BF16)
            gr[at, pl.ds(h * head, head)] = mul(grad, om[h], NT).astype(BF16)
            gr[at, pl.ds(span + h * head, head)] = mul(kf[h, at, :], summary, NT).astype(BF16)

        for h in range(pair):
            settle(1, 1, h)
            if stop == 7:
                continue
            for d in range(1, chips):
                key_grads(d, h)
        if stop in (7, 8):
            return

        def to_mate(d):
            copies = []
            for c in range(cuts):
                at = pl.ds(c * slab, slab)
                keep[d, c] = mul(gr[chip_rows(d), :], wall[c * slab : (c + 1) * slab, :], NT)
                mo[d, :, at] = keep[d, c, rows_of(1 - core, block), :].astype(BF16)
                copies.append(send(
                    mo.at[d, :, at], mi.at[d, :, at], ms.at[d, c], mr.at[d, c], in_row(mate)
                ))
            return copies

        for_mate = {d: to_mate(d) for d in range(1, chips)}
        outward = {}
        for d in range(1, chips):
            for c in range(cuts):
                at = pl.ds(c * slab, slab)
                arrive(for_mate[d][c])
                ro[d - 1, :, at] = (
                    keep[d, c, rows_of(core, block), :] + mi[d, :, at].astype(F32)
                ).astype(BF16)
                outward[d, c] = send(
                    ro.at[d - 1, :, at], ri.at[d - 1, :, at], os_.at[d - 1, c], or_.at[d - 1, c],
                    in_row(seat(d, core)),
                )
        for h in range(pair):
            key_grads(0, h)
        for_mate[0] = to_mate(0)
        for c in range(cuts):
            at = pl.ds(c * slab, slab)
            arrive(for_mate[0][c])
            summed = keep[0, c, rows_of(core, block), :] + mi[0, :, at].astype(F32)
            for d in range(1, chips):
                arrive(outward[d, c])
                summed = summed + ri[d - 1, :, at].astype(F32)
            out_ref[:, at] = summed.astype(BF16)

    body()
    drain()


def fits(n_grp, n_seq, n_sub, events, offsets, cotangent, query_weight, key_weight, value_weight, omega):
    heads, head, features = omega.shape
    block, width = events.shape
    pair = heads // n_seq
    rows = query_weight.shape[0]
    return (
        n_seq >= 4 and n_seq % 2 == 0 and n_grp > 1 and n_sub == 4 and heads % n_seq == 0 and pair <= 8
        and head % 128 == 0 and features % 128 == 0 and block % 128 == 0 and width % 512 == 0
        and head % (16 * n_sub) == 0 and rows % (16 * n_grp) == 0
        and n_seq * block <= 1024 and pair * features <= 512 and width <= 1024
    )


STOP = 99


def fused(n_grp, n_seq, n_sub, events, offsets, cotangent, query_weight, key_weight, value_weight, omega):
    block, width = events.shape
    heads, head, features = omega.shape
    tokens = n_seq * block
    pair = heads // n_seq
    span = pair * head
    piece = head // n_sub
    chips = n_seq // 2
    cuts = 4
    vm = pltpu.VMEM
    dma = pltpu.SemaphoreType.DMA
    scratch = [
        vm((block, width), BF16),
        vm((1, block), jnp.int32),
        vm((tokens, width), BF16),
        vm((tokens, span), BF16),
        vm((width, 3 * span), BF16),
        vm((pair, head, features), BF16),
        vm((tokens, span), BF16),
        vm((tokens, span), BF16),
        vm((pair, tokens, features), BF16),
        vm((pair, tokens, features), BF16),
        vm((pair, tokens, features), F32),
        vm((pair, tokens, features), F32),
        vm((tokens, span), BF16),
        vm((pair, tokens, head), F32),
        vm((pair, tokens, 1), F32),
        vm((tokens, 3 * span), BF16),
        vm((2, span, features), F32),
        vm((2, span, features), BF16),
        vm((2, pair, n_sub, piece, features), BF16),
        vm((2, span, features), BF16),
        vm((2, 8, features), F32),
        vm((2, n_sub - 1, 8, features), F32),
        vm((chips, cuts, 2 * block, width // cuts), F32),
        vm((chips, block, width), BF16),
        vm((chips, block, width), BF16),
        vm((chips - 1, block, width), BF16),
        vm((chips - 1, block, width), BF16),
        dma((7,)),
        dma((2 * chips - 1,)), dma((2 * chips - 1,)),
        dma((n_seq - 1,)), dma((n_seq - 1,)),
        dma((3, n_sub - 1)), dma((3, n_sub)), dma((3,)),
        dma((3, n_sub - 1, n_grp - 1)), dma((3, n_sub - 1, n_grp - 1)),
        dma((2, 2, pair, n_sub - 1)), dma((2, 2, pair, n_sub)),
        dma((2, n_sub - 1)), dma((2, n_sub - 1)),
        dma((chips, cuts)), dma((chips, cuts)),
        dma((chips - 1, cuts)), dma((chips - 1, cuts)),
    ]
    loss_scale = math.sqrt(block * n_seq * n_sub)
    return pl.pallas_call(
        functools.partial(kernel, n_grp, n_seq, n_sub, loss_scale, cuts, STOP),
        out_shape=jax.ShapeDtypeStruct((block, width), BF16),
        in_specs=[pl.BlockSpec(memory_space=pl.ANY)] * 7,
        out_specs=pl.BlockSpec(memory_space=pltpu.VMEM),
        scratch_shapes=scratch,
        compiler_params=pltpu.CompilerParams(
            collective_id=0, has_side_effects=True, vmem_limit_bytes=60 * 1024 * 1024
        ),
    )(events, offsets.reshape(1, block), cotangent, query_weight, key_weight, value_weight, omega)


def solution(mesh):
    in_specs = (
        P(("grp", "seq", "sub"), None),
        P(("grp", "seq", "sub")),
        P(("grp", "seq", "sub"), None),
        P("sub", None),
        P("sub", None),
        P("sub", None),
        P(),
    )
    out_specs = P(("grp", "seq", "sub"), None)
    n_grp, n_seq, n_sub = (mesh.shape[name] for name in ("grp", "seq", "sub"))

    def body(*args):
        if fits(n_grp, n_seq, n_sub, *args):
            return fused(n_grp, n_seq, n_sub, *args)
        return local(*args)

    return jax.shard_map(body, mesh=mesh, in_specs=in_specs, out_specs=out_specs, check_vma=False)
```

```python
import functools
import math

import jax
import jax.numpy as jnp
from jax import lax
from jax.experimental import pallas as pl
from jax.experimental.pallas import tpu as pltpu
from jax.sharding import PartitionSpec as P


def encode(events, offsets):
    half_width = events.shape[1] // 2
    indices = jnp.arange(half_width, dtype=jnp.float32)
    frequency = jnp.exp(indices * (-2.0 * math.log(10000.0) / events.shape[1]))
    angles = offsets.astype(jnp.float32)[:, None] * frequency[None, :]
    encoding = jnp.concatenate([jnp.sin(angles), jnp.cos(angles)], axis=1)
    return (events.astype(jnp.float32) + encoding).astype(jnp.bfloat16)


def split_heads(matrix, head_count):
    return matrix.reshape(matrix.shape[0], head_count, matrix.shape[1] // head_count)


def transposed(left, weight):
    return lax.dot_general(
        left, weight, (((1,), (1,)), ((), ())), preferred_element_type=jnp.float32
    )


def local(events, offsets, cotangent, query_weight, key_weight, value_weight, omega):
    widened_rows = jnp.float32
    head_count = omega.shape[0]
    local_rows = events.shape[0]
    model_width = events.shape[1]
    all_tokens = local_rows * lax.axis_size("seq") * lax.axis_size("sub")
    loss_scale = math.sqrt(all_tokens)
    inputs = encode(events, offsets)
    gathered = (
        lax.all_gather(query_weight, "sub", axis=0, tiled=True),
        lax.all_gather(key_weight, "sub", axis=0, tiled=True),
        lax.all_gather(value_weight, "sub", axis=0, tiled=True),
    )
    queries, key_act, value_act = [
        jnp.dot(inputs, weight, preferred_element_type=widened_rows).astype(jnp.bfloat16)
        for weight in gathered
    ]
    query_pre = jnp.einsum(
        "thd,hdm->thm", split_heads(queries, head_count), omega, preferred_element_type=widened_rows
    )
    key_pre = jnp.einsum(
        "thd,hdm->thm", split_heads(key_act, head_count), omega, preferred_element_type=widened_rows
    )
    query_feature_map = jax.nn.softplus(query_pre).astype(jnp.bfloat16)
    key_feature_map = jax.nn.softplus(key_pre).astype(jnp.bfloat16)
    value_per_head = split_heads(value_act, head_count)
    local_digest = jnp.einsum(
        "reb,rec->ebc", key_feature_map, value_per_head, preferred_element_type=widened_rows
    )
    local_total = jnp.sum(key_feature_map, axis=0, dtype=widened_rows)
    state_digest, key_total = lax.psum((local_digest, local_total), ("seq", "sub"))
    digest_halves = state_digest.astype(jnp.bfloat16)
    total_half = key_total.astype(jnp.bfloat16)
    numerator = jnp.einsum(
        "xls,lsk->xlk", query_feature_map, digest_halves, preferred_element_type=widened_rows
    )
    denom = jnp.einsum(
        "thm,hm->th", query_feature_map, total_half, preferred_element_type=widened_rows
    )
    attended = numerator / denom[..., None]
    upstream = split_heads(cotangent, head_count).astype(widened_rows) * loss_scale
    scaled_grad = upstream / denom[..., None]
    norm_grad = -jnp.sum(scaled_grad * attended, axis=-1)
    scaled_halves = scaled_grad.astype(jnp.bfloat16)
    norm_half = norm_grad.astype(jnp.bfloat16)
    local_gradient = jnp.einsum(
        "reb,rec->ebc", query_feature_map, scaled_halves, preferred_element_type=widened_rows
    )
    local_norm = jnp.einsum(
        "thm,th->hm", query_feature_map, norm_half, preferred_element_type=widened_rows
    )
    summary_grad, overall_gradient = lax.psum((local_gradient, local_norm), ("seq", "sub"))
    gradient_halves = summary_grad.astype(jnp.bfloat16)
    query_feature_gradient = jnp.einsum(
        "pfy,fly->pfl", scaled_halves, digest_halves, preferred_element_type=widened_rows
    )
    query_feature_gradient = (
        query_feature_gradient + norm_grad[..., None] * total_half.astype(widened_rows)[None]
    )
    key_feature_gradient = (
        jnp.einsum(
            "pfy,fly->pfl", value_per_head, gradient_halves, preferred_element_type=widened_rows
        )
        + overall_gradient[None]
    )
    value_gradient = jnp.einsum(
        "xls,lsk->xlk", key_feature_map, gradient_halves, preferred_element_type=widened_rows
    ).astype(jnp.bfloat16)
    query_pre_grad = (query_feature_gradient * jax.nn.sigmoid(query_pre)).astype(jnp.bfloat16)
    key_pre_grad = (key_feature_gradient * jax.nn.sigmoid(key_pre)).astype(jnp.bfloat16)
    query_grad = jnp.einsum(
        "thm,hdm->thd", query_pre_grad, omega, preferred_element_type=widened_rows
    ).astype(jnp.bfloat16)
    key_grad = jnp.einsum(
        "thm,hdm->thd", key_pre_grad, omega, preferred_element_type=widened_rows
    ).astype(jnp.bfloat16)
    query_flat = query_grad.reshape(local_rows, model_width)
    key_flat = key_grad.reshape(local_rows, model_width)
    value_flat = value_gradient.reshape(local_rows, model_width)
    summed = transposed(query_flat, gathered[0])
    summed = summed + transposed(key_flat, gathered[1])
    summed = summed + transposed(value_flat, gathered[2])
    return summed.astype(jnp.bfloat16)


F32, BF16 = jnp.float32, jnp.bfloat16
MESH = pl.DeviceIdType.MESH
NN = (((1,), (0,)), ((), ()))
NT = (((1,), (1,)), ((), ()))
TN = (((0,), (0,)), ((), ()))


def mul(left, right, dims):
    return lax.dot_general(left, right, dims, preferred_element_type=F32)


def activations(pre):
    small = jnp.exp(-jnp.abs(pre))
    feature = jnp.maximum(pre, 0.0) + jnp.log1p(small)
    sigmoid = jnp.where(pre >= 0.0, 1.0, small) / (1.0 + small)
    return feature.astype(BF16), sigmoid


def encoded(events, offsets):
    block, width = events.shape
    row = lax.broadcasted_iota(jnp.int32, (block, block), 0)
    lane = lax.broadcasted_iota(jnp.int32, (block, block), 1)
    spread = jnp.broadcast_to(offsets.astype(F32), (block, block))
    column = jnp.sum(jnp.where(row == lane, spread, 0.0), axis=1, keepdims=True)
    indices = lax.broadcasted_iota(jnp.int32, (1, width // 2), 1).astype(F32)
    frequency = jnp.exp(indices * (-2.0 * math.log(10000.0) / width))
    angles = column * frequency
    turns = jnp.floor(angles * (2.0 / math.pi) + 0.5)
    rest = angles - turns * 1.5703125
    rest = rest - turns * 4.837512969970703125e-4
    rest = rest - turns * 7.54978994e-8
    square = rest * rest
    sine = ((-1.9515295891e-4 * square + 8.3321608736e-3) * square - 1.6666654611e-1) * square * rest + rest
    cosine = ((2.443315711809948e-5 * square - 1.388731625493765e-3) * square + 4.166664568298827e-2)
    cosine = cosine * square * square - 0.5 * square + 1.0
    halves = jnp.floor(turns * 0.5)
    odd = turns - 2.0 * halves
    sign = 1.0 - 2.0 * (halves - 2.0 * jnp.floor(halves * 0.5))
    swap = odd > 0.5
    sines = jnp.where(swap, cosine, sine) * sign
    cosines = jnp.where(swap, -sine, cosine) * sign
    wide = events.astype(F32)
    return (
        (wide[:, : width // 2] + sines).astype(BF16),
        (wide[:, width // 2 :] + cosines).astype(BF16),
    )


def kernel(
    n_grp, n_seq, n_sub, loss_scale, cuts, stop,
    ev_ref, off_ref, cot_ref, wq_ref, wk_ref, wv_ref, omega_ref, out_ref,
    ev, xall, call, wall, om, act, va, qf, kf, qs, ks, sc, inv, nrm, gr,
    acc, part, rsin, half, tot, totin, keep, mo, mi, ro, ri,
    local_sem, xs, xr, cs, cr, ws, wr, hs, ys, yr, ss, sr, ts, tr, ms, mr, os_, or_,
):
    grp, seq, sub = lax.axis_index("grp"), lax.axis_index("seq"), lax.axis_index("sub")
    chips = n_seq // 2
    chip, core = seq // 2, seq % 2
    mate = 2 * chip + 1 - core
    block, width = ev_ref.shape
    pair, head, features = om.shape
    span = pair * head
    rows = wq_ref.shape[0]
    share = rows // n_grp
    piece = head // n_sub
    slab = width // cuts
    edge, middle, far = range(n_sub - 1)

    def in_row(index):
        return {"grp": grp, "seq": index, "sub": sub}

    def in_column(index):
        return {"grp": grp, "seq": seq, "sub": index}

    def in_group(index):
        return {"grp": index, "seq": seq, "sub": sub}

    def seat(d, which):
        return 2 * ((chip + d) % chips) + which

    def rows_of(index, size):
        return pl.ds(pl.multiple_of(index * size, size), size)

    def nearest(k):
        found = 0
        for s in range(n_sub):
            others = sorted((abs(s - t), -abs(2 * t - n_sub + 1), t) for t in range(n_sub) if t != s)
            found = found + jnp.where(sub == s, others[k][2], 0)
        return found

    near = [nearest(k) for k in range(n_sub - 1)]
    unsent, unread, pending = [], [], {}

    def remote(src, dst, send_sem, recv_sem, device):
        return pltpu.make_async_remote_copy(
            src_ref=src, dst_ref=dst, send_sem=send_sem, recv_sem=recv_sem,
            device_id=device, device_id_type=MESH,
        )

    def send(src, dst, send_sem, recv_sem, device):
        copy = remote(src, dst, send_sem, recv_sem, device)
        copy.start()
        unsent.append((copy, None))
        unread.append(copy)
        return copy

    def send_some(condition, src, dst, send_sem, recv_sem, device):
        copy = remote(src, dst, send_sem, recv_sem, device)
        if condition is None:
            copy.start()
        else:
            pl.when(condition)(copy.start)
        unsent.append((copy, condition))

    def arrive(copy):
        copy.wait_recv()
        unread[:] = [other for other in unread if other is not copy]

    def drain():
        for key in list(pending):
            settle(*key)
        for copy in unread:
            copy.wait_recv()
        for copy, condition in unsent:
            if condition is None:
                copy.wait_send()
            else:
                pl.when(condition)(copy.wait_send)

    barrier = pltpu.get_barrier_semaphore()
    for d in range(1, n_seq):
        pl.semaphore_signal(barrier, inc=1, device_id=in_row((seq + d) % n_seq), device_id_type=MESH)
    for d in range(1, n_sub):
        pl.semaphore_signal(barrier, inc=1, device_id=in_column((sub + d) % n_sub), device_id_type=MESH)
    for d in range(1, n_grp):
        pl.semaphore_signal(barrier, inc=1, device_id=in_group((grp + d) % n_grp), device_id_type=MESH)

    weights = (wk_ref, wv_ref, wq_ref)
    mine = rows_of(seq, block)
    columns = rows_of(seq, span)

    def local(src, dst, index):
        copy = pltpu.make_async_copy(src, dst, local_sem.at[index])
        copy.start()
        return copy

    first = [local(ev_ref, ev, 0)]
    later = [
        local(w.at[:, columns], wall.at[rows_of(sub, rows), pl.ds(i * span, span)], 2 + i)
        for i, w in enumerate(weights)
    ]
    later.append(local(omega_ref.at[rows_of(seq, pair)], om, 5))
    later.append(local(cot_ref.at[:, columns], call.at[mine], 6))
    pl.semaphore_wait(barrier, n_seq + n_sub + n_grp - 3)

    def slot(source, i):
        return wall.at[
            pl.ds(pl.multiple_of(source * rows + grp * share, share), share), pl.ds(i * span, span)
        ]

    inner = (sub > 0) & (sub < n_sub - 1)
    outer = jnp.logical_not(inner)

    def slice_copy(i, k):
        return remote(
            weights[i].at[rows_of(grp, share), columns], slot(sub, i),
            ws.at[i, k], wr.at[i, sub], in_column(near[k]),
        )

    @pl.when(inner)
    def _():
        slice_copy(0, edge).start()
        slice_copy(0, middle).start()
        slice_copy(0, far).start()
        slice_copy(1, edge).start()
        slice_copy(2, edge).start()
        slice_copy(1, far).start()
        slice_copy(1, middle).start()
        slice_copy(2, far).start()
        slice_copy(2, middle).start()

    @pl.when(outer)
    def _():
        slice_copy(0, middle).start()
        slice_copy(0, far).start()
        slice_copy(0, edge).start()
        for i in (1, 2):
            slice_copy(i, edge).start()
            slice_copy(i, middle).start()

    for i in range(3):
        unsent.append((slice_copy(i, far), inner if i else None))
        unsent.append((slice_copy(i, middle), None))
        unsent.append((slice_copy(i, edge), None))

    for copy in first:
        copy.wait()
    low, high = encoded(ev[...], off_ref[...])
    xall[mine, : width // 2] = low
    xall[mine, width // 2 :] = high
    xcopies = {}
    for d in range(1, chips):
        xcopies[d] = send(xall.at[mine], xall.at[mine], xs.at[d], xr.at[d], in_row(seat(d, core)))
    xcopies[0] = send(xall.at[mine], xall.at[mine], xs.at[0], xr.at[0], in_row(mate))
    ccopies = []
    for d in range(1, n_seq):
        to = (seq + d) % n_seq
        ccopies.append(send(
            cot_ref.at[:, rows_of(to, span)], call.at[mine], cs.at[d - 1], cr.at[d - 1], in_row(to)
        ))
    xforward = []

    def forward_inputs():
        for d in range(1, chips):
            arrive(xcopies[d])
            at = rows_of((seq - 2 * d + n_seq) % n_seq, block)
            xforward.append(send(xall.at[at], xall.at[at], xs.at[chips + d - 1], xr.at[chips + d - 1], in_row(mate)))

    def relay_copy(i):
        at = slot(near[far], i)
        return remote(at, at, hs.at[i], wr.at[i, near[far]], in_column(near[edge]))

    def group_copies(i, k):
        at = slot(near[k], i)
        return [
            remote(at, at, ys.at[i, k, e - 1], yr.at[i, k, e - 1], in_group((grp + e) % n_grp))
            for e in range(1, n_grp)
        ]

    for i in range(3):
        if i:
            unsent.append((relay_copy(i), inner))
        for k in range(n_sub - 1):
            unsent.extend((copy, None) for copy in group_copies(i, k))

    def landed(i, k):
        at = slot(near[k], i)
        remote(at, at, ws.at[i, k], wr.at[i, near[k]], in_column(near[k])).wait_recv()

    def share_out(i, k):
        for copy in group_copies(i, k):
            copy.start()

    def pass_on(i, k):
        landed(i, k)
        share_out(i, k)

    def steps(inside, outside):
        pl.when(inner)(inside)
        pl.when(outer)(outside)

    def group_done(i):
        for k in range(n_sub - 1):
            for copy in group_copies(i, k):
                copy.wait_recv()

    def relay_on(i):
        landed(i, far)
        relay_copy(i).start()

    def first_inner():
        pass_on(0, far)
        pass_on(0, edge)
        pass_on(0, middle)
        pass_on(1, edge)
        relay_on(1)
        share_out(1, far)

    def first_outer():
        pass_on(0, edge)
        pass_on(0, far)
        pass_on(1, edge)
        pass_on(0, middle)
        pass_on(2, edge)

    def second_inner():
        pass_on(2, edge)

    def second_outer():
        pass_on(1, middle)

    def third_inner():
        relay_on(2)
        pass_on(1, middle)
        share_out(2, far)

    def third_outer():
        pass_on(1, far)

    def fourth_inner():
        pass_on(2, middle)

    def fourth_outer():
        pass_on(2, far)
        pass_on(2, middle)

    def project(i, target):
        target[...] = mul(xall[...], wall[:, i * span : (i + 1) * span], NN).astype(BF16)

    def featurize(feature, sigmoid):
        def step(b, carry):
            at = rows_of(b, block)
            for h in range(pair):
                pre = mul(act[at, h * head : (h + 1) * head], om[h], NN)
                feature[h, at, :], sigmoid[h, at, :] = activations(pre)
            return carry

        lax.fori_loop(0, n_seq, step, 0, unroll=True)

    def start_total(a):
        copies = []
        for d in range(1, n_sub):
            copies.append(send(
                tot.at[a], totin.at[a, d - 1], ts.at[a, d - 1], tr.at[a, d - 1], in_column((sub + d) % n_sub)
            ))
        return copies

    def finish_total(a, copies):
        total = tot[a]
        for d in range(1, n_sub):
            arrive(copies[d - 1])
            total = total + totin[a, d - 1]
        return total

    def start_sum(a, h):
        at = rows_of(h, head)
        part[a, at] = acc[a, at].astype(BF16)
        for k in reversed(range(n_sub - 1)):
            to = near[k]
            send_some(
                None, part.at[a, pl.ds(pl.multiple_of(h * head + to * piece, piece), piece)],
                rsin.at[a, h, sub], ss.at[a, 0, h, k], sr.at[a, 0, h, sub], in_column(to),
            )
        pending[a, 0, h] = [rsin.at[a, h, source] for source in near]

    def middle_sum(a, h):
        own = pl.ds(pl.multiple_of(h * head + sub * piece, piece), piece)
        settle(a, 0, h)
        summed = acc[a, own, :]
        for source in near:
            summed = summed + rsin[a, h, source].astype(F32)
        half[a, own, :] = summed.astype(BF16)
        for k in reversed(range(n_sub - 1)):
            send_some(
                None, half.at[a, own], half.at[a, own],
                ss.at[a, 1, h, k], sr.at[a, 1, h, sub], in_column(near[k]),
            )
        pending[a, 1, h] = [
            half.at[a, pl.ds(pl.multiple_of(h * head + source * piece, piece), piece)] for source in near
        ]

    def settle(a, stage, h):
        for k, dst in enumerate(pending.pop((a, stage, h))):
            remote(dst, dst, ss.at[a, stage, h, k], sr.at[a, stage, h, near[k]], in_column(near[k])).wait_recv()

    def body():
        steps(first_inner, first_outer)
        forward_inputs()
        for copy in later:
            copy.wait()
        steps(second_inner, second_outer)
        group_done(0)
        for copy in xforward:
            arrive(copy)
        arrive(xcopies[0])
        project(0, act)
        steps(third_inner, third_outer)
        featurize(kf, ks)
        steps(fourth_inner, fourth_outer)
        tot[...] = jnp.zeros_like(tot)
        for h in range(pair):
            tot[0, pl.ds(h, 1), :] = jnp.sum(kf[h].astype(F32), axis=0, keepdims=True)
        totals = start_total(0)
        group_done(1)
        if stop == 2:
            return
        project(1, va)
        for h in range(pair):
            acc[0, pl.ds(h * head, head), :] = mul(va[:, h * head : (h + 1) * head], kf[h], TN)
            start_sum(0, h)
        group_done(2)
        if stop == 3:
            return
        project(2, act)
        featurize(qf, qs)
        if stop == 4:
            return
        total_half = finish_total(0, totals).astype(BF16)
        for copy in ccopies:
            arrive(copy)
        for h in range(pair):
            wide = jnp.broadcast_to(total_half[h : h + 1], (head, features))
            lanes = pl.ds(h * head, head)

            def scale(b, carry, h=h, wide=wide, lanes=lanes):
                at = rows_of(b, block)
                inverse = 1.0 / mul(qf[h, at, :], wide, NT)
                inv[h, at, :] = inverse
                sc[at, lanes] = (call[at, lanes].astype(F32) * loss_scale * inverse).astype(BF16)
                return carry

            lax.fori_loop(0, n_seq, scale, 0, unroll=True)
            acc[1, pl.ds(h * head, head), :] = mul(sc[:, lanes], qf[h], TN)
            start_sum(1, h)
        for h in range(pair):
            middle_sum(0, h)
        for h in range(pair):
            middle_sum(1, h)
        if stop == 5:
            return
        for h in range(pair):
            settle(0, 1, h)
            lanes = pl.ds(h * head, head)
            summary = half[0, pl.ds(h * head, head), :]

            def norms(b, carry, h=h, lanes=lanes, summary=summary):
                at = rows_of(b, block)
                inverse = inv[h, at, :]
                attended = mul(qf[h, at, :], summary, NT) * inverse
                scaled = call[at, lanes].astype(F32) * loss_scale * inverse
                nrm[h, at, :] = -jnp.sum(scaled * attended, axis=-1, keepdims=True)
                return carry

            lax.fori_loop(0, n_seq, norms, 0, unroll=True)
            tot[1, pl.ds(h, 1), :] = jnp.sum(
                qf[h].astype(F32) * nrm[h].astype(BF16).astype(F32), axis=0, keepdims=True
            )
        grads = start_total(1)
        if stop == 6:
            return
        for h in range(pair):
            lanes = pl.ds(h * head, head)
            summary = half[0, pl.ds(h * head, head), :]
            weight = total_half[h : h + 1].astype(F32)

            def query_grads(b, carry, h=h, lanes=lanes, summary=summary, weight=weight):
                at = rows_of(b, block)
                grad = mul(sc[at, lanes], summary, NN) + nrm[h, at, :] * weight
                grad = (grad * qs[h, at, :]).astype(BF16)
                gr[at, pl.ds(2 * span + h * head, head)] = mul(grad, om[h], NT).astype(BF16)
                return carry

            lax.fori_loop(0, n_seq, query_grads, 0, unroll=True)
        total_grad = finish_total(1, grads)

        def chip_rows(d):
            return pl.ds(pl.multiple_of((chip + d) % chips * 2 * block, 2 * block), 2 * block)

        def key_grads(d, h):
            at = chip_rows(d)
            lanes = pl.ds(h * head, head)
            summary = half[1, pl.ds(h * head, head), :]
            grad = mul(va[at, lanes], summary, NN) + total_grad[h : h + 1]
            grad = (grad * ks[h, at, :]).astype(BF16)
            gr[at, pl.ds(h * head, head)] = mul(grad, om[h], NT).astype(BF16)
            gr[at, pl.ds(span + h * head, head)] = mul(kf[h, at, :], summary, NT).astype(BF16)

        for h in range(pair):
            settle(1, 1, h)
            if stop == 7:
                continue
            for d in range(1, chips):
                key_grads(d, h)
        if stop in (7, 8):
            return

        def to_mate(d):
            copies = []
            for c in range(cuts):
                at = pl.ds(c * slab, slab)
                keep[d, c] = mul(gr[chip_rows(d), :], wall[c * slab : (c + 1) * slab, :], NT)
                mo[d, :, at] = keep[d, c, rows_of(1 - core, block), :].astype(BF16)
                copies.append(send(
                    mo.at[d, :, at], mi.at[d, :, at], ms.at[d, c], mr.at[d, c], in_row(mate)
                ))
            return copies

        for_mate = {d: to_mate(d) for d in range(1, chips)}
        outward = {}
        for d in range(1, chips):
            for c in range(cuts):
                at = pl.ds(c * slab, slab)
                arrive(for_mate[d][c])
                ro[d - 1, :, at] = (
                    keep[d, c, rows_of(core, block), :] + mi[d, :, at].astype(F32)
                ).astype(BF16)
                outward[d, c] = send(
                    ro.at[d - 1, :, at], ri.at[d - 1, :, at], os_.at[d - 1, c], or_.at[d - 1, c],
                    in_row(seat(d, core)),
                )
        for h in range(pair):
            key_grads(0, h)
        for_mate[0] = to_mate(0)
        for c in range(cuts):
            at = pl.ds(c * slab, slab)
            arrive(for_mate[0][c])
            summed = keep[0, c, rows_of(core, block), :] + mi[0, :, at].astype(F32)
            for d in range(1, chips):
                arrive(outward[d, c])
                summed = summed + ri[d - 1, :, at].astype(F32)
            out_ref[:, at] = summed.astype(BF16)

    body()
    drain()


def fits(n_grp, n_seq, n_sub, events, offsets, cotangent, query_weight, key_weight, value_weight, omega):
    heads, head, features = omega.shape
    block, width = events.shape
    pair = heads // n_seq
    rows = query_weight.shape[0]
    return (
        n_seq >= 4 and n_seq % 2 == 0 and n_grp > 1 and n_sub == 4 and heads % n_seq == 0 and pair <= 8
        and head % 128 == 0 and features % 128 == 0 and block % 128 == 0 and width % 512 == 0
        and head % (16 * n_sub) == 0 and rows % (16 * n_grp) == 0
        and n_seq * block <= 1024 and pair * features <= 512 and width <= 1024
    )


STOP = 99


def fused(n_grp, n_seq, n_sub, events, offsets, cotangent, query_weight, key_weight, value_weight, omega):
    block, width = events.shape
    heads, head, features = omega.shape
    tokens = n_seq * block
    pair = heads // n_seq
    span = pair * head
    piece = head // n_sub
    chips = n_seq // 2
    cuts = 4
    vm = pltpu.VMEM
    dma = pltpu.SemaphoreType.DMA
    scratch = [
        vm((block, width), BF16),
        vm((tokens, width), BF16),
        vm((tokens, span), BF16),
        vm((width, 3 * span), BF16),
        vm((pair, head, features), BF16),
        vm((tokens, span), BF16),
        vm((tokens, span), BF16),
        vm((pair, tokens, features), BF16),
        vm((pair, tokens, features), BF16),
        vm((pair, tokens, features), F32),
        vm((pair, tokens, features), F32),
        vm((tokens, span), BF16),
        vm((pair, tokens, head), F32),
        vm((pair, tokens, 1), F32),
        vm((tokens, 3 * span), BF16),
        vm((2, span, features), F32),
        vm((2, span, features), BF16),
        vm((2, pair, n_sub, piece, features), BF16),
        vm((2, span, features), BF16),
        vm((2, 8, features), F32),
        vm((2, n_sub - 1, 8, features), F32),
        vm((chips, cuts, 2 * block, width // cuts), F32),
        vm((chips, block, width), BF16),
        vm((chips, block, width), BF16),
        vm((chips - 1, block, width), BF16),
        vm((chips - 1, block, width), BF16),
        dma((7,)),
        dma((2 * chips - 1,)), dma((2 * chips - 1,)),
        dma((n_seq - 1,)), dma((n_seq - 1,)),
        dma((3, n_sub - 1)), dma((3, n_sub)), dma((3,)),
        dma((3, n_sub - 1, n_grp - 1)), dma((3, n_sub - 1, n_grp - 1)),
        dma((2, 2, pair, n_sub - 1)), dma((2, 2, pair, n_sub)),
        dma((2, n_sub - 1)), dma((2, n_sub - 1)),
        dma((chips, cuts)), dma((chips, cuts)),
        dma((chips - 1, cuts)), dma((chips - 1, cuts)),
    ]
    loss_scale = math.sqrt(block * n_seq * n_sub)
    return pl.pallas_call(
        functools.partial(kernel, n_grp, n_seq, n_sub, loss_scale, cuts, STOP),
        out_shape=jax.ShapeDtypeStruct((block, width), BF16),
        in_specs=[pl.BlockSpec(memory_space=pl.ANY), pl.BlockSpec(memory_space=pltpu.VMEM)] + [pl.BlockSpec(memory_space=pl.ANY)] * 5,
        out_specs=pl.BlockSpec(memory_space=pltpu.VMEM),
        scratch_shapes=scratch,
        compiler_params=pltpu.CompilerParams(
            collective_id=0, has_side_effects=True, vmem_limit_bytes=54784 * 1024
        ),
    )(events, offsets.reshape(1, block), cotangent, query_weight, key_weight, value_weight, omega)


def solution(mesh):
    in_specs = (
        P(("grp", "seq", "sub"), None),
        P(("grp", "seq", "sub")),
        P(("grp", "seq", "sub"), None),
        P("sub", None),
        P("sub", None),
        P("sub", None),
        P(),
    )
    out_specs = P(("grp", "seq", "sub"), None)
    n_grp, n_seq, n_sub = (mesh.shape[name] for name in ("grp", "seq", "sub"))

    def body(*args):
        if fits(n_grp, n_seq, n_sub, *args):
            return fused(n_grp, n_seq, n_sub, *args)
        return local(*args)

    return jax.shard_map(body, mesh=mesh, in_specs=in_specs, out_specs=out_specs, check_vma=False)
```

```python
import functools
import math

import jax
import jax.numpy as jnp
from jax import lax
from jax.experimental import pallas as pl
from jax.experimental.pallas import tpu as pltpu
from jax.sharding import PartitionSpec as P


def encode(events, offsets):
    half_width = events.shape[1] // 2
    indices = jnp.arange(half_width, dtype=jnp.float32)
    frequency = jnp.exp(indices * (-2.0 * math.log(10000.0) / events.shape[1]))
    angles = offsets.astype(jnp.float32)[:, None] * frequency[None, :]
    encoding = jnp.concatenate([jnp.sin(angles), jnp.cos(angles)], axis=1)
    return (events.astype(jnp.float32) + encoding).astype(jnp.bfloat16)


def split_heads(matrix, head_count):
    return matrix.reshape(matrix.shape[0], head_count, matrix.shape[1] // head_count)


def transposed(left, weight):
    return lax.dot_general(
        left, weight, (((1,), (1,)), ((), ())), preferred_element_type=jnp.float32
    )


def local(events, offsets, cotangent, query_weight, key_weight, value_weight, omega):
    widened_rows = jnp.float32
    head_count = omega.shape[0]
    local_rows = events.shape[0]
    model_width = events.shape[1]
    all_tokens = local_rows * lax.axis_size("seq") * lax.axis_size("sub")
    loss_scale = math.sqrt(all_tokens)
    inputs = encode(events, offsets)
    gathered = (
        lax.all_gather(query_weight, "sub", axis=0, tiled=True),
        lax.all_gather(key_weight, "sub", axis=0, tiled=True),
        lax.all_gather(value_weight, "sub", axis=0, tiled=True),
    )
    queries, key_act, value_act = [
        jnp.dot(inputs, weight, preferred_element_type=widened_rows).astype(jnp.bfloat16)
        for weight in gathered
    ]
    query_pre = jnp.einsum(
        "thd,hdm->thm", split_heads(queries, head_count), omega, preferred_element_type=widened_rows
    )
    key_pre = jnp.einsum(
        "thd,hdm->thm", split_heads(key_act, head_count), omega, preferred_element_type=widened_rows
    )
    query_feature_map = jax.nn.softplus(query_pre).astype(jnp.bfloat16)
    key_feature_map = jax.nn.softplus(key_pre).astype(jnp.bfloat16)
    value_per_head = split_heads(value_act, head_count)
    local_digest = jnp.einsum(
        "reb,rec->ebc", key_feature_map, value_per_head, preferred_element_type=widened_rows
    )
    local_total = jnp.sum(key_feature_map, axis=0, dtype=widened_rows)
    state_digest, key_total = lax.psum((local_digest, local_total), ("seq", "sub"))
    digest_halves = state_digest.astype(jnp.bfloat16)
    total_half = key_total.astype(jnp.bfloat16)
    numerator = jnp.einsum(
        "xls,lsk->xlk", query_feature_map, digest_halves, preferred_element_type=widened_rows
    )
    denom = jnp.einsum(
        "thm,hm->th", query_feature_map, total_half, preferred_element_type=widened_rows
    )
    attended = numerator / denom[..., None]
    upstream = split_heads(cotangent, head_count).astype(widened_rows) * loss_scale
    scaled_grad = upstream / denom[..., None]
    norm_grad = -jnp.sum(scaled_grad * attended, axis=-1)
    scaled_halves = scaled_grad.astype(jnp.bfloat16)
    norm_half = norm_grad.astype(jnp.bfloat16)
    local_gradient = jnp.einsum(
        "reb,rec->ebc", query_feature_map, scaled_halves, preferred_element_type=widened_rows
    )
    local_norm = jnp.einsum(
        "thm,th->hm", query_feature_map, norm_half, preferred_element_type=widened_rows
    )
    summary_grad, overall_gradient = lax.psum((local_gradient, local_norm), ("seq", "sub"))
    gradient_halves = summary_grad.astype(jnp.bfloat16)
    query_feature_gradient = jnp.einsum(
        "pfy,fly->pfl", scaled_halves, digest_halves, preferred_element_type=widened_rows
    )
    query_feature_gradient = (
        query_feature_gradient + norm_grad[..., None] * total_half.astype(widened_rows)[None]
    )
    key_feature_gradient = (
        jnp.einsum(
            "pfy,fly->pfl", value_per_head, gradient_halves, preferred_element_type=widened_rows
        )
        + overall_gradient[None]
    )
    value_gradient = jnp.einsum(
        "xls,lsk->xlk", key_feature_map, gradient_halves, preferred_element_type=widened_rows
    ).astype(jnp.bfloat16)
    query_pre_grad = (query_feature_gradient * jax.nn.sigmoid(query_pre)).astype(jnp.bfloat16)
    key_pre_grad = (key_feature_gradient * jax.nn.sigmoid(key_pre)).astype(jnp.bfloat16)
    query_grad = jnp.einsum(
        "thm,hdm->thd", query_pre_grad, omega, preferred_element_type=widened_rows
    ).astype(jnp.bfloat16)
    key_grad = jnp.einsum(
        "thm,hdm->thd", key_pre_grad, omega, preferred_element_type=widened_rows
    ).astype(jnp.bfloat16)
    query_flat = query_grad.reshape(local_rows, model_width)
    key_flat = key_grad.reshape(local_rows, model_width)
    value_flat = value_gradient.reshape(local_rows, model_width)
    summed = transposed(query_flat, gathered[0])
    summed = summed + transposed(key_flat, gathered[1])
    summed = summed + transposed(value_flat, gathered[2])
    return summed.astype(jnp.bfloat16)


F32, BF16 = jnp.float32, jnp.bfloat16
MESH = pl.DeviceIdType.MESH
NN = (((1,), (0,)), ((), ()))
NT = (((1,), (1,)), ((), ()))
TN = (((0,), (0,)), ((), ()))


def mul(left, right, dims):
    return lax.dot_general(left, right, dims, preferred_element_type=F32)


def activations(pre):
    small = jnp.exp(-jnp.abs(pre))
    feature = jnp.maximum(pre, 0.0) + jnp.log1p(small)
    sigmoid = jnp.where(pre >= 0.0, 1.0, small) / (1.0 + small)
    return feature.astype(BF16), sigmoid


def encoded(events, offsets):
    block, width = events.shape
    row = lax.broadcasted_iota(jnp.int32, (block, block), 0)
    lane = lax.broadcasted_iota(jnp.int32, (block, block), 1)
    spread = jnp.broadcast_to(offsets.astype(F32), (block, block))
    column = jnp.sum(jnp.where(row == lane, spread, 0.0), axis=1, keepdims=True)
    indices = lax.broadcasted_iota(jnp.int32, (1, width // 2), 1).astype(F32)
    frequency = jnp.exp(indices * (-2.0 * math.log(10000.0) / width))
    angles = column * frequency
    turns = jnp.floor(angles * (2.0 / math.pi) + 0.5)
    rest = angles - turns * 1.5703125
    rest = rest - turns * 4.837512969970703125e-4
    rest = rest - turns * 7.54978994e-8
    square = rest * rest
    sine = ((-1.9515295891e-4 * square + 8.3321608736e-3) * square - 1.6666654611e-1) * square * rest + rest
    cosine = ((2.443315711809948e-5 * square - 1.388731625493765e-3) * square + 4.166664568298827e-2)
    cosine = cosine * square * square - 0.5 * square + 1.0
    halves = jnp.floor(turns * 0.5)
    odd = turns - 2.0 * halves
    sign = 1.0 - 2.0 * (halves - 2.0 * jnp.floor(halves * 0.5))
    swap = odd > 0.5
    sines = jnp.where(swap, cosine, sine) * sign
    cosines = jnp.where(swap, -sine, cosine) * sign
    wide = events.astype(F32)
    return (
        (wide[:, : width // 2] + sines).astype(BF16),
        (wide[:, width // 2 :] + cosines).astype(BF16),
    )


def kernel(
    n_grp, n_seq, n_sub, loss_scale, cuts, stop,
    ev_ref, off_ref, cot_ref, wq_ref, wk_ref, wv_ref, omega_ref, out_ref,
    ev, off, xall, call, wall, om, act, va, qf, kf, qs, ks, sc, inv, nrm, gr,
    acc, part, rsin, half, tot, totin, keep, mo, mi, ro, ri,
    local_sem, xs, xr, cs, cr, ws, wr, hs, ys, yr, ss, sr, ts, tr, ms, mr, os_, or_,
):
    grp, seq, sub = lax.axis_index("grp"), lax.axis_index("seq"), lax.axis_index("sub")
    chips = n_seq // 2
    chip, core = seq // 2, seq % 2
    mate = 2 * chip + 1 - core
    block, width = ev_ref.shape
    pair, head, features = om.shape
    span = pair * head
    rows = wq_ref.shape[0]
    share = rows // n_grp
    piece = head // n_sub
    slab = width // cuts
    edge, middle, far = range(n_sub - 1)

    def in_row(index):
        return {"grp": grp, "seq": index, "sub": sub}

    def in_column(index):
        return {"grp": grp, "seq": seq, "sub": index}

    def in_group(index):
        return {"grp": index, "seq": seq, "sub": sub}

    def seat(d, which):
        return 2 * ((chip + d) % chips) + which

    def rows_of(index, size):
        return pl.ds(pl.multiple_of(index * size, size), size)

    def nearest(k):
        found = 0
        for s in range(n_sub):
            others = sorted((abs(s - t), -abs(2 * t - n_sub + 1), t) for t in range(n_sub) if t != s)
            found = found + jnp.where(sub == s, others[k][2], 0)
        return found

    near = [nearest(k) for k in range(n_sub - 1)]
    unsent, unread, pending = [], [], {}

    def remote(src, dst, send_sem, recv_sem, device):
        return pltpu.make_async_remote_copy(
            src_ref=src, dst_ref=dst, send_sem=send_sem, recv_sem=recv_sem,
            device_id=device, device_id_type=MESH,
        )

    def send(src, dst, send_sem, recv_sem, device):
        copy = remote(src, dst, send_sem, recv_sem, device)
        copy.start()
        unsent.append((copy, None))
        unread.append(copy)
        return copy

    def send_some(condition, src, dst, send_sem, recv_sem, device):
        copy = remote(src, dst, send_sem, recv_sem, device)
        if condition is None:
            copy.start()
        else:
            pl.when(condition)(copy.start)
        unsent.append((copy, condition))

    def arrive(copy):
        copy.wait_recv()
        unread[:] = [other for other in unread if other is not copy]

    def drain():
        for key in list(pending):
            settle(*key)
        for copy in unread:
            copy.wait_recv()
        for copy, condition in unsent:
            if condition is None:
                copy.wait_send()
            else:
                pl.when(condition)(copy.wait_send)

    barrier = pltpu.get_barrier_semaphore()
    for d in range(1, n_seq):
        pl.semaphore_signal(barrier, inc=1, device_id=in_row((seq + d) % n_seq), device_id_type=MESH)
    for d in range(1, n_sub):
        pl.semaphore_signal(barrier, inc=1, device_id=in_column((sub + d) % n_sub), device_id_type=MESH)
    for d in range(1, n_grp):
        pl.semaphore_signal(barrier, inc=1, device_id=in_group((grp + d) % n_grp), device_id_type=MESH)

    weights = (wk_ref, wv_ref, wq_ref)
    mine = rows_of(seq, block)
    columns = rows_of(seq, span)

    def local(src, dst, index):
        copy = pltpu.make_async_copy(src, dst, local_sem.at[index])
        copy.start()
        return copy

    first = [local(ev_ref, ev, 0), local(off_ref, off, 1)]
    later = [
        local(w.at[:, columns], wall.at[rows_of(sub, rows), pl.ds(i * span, span)], 2 + i)
        for i, w in enumerate(weights)
    ]
    later.append(local(omega_ref.at[rows_of(seq, pair)], om, 5))
    later.append(local(cot_ref.at[:, columns], call.at[mine], 6))
    for copy in later[:3]:
        copy.wait()
    pl.semaphore_wait(barrier, n_seq + n_sub + n_grp - 3)

    def slot(source, i):
        return wall.at[
            pl.ds(pl.multiple_of(source * rows + grp * share, share), share), pl.ds(i * span, span)
        ]

    inner = (sub > 0) & (sub < n_sub - 1)
    outer = jnp.logical_not(inner)

    def slice_copy(i, k):
        return remote(
            slot(sub, i), slot(sub, i),
            ws.at[i, k], wr.at[i, sub], in_column(near[k]),
        )

    @pl.when(inner)
    def _():
        slice_copy(0, edge).start()
        slice_copy(0, middle).start()
        slice_copy(0, far).start()
        slice_copy(1, edge).start()
        slice_copy(2, edge).start()
        slice_copy(1, far).start()
        slice_copy(1, middle).start()
        slice_copy(2, far).start()
        slice_copy(2, middle).start()

    @pl.when(outer)
    def _():
        slice_copy(0, middle).start()
        slice_copy(0, far).start()
        slice_copy(0, edge).start()
        slice_copy(1, edge).start()
        slice_copy(1, middle).start()

    for i in range(3):
        unsent.append((slice_copy(i, far), inner if i else None))
        unsent.append((slice_copy(i, middle), None))
        unsent.append((slice_copy(i, edge), None))

    for copy in first:
        copy.wait()
    low, high = encoded(ev[...], off[...])
    xall[mine, : width // 2] = low
    xall[mine, width // 2 :] = high
    xcopies = {}
    for d in range(1, chips):
        xcopies[d] = send(xall.at[mine], xall.at[mine], xs.at[d], xr.at[d], in_row(seat(d, core)))
    xcopies[0] = send(xall.at[mine], xall.at[mine], xs.at[0], xr.at[0], in_row(mate))
    ccopies = []
    for d in range(1, n_seq):
        to = (seq + d) % n_seq
        ccopies.append(send(
            cot_ref.at[:, rows_of(to, span)], call.at[mine], cs.at[d - 1], cr.at[d - 1], in_row(to)
        ))
    xforward = []

    def forward_inputs():
        for d in range(1, chips):
            arrive(xcopies[d])
            at = rows_of((seq - 2 * d + n_seq) % n_seq, block)
            xforward.append(send(xall.at[at], xall.at[at], xs.at[chips + d - 1], xr.at[chips + d - 1], in_row(mate)))

    def relay_copy(i):
        at = slot(near[far], i)
        return remote(at, at, hs.at[i], wr.at[i, near[far]], in_column(near[edge]))

    def group_copies(i, k):
        at = slot(near[k], i)
        return [
            remote(at, at, ys.at[i, k, e - 1], yr.at[i, k, e - 1], in_group((grp + e) % n_grp))
            for e in range(1, n_grp)
        ]

    for i in range(3):
        if i:
            unsent.append((relay_copy(i), inner))
        for k in range(n_sub - 1):
            unsent.extend((copy, None) for copy in group_copies(i, k))

    def landed(i, k):
        at = slot(near[k], i)
        remote(at, at, ws.at[i, k], wr.at[i, near[k]], in_column(near[k])).wait_recv()

    def share_out(i, k):
        for copy in group_copies(i, k):
            copy.start()

    def pass_on(i, k):
        landed(i, k)
        share_out(i, k)

    def steps(inside, outside):
        pl.when(inner)(inside)
        pl.when(outer)(outside)

    def group_done(i):
        for k in range(n_sub - 1):
            for copy in group_copies(i, k):
                copy.wait_recv()

    def relay_on(i):
        landed(i, far)
        relay_copy(i).start()

    def first_inner():
        pass_on(0, far)
        pass_on(0, edge)
        pass_on(0, middle)
        pass_on(1, edge)
        relay_on(1)
        share_out(1, far)

    def first_outer():
        pass_on(0, edge)
        pass_on(0, far)
        pass_on(1, edge)
        pass_on(0, middle)
        slice_copy(2, edge).start()
        slice_copy(2, middle).start()
        pass_on(2, edge)

    def second_outer():
        pass_on(1, middle)

    def third_inner():
        relay_on(2)
        pass_on(1, middle)
        pass_on(2, edge)
        share_out(2, far)

    def third_outer():
        pass_on(1, far)

    def fourth_inner():
        pass_on(2, middle)

    def fourth_outer():
        pass_on(2, far)
        pass_on(2, middle)

    def project(i, target):
        target[...] = mul(xall[...], wall[:, i * span : (i + 1) * span], NN).astype(BF16)

    def featurize(feature, sigmoid, some):
        def step(b, carry):
            at = rows_of(b, block)
            for h in some:
                pre = mul(act[at, h * head : (h + 1) * head], om[h], NN)
                feature[h, at, :], sigmoid[h, at, :] = activations(pre)
            return carry

        lax.fori_loop(0, n_seq, step, 0, unroll=True)

    def start_total(a):
        copies = []
        for d in range(1, n_sub):
            copies.append(send(
                tot.at[a], totin.at[a, d - 1], ts.at[a, d - 1], tr.at[a, d - 1], in_column((sub + d) % n_sub)
            ))
        return copies

    def finish_total(a, copies):
        total = tot[a]
        for d in range(1, n_sub):
            arrive(copies[d - 1])
            total = total + totin[a, d - 1]
        return total

    def start_sum(a):
        part[a] = acc[a].astype(BF16)
        for k in reversed(range(n_sub - 1)):
            send_some(
                None, part.at[a, :, rows_of(near[k], piece)], rsin.at[a, sub],
                ss.at[a, 0, k], sr.at[a, 0, sub], in_column(near[k]),
            )
        pending[a, 0] = [rsin.at[a, source] for source in near]

    def middle_sum(a):
        own = rows_of(sub, piece)
        settle(a, 0)
        summed = acc[a, :, own, :]
        for source in near:
            summed = summed + rsin[a, source].astype(F32)
        half[a, :, own, :] = summed.astype(BF16)
        for k in reversed(range(n_sub - 1)):
            send_some(
                None, half.at[a, :, own], half.at[a, :, own],
                ss.at[a, 1, k], sr.at[a, 1, sub], in_column(near[k]),
            )
        pending[a, 1] = [half.at[a, :, rows_of(source, piece)] for source in near]

    def settle(a, stage):
        for k, dst in enumerate(pending.pop((a, stage))):
            remote(dst, dst, ss.at[a, stage, k], sr.at[a, stage, near[k]], in_column(near[k])).wait_recv()

    def summed_half(a, h):
        return half[a, h]

    def body():
        steps(first_inner, first_outer)
        forward_inputs()
        for copy in later[3:]:
            copy.wait()
        pl.when(outer)(second_outer)
        group_done(0)
        for copy in xforward:
            arrive(copy)
        arrive(xcopies[0])
        project(0, act)
        steps(third_inner, third_outer)
        featurize(kf, ks, range(pair))
        steps(fourth_inner, fourth_outer)
        tot[...] = jnp.zeros_like(tot)
        for h in range(pair):
            tot[0, pl.ds(h, 1), :] = jnp.sum(kf[h].astype(F32), axis=0, keepdims=True)
        totals = start_total(0)
        group_done(1)
        if stop == 2:
            return
        project(1, va)
        for h in range(pair):
            acc[0, h] = mul(va[:, h * head : (h + 1) * head], kf[h], TN)
        start_sum(0)
        group_done(2)
        if stop == 3:
            return
        project(2, act)
        total_half = finish_total(0, totals).astype(BF16)
        for copy in ccopies:
            arrive(copy)
        for h in range(pair):
            featurize(qf, qs, [h])
            wide = jnp.broadcast_to(total_half[h : h + 1], (head, features))
            lanes = pl.ds(h * head, head)

            def scale(b, carry, h=h, wide=wide, lanes=lanes):
                at = rows_of(b, block)
                inverse = 1.0 / mul(qf[h, at, :], wide, NT)
                inv[h, at, :] = inverse
                sc[at, lanes] = (call[at, lanes].astype(F32) * loss_scale * inverse).astype(BF16)
                return carry

            lax.fori_loop(0, n_seq, scale, 0, unroll=True)
            acc[1, h] = mul(sc[:, lanes], qf[h], TN)
        start_sum(1)
        middle_sum(0)
        middle_sum(1)
        if stop == 5:
            return
        settle(0, 1)
        for h in range(pair):
            lanes = pl.ds(h * head, head)
            summary = half[0, h]

            def norms(b, carry, h=h, lanes=lanes, summary=summary):
                at = rows_of(b, block)
                inverse = inv[h, at, :]
                attended = mul(qf[h, at, :], summary, NT) * inverse
                scaled = call[at, lanes].astype(F32) * loss_scale * inverse
                nrm[h, at, :] = -jnp.sum(scaled * attended, axis=-1, keepdims=True)
                return carry

            lax.fori_loop(0, n_seq, norms, 0, unroll=True)
            tot[1, pl.ds(h, 1), :] = jnp.sum(
                qf[h].astype(F32) * nrm[h].astype(BF16).astype(F32), axis=0, keepdims=True
            )
        grads = start_total(1)
        if stop == 6:
            return
        for h in range(pair):
            lanes = pl.ds(h * head, head)
            summary = half[0, h]
            weight = total_half[h : h + 1].astype(F32)

            def query_grads(b, carry, h=h, lanes=lanes, summary=summary, weight=weight):
                at = rows_of(b, block)
                grad = mul(sc[at, lanes], summary, NN) + nrm[h, at, :] * weight
                grad = (grad * qs[h, at, :]).astype(BF16)
                gr[at, pl.ds(2 * span + h * head, head)] = mul(grad, om[h], NT).astype(BF16)
                return carry

            lax.fori_loop(0, n_seq, query_grads, 0, unroll=True)
        def chip_rows(d):
            return pl.ds(pl.multiple_of((chip + d) % chips * 2 * block, 2 * block), 2 * block)

        for d in range(1, chips):
            for c in range(cuts):
                keep[d, c] = mul(
                    gr[chip_rows(d), 2 * span :], wall[c * slab : (c + 1) * slab, 2 * span :], NT
                )
        def value_grads(d, h):
            at = chip_rows(d)
            gr[at, pl.ds(span + h * head, head)] = mul(kf[h, at, :], summed_half(1, h), NT).astype(BF16)

        def key_grads(d, h):
            at = chip_rows(d)
            lanes = pl.ds(h * head, head)
            grad = mul(va[at, lanes], summed_half(1, h), NN) + total_grad[h : h + 1]
            grad = (grad * ks[h, at, :]).astype(BF16)
            gr[at, pl.ds(h * head, head)] = mul(grad, om[h], NT).astype(BF16)

        settle(1, 1)
        for h in range(pair):
            for d in range(1, chips):
                value_grads(d, h)
        for d in range(1, chips):
            for c in range(cuts):
                keep[d, c] = keep[d, c] + mul(
                    gr[chip_rows(d), span : 2 * span], wall[c * slab : (c + 1) * slab, span : 2 * span], NT
                )
        total_grad = finish_total(1, grads)
        for h in range(pair):
            for d in range(1, chips):
                key_grads(d, h)
        if stop in (7, 8):
            return

        def to_mate(d):
            copies = []
            for c in range(cuts):
                at = pl.ds(c * slab, slab)
                columns_of = slice(0, span if d else 3 * span)
                grads = mul(gr[chip_rows(d), columns_of], wall[c * slab : (c + 1) * slab, columns_of], NT)
                keep[d, c] = keep[d, c] + grads if d else grads
                mo[d, :, at] = keep[d, c, rows_of(1 - core, block), :].astype(BF16)
                copies.append(send(
                    mo.at[d, :, at], mi.at[d, :, at], ms.at[d, c], mr.at[d, c], in_row(mate)
                ))
            return copies

        for_mate = {d: to_mate(d) for d in range(1, chips)}
        outward = {}
        for d in range(1, chips):
            for c in range(cuts):
                at = pl.ds(c * slab, slab)
                arrive(for_mate[d][c])
                ro[d - 1, :, at] = (
                    keep[d, c, rows_of(core, block), :] + mi[d, :, at].astype(F32)
                ).astype(BF16)
                outward[d, c] = send(
                    ro.at[d - 1, :, at], ri.at[d - 1, :, at], os_.at[d - 1, c], or_.at[d - 1, c],
                    in_row(seat(d, core)),
                )
        for h in range(pair):
            value_grads(0, h)
            key_grads(0, h)
        for_mate[0] = to_mate(0)
        for c in range(cuts):
            at = pl.ds(c * slab, slab)
            arrive(for_mate[0][c])
            summed = keep[0, c, rows_of(core, block), :] + mi[0, :, at].astype(F32)
            for d in range(1, chips):
                arrive(outward[d, c])
                summed = summed + ri[d - 1, :, at].astype(F32)
            out_ref[:, at] = summed.astype(BF16)

    body()
    drain()


def fits(n_grp, n_seq, n_sub, events, offsets, cotangent, query_weight, key_weight, value_weight, omega):
    heads, head, features = omega.shape
    block, width = events.shape
    pair = heads // n_seq
    rows = query_weight.shape[0]
    return (
        n_seq >= 4 and n_seq % 2 == 0 and n_grp > 1 and n_sub == 4 and heads % n_seq == 0 and pair <= 8
        and head % 128 == 0 and features % 128 == 0 and block % 128 == 0 and width % 512 == 0
        and head % (16 * n_sub) == 0 and rows % (16 * n_grp) == 0
        and n_seq * block <= 1024 and pair * features <= 512 and width <= 1024
    )


STOP = 99


def fused(n_grp, n_seq, n_sub, events, offsets, cotangent, query_weight, key_weight, value_weight, omega):
    block, width = events.shape
    heads, head, features = omega.shape
    tokens = n_seq * block
    pair = heads // n_seq
    span = pair * head
    piece = head // n_sub
    chips = n_seq // 2
    cuts = 4
    vm = pltpu.VMEM
    dma = pltpu.SemaphoreType.DMA
    scratch = [
        vm((block, width), BF16),
        vm((1, block), jnp.int32),
        vm((tokens, width), BF16),
        vm((tokens, span), BF16),
        vm((width, 3 * span), BF16),
        vm((pair, head, features), BF16),
        vm((tokens, span), BF16),
        vm((tokens, span), BF16),
        vm((pair, tokens, features), BF16),
        vm((pair, tokens, features), BF16),
        vm((pair, tokens, features), F32),
        vm((pair, tokens, features), F32),
        vm((tokens, span), BF16),
        vm((pair, tokens, head), F32),
        vm((pair, tokens, 1), F32),
        vm((tokens, 3 * span), BF16),
        vm((2, pair, head, features), F32),
        vm((2, pair, head, features), BF16),
        vm((2, n_sub, pair, piece, features), BF16),
        vm((2, pair, head, features), BF16),
        vm((2, 8, features), F32),
        vm((2, n_sub - 1, 8, features), F32),
        vm((chips, cuts, 2 * block, width // cuts), F32),
        vm((chips, block, width), BF16),
        vm((chips, block, width), BF16),
        vm((chips - 1, block, width), BF16),
        vm((chips - 1, block, width), BF16),
        dma((7,)),
        dma((2 * chips - 1,)), dma((2 * chips - 1,)),
        dma((n_seq - 1,)), dma((n_seq - 1,)),
        dma((3, n_sub - 1)), dma((3, n_sub)), dma((3,)),
        dma((3, n_sub - 1, n_grp - 1)), dma((3, n_sub - 1, n_grp - 1)),
        dma((2, 2, n_sub - 1)), dma((2, 2, n_sub)),
        dma((2, n_sub - 1)), dma((2, n_sub - 1)),
        dma((chips, cuts)), dma((chips, cuts)),
        dma((chips - 1, cuts)), dma((chips - 1, cuts)),
    ]
    loss_scale = math.sqrt(block * n_seq * n_sub)
    return pl.pallas_call(
        functools.partial(kernel, n_grp, n_seq, n_sub, loss_scale, cuts, STOP),
        out_shape=jax.ShapeDtypeStruct((block, width), BF16),
        in_specs=[pl.BlockSpec(memory_space=pl.ANY)] * 7,
        out_specs=pl.BlockSpec(memory_space=pltpu.VMEM),
        scratch_shapes=scratch,
        compiler_params=pltpu.CompilerParams(
            collective_id=0, has_side_effects=True, vmem_limit_bytes=48 * 1024 * 1024
        ),
    )(*[
        pltpu.with_memory_space_constraint(array, pltpu.HBM)
        for array in (
            events, offsets.reshape(1, block), cotangent, query_weight, key_weight, value_weight, omega
        )
    ])


def solution(mesh):
    in_specs = (
        P(("grp", "seq", "sub"), None),
        P(("grp", "seq", "sub")),
        P(("grp", "seq", "sub"), None),
        P("sub", None),
        P("sub", None),
        P("sub", None),
        P(),
    )
    out_specs = P(("grp", "seq", "sub"), None)
    n_grp, n_seq, n_sub = (mesh.shape[name] for name in ("grp", "seq", "sub"))

    def body(*args):
        if fits(n_grp, n_seq, n_sub, *args):
            return fused(n_grp, n_seq, n_sub, *args)
        return local(*args)

    return jax.shard_map(body, mesh=mesh, in_specs=in_specs, out_specs=out_specs, check_vma=False)
```

```python
import functools
import math

import jax
import jax.numpy as jnp
from jax import lax
from jax.experimental import pallas as pl
from jax.experimental.pallas import tpu as pltpu
from jax.sharding import PartitionSpec as P


def encode(events, offsets):
    half_width = events.shape[1] // 2
    indices = jnp.arange(half_width, dtype=jnp.float32)
    frequency = jnp.exp(indices * (-2.0 * math.log(10000.0) / events.shape[1]))
    angles = offsets.astype(jnp.float32)[:, None] * frequency[None, :]
    encoding = jnp.concatenate([jnp.sin(angles), jnp.cos(angles)], axis=1)
    return (events.astype(jnp.float32) + encoding).astype(jnp.bfloat16)


def split_heads(matrix, head_count):
    return matrix.reshape(matrix.shape[0], head_count, matrix.shape[1] // head_count)


def transposed(left, weight):
    return lax.dot_general(
        left, weight, (((1,), (1,)), ((), ())), preferred_element_type=jnp.float32
    )


def local(events, offsets, cotangent, query_weight, key_weight, value_weight, omega):
    widened_rows = jnp.float32
    head_count = omega.shape[0]
    local_rows = events.shape[0]
    model_width = events.shape[1]
    all_tokens = local_rows * lax.axis_size("seq") * lax.axis_size("sub")
    loss_scale = math.sqrt(all_tokens)
    inputs = encode(events, offsets)
    gathered = (
        lax.all_gather(query_weight, "sub", axis=0, tiled=True),
        lax.all_gather(key_weight, "sub", axis=0, tiled=True),
        lax.all_gather(value_weight, "sub", axis=0, tiled=True),
    )
    queries, key_act, value_act = [
        jnp.dot(inputs, weight, preferred_element_type=widened_rows).astype(jnp.bfloat16)
        for weight in gathered
    ]
    query_pre = jnp.einsum(
        "thd,hdm->thm", split_heads(queries, head_count), omega, preferred_element_type=widened_rows
    )
    key_pre = jnp.einsum(
        "thd,hdm->thm", split_heads(key_act, head_count), omega, preferred_element_type=widened_rows
    )
    query_feature_map = jax.nn.softplus(query_pre).astype(jnp.bfloat16)
    key_feature_map = jax.nn.softplus(key_pre).astype(jnp.bfloat16)
    value_per_head = split_heads(value_act, head_count)
    local_digest = jnp.einsum(
        "reb,rec->ebc", key_feature_map, value_per_head, preferred_element_type=widened_rows
    )
    local_total = jnp.sum(key_feature_map, axis=0, dtype=widened_rows)
    state_digest, key_total = lax.psum((local_digest, local_total), ("seq", "sub"))
    digest_halves = state_digest.astype(jnp.bfloat16)
    total_half = key_total.astype(jnp.bfloat16)
    numerator = jnp.einsum(
        "xls,lsk->xlk", query_feature_map, digest_halves, preferred_element_type=widened_rows
    )
    denom = jnp.einsum(
        "thm,hm->th", query_feature_map, total_half, preferred_element_type=widened_rows
    )
    attended = numerator / denom[..., None]
    upstream = split_heads(cotangent, head_count).astype(widened_rows) * loss_scale
    scaled_grad = upstream / denom[..., None]
    norm_grad = -jnp.sum(scaled_grad * attended, axis=-1)
    scaled_halves = scaled_grad.astype(jnp.bfloat16)
    norm_half = norm_grad.astype(jnp.bfloat16)
    local_gradient = jnp.einsum(
        "reb,rec->ebc", query_feature_map, scaled_halves, preferred_element_type=widened_rows
    )
    local_norm = jnp.einsum(
        "thm,th->hm", query_feature_map, norm_half, preferred_element_type=widened_rows
    )
    summary_grad, overall_gradient = lax.psum((local_gradient, local_norm), ("seq", "sub"))
    gradient_halves = summary_grad.astype(jnp.bfloat16)
    query_feature_gradient = jnp.einsum(
        "pfy,fly->pfl", scaled_halves, digest_halves, preferred_element_type=widened_rows
    )
    query_feature_gradient = (
        query_feature_gradient + norm_grad[..., None] * total_half.astype(widened_rows)[None]
    )
    key_feature_gradient = (
        jnp.einsum(
            "pfy,fly->pfl", value_per_head, gradient_halves, preferred_element_type=widened_rows
        )
        + overall_gradient[None]
    )
    value_gradient = jnp.einsum(
        "xls,lsk->xlk", key_feature_map, gradient_halves, preferred_element_type=widened_rows
    ).astype(jnp.bfloat16)
    query_pre_grad = (query_feature_gradient * jax.nn.sigmoid(query_pre)).astype(jnp.bfloat16)
    key_pre_grad = (key_feature_gradient * jax.nn.sigmoid(key_pre)).astype(jnp.bfloat16)
    query_grad = jnp.einsum(
        "thm,hdm->thd", query_pre_grad, omega, preferred_element_type=widened_rows
    ).astype(jnp.bfloat16)
    key_grad = jnp.einsum(
        "thm,hdm->thd", key_pre_grad, omega, preferred_element_type=widened_rows
    ).astype(jnp.bfloat16)
    query_flat = query_grad.reshape(local_rows, model_width)
    key_flat = key_grad.reshape(local_rows, model_width)
    value_flat = value_gradient.reshape(local_rows, model_width)
    summed = transposed(query_flat, gathered[0])
    summed = summed + transposed(key_flat, gathered[1])
    summed = summed + transposed(value_flat, gathered[2])
    return summed.astype(jnp.bfloat16)


F32, BF16 = jnp.float32, jnp.bfloat16
MESH = pl.DeviceIdType.MESH
NN = (((1,), (0,)), ((), ()))
NT = (((1,), (1,)), ((), ()))
TN = (((0,), (0,)), ((), ()))


def mul(left, right, dims):
    return lax.dot_general(left, right, dims, preferred_element_type=F32)


def activations(pre):
    small = jnp.exp(-jnp.abs(pre))
    feature = jnp.maximum(pre, 0.0) + jnp.log1p(small)
    sigmoid = jnp.where(pre >= 0.0, 1.0, small) / (1.0 + small)
    return feature.astype(BF16), sigmoid


def encoded(events, offsets):
    block, width = events.shape
    row = lax.broadcasted_iota(jnp.int32, (block, block), 0)
    lane = lax.broadcasted_iota(jnp.int32, (block, block), 1)
    spread = jnp.broadcast_to(offsets.astype(F32), (block, block))
    column = jnp.sum(jnp.where(row == lane, spread, 0.0), axis=1, keepdims=True)
    indices = lax.broadcasted_iota(jnp.int32, (1, width // 2), 1).astype(F32)
    frequency = jnp.exp(indices * (-2.0 * math.log(10000.0) / width))
    angles = column * frequency
    turns = jnp.floor(angles * (2.0 / math.pi) + 0.5)
    rest = angles - turns * 1.5703125
    rest = rest - turns * 4.837512969970703125e-4
    rest = rest - turns * 7.54978994e-8
    square = rest * rest
    sine = ((-1.9515295891e-4 * square + 8.3321608736e-3) * square - 1.6666654611e-1) * square * rest + rest
    cosine = ((2.443315711809948e-5 * square - 1.388731625493765e-3) * square + 4.166664568298827e-2)
    cosine = cosine * square * square - 0.5 * square + 1.0
    halves = jnp.floor(turns * 0.5)
    odd = turns - 2.0 * halves
    sign = 1.0 - 2.0 * (halves - 2.0 * jnp.floor(halves * 0.5))
    swap = odd > 0.5
    sines = jnp.where(swap, cosine, sine) * sign
    cosines = jnp.where(swap, -sine, cosine) * sign
    wide = events.astype(F32)
    return (
        (wide[:, : width // 2] + sines).astype(BF16),
        (wide[:, width // 2 :] + cosines).astype(BF16),
    )


def kernel(
    n_grp, n_seq, n_sub, loss_scale, cuts, stop,
    ev_ref, off_ref, cot_ref, wq_ref, wk_ref, wv_ref, omega_ref, out_ref,
    ev, off, xall, call, wall, om, act, va, qf, kf, qs, ks, sc, inv, nrm, gr,
    acc, part, rsin, half, tot, totin, keep, mo, mi, ro, ri,
    local_sem, xs, xr, cs, cr, ws, wr, hs, ys, yr, ss, sr, ts, tr, ms, mr, os_, or_,
):
    grp, seq, sub = lax.axis_index("grp"), lax.axis_index("seq"), lax.axis_index("sub")
    chips = n_seq // 2
    chip, core = seq // 2, seq % 2
    mate = 2 * chip + 1 - core
    block, width = ev_ref.shape
    pair, head, features = om.shape
    span = pair * head
    rows = wq_ref.shape[0]
    share = rows // n_grp
    piece = head // n_sub
    slab = width // cuts
    edge, middle, far = range(n_sub - 1)

    def in_row(index):
        return {"grp": grp, "seq": index, "sub": sub}

    def in_column(index):
        return {"grp": grp, "seq": seq, "sub": index}

    def in_group(index):
        return {"grp": index, "seq": seq, "sub": sub}

    def seat(d, which):
        return 2 * ((chip + d) % chips) + which

    def rows_of(index, size):
        return pl.ds(pl.multiple_of(index * size, size), size)

    def nearest(k):
        found = 0
        for s in range(n_sub):
            others = sorted((abs(s - t), -abs(2 * t - n_sub + 1), t) for t in range(n_sub) if t != s)
            found = found + jnp.where(sub == s, others[k][2], 0)
        return found

    near = [nearest(k) for k in range(n_sub - 1)]
    unsent, unread, pending = [], [], {}

    def remote(src, dst, send_sem, recv_sem, device):
        return pltpu.make_async_remote_copy(
            src_ref=src, dst_ref=dst, send_sem=send_sem, recv_sem=recv_sem,
            device_id=device, device_id_type=MESH,
        )

    def send(src, dst, send_sem, recv_sem, device):
        copy = remote(src, dst, send_sem, recv_sem, device)
        copy.start()
        unsent.append((copy, None))
        unread.append(copy)
        return copy

    def send_some(condition, src, dst, send_sem, recv_sem, device):
        copy = remote(src, dst, send_sem, recv_sem, device)
        if condition is None:
            copy.start()
        else:
            pl.when(condition)(copy.start)
        unsent.append((copy, condition))

    def arrive(copy):
        copy.wait_recv()
        unread[:] = [other for other in unread if other is not copy]

    def drain():
        for key in list(pending):
            settle(*key)
        for copy in unread:
            copy.wait_recv()
        for copy, condition in unsent:
            if condition is None:
                copy.wait_send()
            else:
                pl.when(condition)(copy.wait_send)

    barrier = pltpu.get_barrier_semaphore()
    for d in range(1, n_seq):
        pl.semaphore_signal(barrier, inc=1, device_id=in_row((seq + d) % n_seq), device_id_type=MESH)
    for d in range(1, n_sub):
        pl.semaphore_signal(barrier, inc=1, device_id=in_column((sub + d) % n_sub), device_id_type=MESH)
    for d in range(1, n_grp):
        pl.semaphore_signal(barrier, inc=1, device_id=in_group((grp + d) % n_grp), device_id_type=MESH)

    weights = (wk_ref, wv_ref, wq_ref)
    mine = rows_of(seq, block)
    columns = rows_of(seq, span)

    def local(src, dst, index):
        copy = pltpu.make_async_copy(src, dst, local_sem.at[index])
        copy.start()
        return copy

    later = [
        local(w.at[:, columns], wall.at[rows_of(sub, rows), pl.ds(i * span, span)], 2 + i)
        for i, w in enumerate(weights)
    ]
    first = [local(ev_ref, ev, 0), local(off_ref, off, 1)]
    later.append(local(omega_ref.at[rows_of(seq, pair)], om, 5))
    later.append(local(cot_ref.at[:, columns], call.at[mine], 6))
    later[0].wait()
    pl.semaphore_wait(barrier, n_seq + n_sub + n_grp - 3)

    def slot(source, i):
        return wall.at[
            pl.ds(pl.multiple_of(source * rows + grp * share, share), share), pl.ds(i * span, span)
        ]

    inner = (sub > 0) & (sub < n_sub - 1)
    outer = jnp.logical_not(inner)

    def slice_copy(i, k):
        return remote(
            slot(sub, i), slot(sub, i),
            ws.at[i, k], wr.at[i, sub], in_column(near[k]),
        )

    @pl.when(inner)
    def _():
        slice_copy(0, edge).start()
        slice_copy(0, middle).start()
        slice_copy(0, far).start()

    @pl.when(outer)
    def _():
        slice_copy(0, middle).start()
        slice_copy(0, far).start()
        slice_copy(0, edge).start()

    for copy in later[1:3]:
        copy.wait()

    @pl.when(inner)
    def _():
        slice_copy(1, edge).start()
        slice_copy(2, edge).start()
        slice_copy(1, far).start()
        slice_copy(1, middle).start()
        slice_copy(2, far).start()
        slice_copy(2, middle).start()

    @pl.when(outer)
    def _():
        slice_copy(1, edge).start()
        slice_copy(1, middle).start()

    for i in range(3):
        unsent.append((slice_copy(i, far), inner if i else None))
        unsent.append((slice_copy(i, middle), None))
        unsent.append((slice_copy(i, edge), None))

    for copy in first:
        copy.wait()
    low, high = encoded(ev[...], off[...])
    xall[mine, : width // 2] = low
    xall[mine, width // 2 :] = high
    xcopies = {}
    for d in range(1, chips):
        xcopies[d] = send(xall.at[mine], xall.at[mine], xs.at[d], xr.at[d], in_row(seat(d, core)))
    xcopies[0] = send(xall.at[mine], xall.at[mine], xs.at[0], xr.at[0], in_row(mate))
    ccopies = []
    for d in range(1, n_seq):
        to = (seq + d) % n_seq
        ccopies.append(send(
            cot_ref.at[:, rows_of(to, span)], call.at[mine], cs.at[d - 1], cr.at[d - 1], in_row(to)
        ))
    xforward = []

    def forward_inputs():
        for d in range(1, chips):
            arrive(xcopies[d])
            at = rows_of((seq - 2 * d + n_seq) % n_seq, block)
            xforward.append(send(xall.at[at], xall.at[at], xs.at[chips + d - 1], xr.at[chips + d - 1], in_row(mate)))

    def relay_copy(i):
        at = slot(near[far], i)
        return remote(at, at, hs.at[i], wr.at[i, near[far]], in_column(near[edge]))

    def group_copies(i, k):
        at = slot(near[k], i)
        return [
            remote(at, at, ys.at[i, k, e - 1], yr.at[i, k, e - 1], in_group((grp + e) % n_grp))
            for e in range(1, n_grp)
        ]

    for i in range(3):
        if i:
            unsent.append((relay_copy(i), inner))
        for k in range(n_sub - 1):
            unsent.extend((copy, None) for copy in group_copies(i, k))

    def landed(i, k):
        at = slot(near[k], i)
        remote(at, at, ws.at[i, k], wr.at[i, near[k]], in_column(near[k])).wait_recv()

    def share_out(i, k):
        for copy in group_copies(i, k):
            copy.start()

    def pass_on(i, k):
        landed(i, k)
        share_out(i, k)

    def steps(inside, outside):
        pl.when(inner)(inside)
        pl.when(outer)(outside)

    def group_done(i):
        for k in range(n_sub - 1):
            for copy in group_copies(i, k):
                copy.wait_recv()

    def relay_on(i):
        landed(i, far)
        relay_copy(i).start()

    def first_inner():
        pass_on(0, far)
        pass_on(0, edge)
        pass_on(0, middle)
        pass_on(1, edge)
        relay_on(1)
        share_out(1, far)

    def first_outer():
        pass_on(0, edge)
        pass_on(0, far)
        pass_on(1, edge)
        pass_on(0, middle)
        slice_copy(2, edge).start()
        slice_copy(2, middle).start()
        pass_on(2, edge)

    def second_outer():
        pass_on(1, middle)

    def third_inner():
        relay_on(2)
        pass_on(1, middle)
        pass_on(2, edge)
        share_out(2, far)

    def third_outer():
        pass_on(1, far)

    def fourth_inner():
        pass_on(2, middle)

    def fourth_outer():
        pass_on(2, middle)
        pass_on(2, far)

    def project(i, target):
        target[...] = mul(xall[...], wall[:, i * span : (i + 1) * span], NN).astype(BF16)

    def featurize(feature, sigmoid, some):
        def step(b, carry):
            at = rows_of(b, block)
            for h in some:
                pre = mul(act[at, h * head : (h + 1) * head], om[h], NN)
                feature[h, at, :], sigmoid[h, at, :] = activations(pre)
            return carry

        lax.fori_loop(0, n_seq, step, 0, unroll=True)

    def start_total(a):
        copies = []
        for d in range(1, n_sub):
            copies.append(send(
                tot.at[a], totin.at[a, d - 1], ts.at[a, d - 1], tr.at[a, d - 1], in_column((sub + d) % n_sub)
            ))
        return copies

    def finish_total(a, copies):
        total = tot[a]
        for d in range(1, n_sub):
            arrive(copies[d - 1])
            total = total + totin[a, d - 1]
        return total

    def start_sum(a):
        part[a] = acc[a].astype(BF16)
        for k in reversed(range(n_sub - 1)):
            send_some(
                None, part.at[a, :, rows_of(near[k], piece)], rsin.at[a, sub],
                ss.at[a, 0, k], sr.at[a, 0, sub], in_column(near[k]),
            )
        pending[a, 0] = [rsin.at[a, source] for source in near]

    def middle_sum(a):
        own = rows_of(sub, piece)
        settle(a, 0)
        summed = acc[a, :, own, :]
        for source in near:
            summed = summed + rsin[a, source].astype(F32)
        half[a, :, own, :] = summed.astype(BF16)
        for k in reversed(range(n_sub - 1)):
            send_some(
                None, half.at[a, :, own], half.at[a, :, own],
                ss.at[a, 1, k], sr.at[a, 1, sub], in_column(near[k]),
            )
        pending[a, 1] = [half.at[a, :, rows_of(source, piece)] for source in near]

    def settle(a, stage):
        for k, dst in enumerate(pending.pop((a, stage))):
            remote(dst, dst, ss.at[a, stage, k], sr.at[a, stage, near[k]], in_column(near[k])).wait_recv()

    def summed_half(a, h):
        return half[a, h]

    def body():
        steps(first_inner, first_outer)
        forward_inputs()
        for copy in later[3:]:
            copy.wait()
        pl.when(outer)(second_outer)
        group_done(0)
        for copy in xforward:
            arrive(copy)
        arrive(xcopies[0])
        pl.when(inner)(third_inner)
        project(0, act)
        pl.when(outer)(third_outer)
        featurize(kf, ks, range(pair))
        steps(fourth_inner, fourth_outer)
        tot[...] = jnp.zeros_like(tot)
        for h in range(pair):
            tot[0, pl.ds(h, 1), :] = jnp.sum(kf[h].astype(F32), axis=0, keepdims=True)
        totals = start_total(0)
        group_done(1)
        if stop == 2:
            return
        project(1, va)
        for h in range(pair):
            acc[0, h] = mul(va[:, h * head : (h + 1) * head], kf[h], TN)
        start_sum(0)
        group_done(2)
        if stop == 3:
            return
        project(2, act)
        total_half = finish_total(0, totals).astype(BF16)
        for copy in ccopies:
            arrive(copy)
        for h in range(pair):
            featurize(qf, qs, [h])
            wide = jnp.broadcast_to(total_half[h : h + 1], (head, features))
            lanes = pl.ds(h * head, head)

            def scale(b, carry, h=h, wide=wide, lanes=lanes):
                at = rows_of(b, block)
                inverse = 1.0 / mul(qf[h, at, :], wide, NT)
                inv[h, at, :] = inverse
                sc[at, lanes] = (call[at, lanes].astype(F32) * loss_scale * inverse).astype(BF16)
                return carry

            lax.fori_loop(0, n_seq, scale, 0, unroll=True)
            acc[1, h] = mul(sc[:, lanes], qf[h], TN)
        start_sum(1)
        middle_sum(0)
        middle_sum(1)
        if stop == 5:
            return
        settle(0, 1)
        for h in range(pair):
            lanes = pl.ds(h * head, head)
            summary = half[0, h]

            def norms(b, carry, h=h, lanes=lanes, summary=summary):
                at = rows_of(b, block)
                inverse = inv[h, at, :]
                attended = mul(qf[h, at, :], summary, NT) * inverse
                scaled = call[at, lanes].astype(F32) * loss_scale * inverse
                nrm[h, at, :] = -jnp.sum(scaled * attended, axis=-1, keepdims=True)
                return carry

            lax.fori_loop(0, n_seq, norms, 0, unroll=True)
            tot[1, pl.ds(h, 1), :] = jnp.sum(
                qf[h].astype(F32) * nrm[h].astype(BF16).astype(F32), axis=0, keepdims=True
            )
        grads = start_total(1)
        if stop == 6:
            return
        for h in range(pair):
            lanes = pl.ds(h * head, head)
            summary = half[0, h]
            weight = total_half[h : h + 1].astype(F32)

            def query_grads(b, carry, h=h, lanes=lanes, summary=summary, weight=weight):
                at = rows_of(b, block)
                grad = mul(sc[at, lanes], summary, NN) + nrm[h, at, :] * weight
                grad = (grad * qs[h, at, :]).astype(BF16)
                gr[at, pl.ds(2 * span + h * head, head)] = mul(grad, om[h], NT).astype(BF16)
                return carry

            lax.fori_loop(0, n_seq, query_grads, 0, unroll=True)
        def chip_rows(d):
            return pl.ds(pl.multiple_of((chip + d) % chips * 2 * block, 2 * block), 2 * block)

        for d in range(1, chips):
            for c in range(cuts):
                keep[d, c] = mul(
                    gr[chip_rows(d), 2 * span :], wall[c * slab : (c + 1) * slab, 2 * span :], NT
                )
        def value_grads(d, h):
            at = chip_rows(d)
            gr[at, pl.ds(span + h * head, head)] = mul(kf[h, at, :], summed_half(1, h), NT).astype(BF16)

        def key_grads(d, h):
            at = chip_rows(d)
            lanes = pl.ds(h * head, head)
            grad = mul(va[at, lanes], summed_half(1, h), NN) + total_grad[h : h + 1]
            grad = (grad * ks[h, at, :]).astype(BF16)
            gr[at, pl.ds(h * head, head)] = mul(grad, om[h], NT).astype(BF16)

        settle(1, 1)
        for h in range(pair):
            for d in range(1, chips):
                value_grads(d, h)
        for d in range(1, chips):
            for c in range(cuts):
                keep[d, c] = keep[d, c] + mul(
                    gr[chip_rows(d), span : 2 * span], wall[c * slab : (c + 1) * slab, span : 2 * span], NT
                )
        total_grad = finish_total(1, grads)
        for h in range(pair):
            for d in range(1, chips):
                key_grads(d, h)
        if stop in (7, 8):
            return

        def to_mate(d):
            copies = []
            for c in range(cuts):
                at = pl.ds(c * slab, slab)
                columns_of = slice(0, span if d else 3 * span)
                grads = mul(gr[chip_rows(d), columns_of], wall[c * slab : (c + 1) * slab, columns_of], NT)
                keep[d, c] = keep[d, c] + grads if d else grads
                mo[d, :, at] = keep[d, c, rows_of(1 - core, block), :].astype(BF16)
                copies.append(send(
                    mo.at[d, :, at], mi.at[d, :, at], ms.at[d, c], mr.at[d, c], in_row(mate)
                ))
            return copies

        for_mate = {d: to_mate(d) for d in range(1, chips)}
        outward = {}
        for d in range(1, chips):
            for c in range(cuts):
                at = pl.ds(c * slab, slab)
                arrive(for_mate[d][c])
                ro[d - 1, :, at] = (
                    keep[d, c, rows_of(core, block), :] + mi[d, :, at].astype(F32)
                ).astype(BF16)
                outward[d, c] = send(
                    ro.at[d - 1, :, at], ri.at[d - 1, :, at], os_.at[d - 1, c], or_.at[d - 1, c],
                    in_row(seat(d, core)),
                )
        for h in range(pair):
            value_grads(0, h)
            key_grads(0, h)
        for_mate[0] = to_mate(0)
        for c in range(cuts):
            at = pl.ds(c * slab, slab)
            arrive(for_mate[0][c])
            summed = keep[0, c, rows_of(core, block), :] + mi[0, :, at].astype(F32)
            for d in range(1, chips):
                arrive(outward[d, c])
                summed = summed + ri[d - 1, :, at].astype(F32)
            out_ref[:, at] = summed.astype(BF16)

    body()
    drain()


def fits(n_grp, n_seq, n_sub, events, offsets, cotangent, query_weight, key_weight, value_weight, omega):
    heads, head, features = omega.shape
    block, width = events.shape
    pair = heads // n_seq
    rows = query_weight.shape[0]
    return (
        n_seq >= 4 and n_seq % 2 == 0 and n_grp > 1 and n_sub == 4 and heads % n_seq == 0 and pair <= 8
        and head % 128 == 0 and features % 128 == 0 and block % 128 == 0 and width % 512 == 0
        and head % (16 * n_sub) == 0 and rows % (16 * n_grp) == 0
        and n_seq * block <= 1024 and pair * features <= 512 and width <= 1024
    )


STOP = 99


def fused(n_grp, n_seq, n_sub, events, offsets, cotangent, query_weight, key_weight, value_weight, omega):
    block, width = events.shape
    heads, head, features = omega.shape
    tokens = n_seq * block
    pair = heads // n_seq
    span = pair * head
    piece = head // n_sub
    chips = n_seq // 2
    cuts = 4
    vm = pltpu.VMEM
    dma = pltpu.SemaphoreType.DMA
    scratch = [
        vm((block, width), BF16),
        vm((1, block), jnp.int32),
        vm((tokens, width), BF16),
        vm((tokens, span), BF16),
        vm((width, 3 * span), BF16),
        vm((pair, head, features), BF16),
        vm((tokens, span), BF16),
        vm((tokens, span), BF16),
        vm((pair, tokens, features), BF16),
        vm((pair, tokens, features), BF16),
        vm((pair, tokens, features), F32),
        vm((pair, tokens, features), F32),
        vm((tokens, span), BF16),
        vm((pair, tokens, head), F32),
        vm((pair, tokens, 1), F32),
        vm((tokens, 3 * span), BF16),
        vm((2, pair, head, features), F32),
        vm((2, pair, head, features), BF16),
        vm((2, n_sub, pair, piece, features), BF16),
        vm((2, pair, head, features), BF16),
        vm((2, 8, features), F32),
        vm((2, n_sub - 1, 8, features), F32),
        vm((chips, cuts, 2 * block, width // cuts), F32),
        vm((chips, block, width), BF16),
        vm((chips, block, width), BF16),
        vm((chips - 1, block, width), BF16),
        vm((chips - 1, block, width), BF16),
        dma((7,)),
        dma((2 * chips - 1,)), dma((2 * chips - 1,)),
        dma((n_seq - 1,)), dma((n_seq - 1,)),
        dma((3, n_sub - 1)), dma((3, n_sub)), dma((3,)),
        dma((3, n_sub - 1, n_grp - 1)), dma((3, n_sub - 1, n_grp - 1)),
        dma((2, 2, n_sub - 1)), dma((2, 2, n_sub)),
        dma((2, n_sub - 1)), dma((2, n_sub - 1)),
        dma((chips, cuts)), dma((chips, cuts)),
        dma((chips - 1, cuts)), dma((chips - 1, cuts)),
    ]
    loss_scale = math.sqrt(block * n_seq * n_sub)
    return pl.pallas_call(
        functools.partial(kernel, n_grp, n_seq, n_sub, loss_scale, cuts, STOP),
        out_shape=jax.ShapeDtypeStruct((block, width), BF16),
        in_specs=[pl.BlockSpec(memory_space=pl.ANY)] * 7,
        out_specs=pl.BlockSpec(memory_space=pltpu.VMEM),
        scratch_shapes=scratch,
        compiler_params=pltpu.CompilerParams(
            collective_id=0, has_side_effects=True, vmem_limit_bytes=48 * 1024 * 1024
        ),
    )(*[
        pltpu.with_memory_space_constraint(array, pltpu.HBM)
        for array in (
            events, offsets.reshape(1, block), cotangent, query_weight, key_weight, value_weight, omega
        )
    ])


def solution(mesh):
    in_specs = (
        P(("grp", "seq", "sub"), None),
        P(("grp", "seq", "sub")),
        P(("grp", "seq", "sub"), None),
        P("sub", None),
        P("sub", None),
        P("sub", None),
        P(),
    )
    out_specs = P(("grp", "seq", "sub"), None)
    n_grp, n_seq, n_sub = (mesh.shape[name] for name in ("grp", "seq", "sub"))

    def body(*args):
        if fits(n_grp, n_seq, n_sub, *args):
            return fused(n_grp, n_seq, n_sub, *args)
        return local(*args)

    return jax.shard_map(body, mesh=mesh, in_specs=in_specs, out_specs=out_specs, check_vma=False)
```

```python
import functools
import math

import jax
import jax.numpy as jnp
from jax import lax
from jax.experimental import pallas as pl
from jax.experimental.pallas import tpu as pltpu
from jax.sharding import PartitionSpec as P


def encode(events, offsets):
    half_width = events.shape[1] // 2
    indices = jnp.arange(half_width, dtype=jnp.float32)
    frequency = jnp.exp(indices * (-2.0 * math.log(10000.0) / events.shape[1]))
    angles = offsets.astype(jnp.float32)[:, None] * frequency[None, :]
    encoding = jnp.concatenate([jnp.sin(angles), jnp.cos(angles)], axis=1)
    return (events.astype(jnp.float32) + encoding).astype(jnp.bfloat16)


def split_heads(matrix, head_count):
    return matrix.reshape(matrix.shape[0], head_count, matrix.shape[1] // head_count)


def transposed(left, weight):
    return lax.dot_general(
        left, weight, (((1,), (1,)), ((), ())), preferred_element_type=jnp.float32
    )


def local(events, offsets, cotangent, query_weight, key_weight, value_weight, omega):
    widened_rows = jnp.float32
    head_count = omega.shape[0]
    local_rows = events.shape[0]
    model_width = events.shape[1]
    all_tokens = local_rows * lax.axis_size("seq") * lax.axis_size("sub")
    loss_scale = math.sqrt(all_tokens)
    inputs = encode(events, offsets)
    gathered = (
        lax.all_gather(query_weight, "sub", axis=0, tiled=True),
        lax.all_gather(key_weight, "sub", axis=0, tiled=True),
        lax.all_gather(value_weight, "sub", axis=0, tiled=True),
    )
    queries, key_act, value_act = [
        jnp.dot(inputs, weight, preferred_element_type=widened_rows).astype(jnp.bfloat16)
        for weight in gathered
    ]
    query_pre = jnp.einsum(
        "thd,hdm->thm", split_heads(queries, head_count), omega, preferred_element_type=widened_rows
    )
    key_pre = jnp.einsum(
        "thd,hdm->thm", split_heads(key_act, head_count), omega, preferred_element_type=widened_rows
    )
    query_feature_map = jax.nn.softplus(query_pre).astype(jnp.bfloat16)
    key_feature_map = jax.nn.softplus(key_pre).astype(jnp.bfloat16)
    value_per_head = split_heads(value_act, head_count)
    local_digest = jnp.einsum(
        "reb,rec->ebc", key_feature_map, value_per_head, preferred_element_type=widened_rows
    )
    local_total = jnp.sum(key_feature_map, axis=0, dtype=widened_rows)
    state_digest, key_total = lax.psum((local_digest, local_total), ("seq", "sub"))
    digest_halves = state_digest.astype(jnp.bfloat16)
    total_half = key_total.astype(jnp.bfloat16)
    numerator = jnp.einsum(
        "xls,lsk->xlk", query_feature_map, digest_halves, preferred_element_type=widened_rows
    )
    denom = jnp.einsum(
        "thm,hm->th", query_feature_map, total_half, preferred_element_type=widened_rows
    )
    attended = numerator / denom[..., None]
    upstream = split_heads(cotangent, head_count).astype(widened_rows) * loss_scale
    scaled_grad = upstream / denom[..., None]
    norm_grad = -jnp.sum(scaled_grad * attended, axis=-1)
    scaled_halves = scaled_grad.astype(jnp.bfloat16)
    norm_half = norm_grad.astype(jnp.bfloat16)
    local_gradient = jnp.einsum(
        "reb,rec->ebc", query_feature_map, scaled_halves, preferred_element_type=widened_rows
    )
    local_norm = jnp.einsum(
        "thm,th->hm", query_feature_map, norm_half, preferred_element_type=widened_rows
    )
    summary_grad, overall_gradient = lax.psum((local_gradient, local_norm), ("seq", "sub"))
    gradient_halves = summary_grad.astype(jnp.bfloat16)
    query_feature_gradient = jnp.einsum(
        "pfy,fly->pfl", scaled_halves, digest_halves, preferred_element_type=widened_rows
    )
    query_feature_gradient = (
        query_feature_gradient + norm_grad[..., None] * total_half.astype(widened_rows)[None]
    )
    key_feature_gradient = (
        jnp.einsum(
            "pfy,fly->pfl", value_per_head, gradient_halves, preferred_element_type=widened_rows
        )
        + overall_gradient[None]
    )
    value_gradient = jnp.einsum(
        "xls,lsk->xlk", key_feature_map, gradient_halves, preferred_element_type=widened_rows
    ).astype(jnp.bfloat16)
    query_pre_grad = (query_feature_gradient * jax.nn.sigmoid(query_pre)).astype(jnp.bfloat16)
    key_pre_grad = (key_feature_gradient * jax.nn.sigmoid(key_pre)).astype(jnp.bfloat16)
    query_grad = jnp.einsum(
        "thm,hdm->thd", query_pre_grad, omega, preferred_element_type=widened_rows
    ).astype(jnp.bfloat16)
    key_grad = jnp.einsum(
        "thm,hdm->thd", key_pre_grad, omega, preferred_element_type=widened_rows
    ).astype(jnp.bfloat16)
    query_flat = query_grad.reshape(local_rows, model_width)
    key_flat = key_grad.reshape(local_rows, model_width)
    value_flat = value_gradient.reshape(local_rows, model_width)
    summed = transposed(query_flat, gathered[0])
    summed = summed + transposed(key_flat, gathered[1])
    summed = summed + transposed(value_flat, gathered[2])
    return summed.astype(jnp.bfloat16)


F32, BF16 = jnp.float32, jnp.bfloat16
MESH = pl.DeviceIdType.MESH
NN = (((1,), (0,)), ((), ()))
NT = (((1,), (1,)), ((), ()))
TN = (((0,), (0,)), ((), ()))


def mul(left, right, dims):
    return lax.dot_general(left, right, dims, preferred_element_type=F32)


def activations(pre):
    small = jnp.exp(-jnp.abs(pre))
    feature = jnp.maximum(pre, 0.0) + jnp.log1p(small)
    sigmoid = jnp.where(pre >= 0.0, 1.0, small) / (1.0 + small)
    return feature.astype(BF16), sigmoid


def encoded(events, offsets):
    block, width = events.shape
    row = lax.broadcasted_iota(jnp.int32, (block, block), 0)
    lane = lax.broadcasted_iota(jnp.int32, (block, block), 1)
    spread = jnp.broadcast_to(offsets.astype(F32), (block, block))
    column = jnp.sum(jnp.where(row == lane, spread, 0.0), axis=1, keepdims=True)
    indices = lax.broadcasted_iota(jnp.int32, (1, width // 2), 1).astype(F32)
    frequency = jnp.exp(indices * (-2.0 * math.log(10000.0) / width))
    angles = column * frequency
    turns = jnp.floor(angles * (2.0 / math.pi) + 0.5)
    rest = angles - turns * 1.5703125
    rest = rest - turns * 4.837512969970703125e-4
    rest = rest - turns * 7.54978994e-8
    square = rest * rest
    sine = ((-1.9515295891e-4 * square + 8.3321608736e-3) * square - 1.6666654611e-1) * square * rest + rest
    cosine = ((2.443315711809948e-5 * square - 1.388731625493765e-3) * square + 4.166664568298827e-2)
    cosine = cosine * square * square - 0.5 * square + 1.0
    halves = jnp.floor(turns * 0.5)
    odd = turns - 2.0 * halves
    sign = 1.0 - 2.0 * (halves - 2.0 * jnp.floor(halves * 0.5))
    swap = odd > 0.5
    sines = jnp.where(swap, cosine, sine) * sign
    cosines = jnp.where(swap, -sine, cosine) * sign
    wide = events.astype(F32)
    return (
        (wide[:, : width // 2] + sines).astype(BF16),
        (wide[:, width // 2 :] + cosines).astype(BF16),
    )


def kernel(
    n_grp, n_seq, n_sub, loss_scale, cuts, stop,
    ev_ref, off_ref, cot_ref, wq_ref, wk_ref, wv_ref, omega_ref, out_ref,
    ev, off, xall, call, wall, om, act, va, qf, kf, qs, ks, sc, inv, nrm, gr,
    acc, part, rsin, half, tot, totin, keep, mo, mi, ro, ri,
    local_sem, xs, xr, cs, cr, ws, wr, hs, ys, yr, ss, sr, ts, tr, ms, mr, os_, or_,
):
    grp, seq, sub = lax.axis_index("grp"), lax.axis_index("seq"), lax.axis_index("sub")
    chips = n_seq // 2
    chip, core = seq // 2, seq % 2
    mate = 2 * chip + 1 - core
    block, width = ev_ref.shape
    pair, head, features = om.shape
    span = pair * head
    rows = wq_ref.shape[0]
    share = rows // n_grp
    piece = head // n_sub
    slab = width // cuts
    edge, middle, far = range(n_sub - 1)

    def in_row(index):
        return {"grp": grp, "seq": index, "sub": sub}

    def in_column(index):
        return {"grp": grp, "seq": seq, "sub": index}

    def in_group(index):
        return {"grp": index, "seq": seq, "sub": sub}

    def seat(d, which):
        return 2 * ((chip + d) % chips) + which

    def rows_of(index, size):
        return pl.ds(pl.multiple_of(index * size, size), size)

    def nearest(k):
        found = 0
        for s in range(n_sub):
            others = sorted((abs(s - t), -abs(2 * t - n_sub + 1), t) for t in range(n_sub) if t != s)
            found = found + jnp.where(sub == s, others[k][2], 0)
        return found

    near = [nearest(k) for k in range(n_sub - 1)]
    unsent, unread, pending = [], [], {}

    def remote(src, dst, send_sem, recv_sem, device):
        return pltpu.make_async_remote_copy(
            src_ref=src, dst_ref=dst, send_sem=send_sem, recv_sem=recv_sem,
            device_id=device, device_id_type=MESH,
        )

    def send(src, dst, send_sem, recv_sem, device):
        copy = remote(src, dst, send_sem, recv_sem, device)
        copy.start()
        unsent.append((copy, None))
        unread.append(copy)
        return copy

    def send_some(condition, src, dst, send_sem, recv_sem, device):
        copy = remote(src, dst, send_sem, recv_sem, device)
        if condition is None:
            copy.start()
        else:
            pl.when(condition)(copy.start)
        unsent.append((copy, condition))

    def arrive(copy):
        copy.wait_recv()
        unread[:] = [other for other in unread if other is not copy]

    def drain():
        for key in list(pending):
            settle(*key)
        for copy in unread:
            copy.wait_recv()
        for copy, condition in unsent:
            if condition is None:
                copy.wait_send()
            else:
                pl.when(condition)(copy.wait_send)

    barrier = pltpu.get_barrier_semaphore()
    for d in range(1, n_seq):
        pl.semaphore_signal(barrier, inc=1, device_id=in_row((seq + d) % n_seq), device_id_type=MESH)
    for d in range(1, n_sub):
        pl.semaphore_signal(barrier, inc=1, device_id=in_column((sub + d) % n_sub), device_id_type=MESH)
    for d in range(1, n_grp):
        pl.semaphore_signal(barrier, inc=1, device_id=in_group((grp + d) % n_grp), device_id_type=MESH)

    weights = (wk_ref, wv_ref, wq_ref)
    mine = rows_of(seq, block)
    columns = rows_of(seq, span)

    def local(src, dst, index):
        copy = pltpu.make_async_copy(src, dst, local_sem.at[index])
        copy.start()
        return copy

    later = [
        local(w.at[:, columns], wall.at[rows_of(sub, rows), pl.ds(i * span, span)], 2 + i)
        for i, w in enumerate(weights)
    ]
    first = [local(ev_ref, ev, 0), local(off_ref, off, 1)]
    later.append(local(omega_ref.at[rows_of(seq, pair)], om, 5))
    later.append(local(cot_ref.at[:, columns], call.at[mine], 6))
    later[0].wait()
    pl.semaphore_wait(barrier, n_seq + n_sub + n_grp - 3)

    def slot(source, i):
        return wall.at[
            pl.ds(pl.multiple_of(source * rows + grp * share, share), share), pl.ds(i * span, span)
        ]

    inner = (sub > 0) & (sub < n_sub - 1)
    outer = jnp.logical_not(inner)

    def slice_copy(i, k):
        return remote(
            slot(sub, i), slot(sub, i),
            ws.at[i, k], wr.at[i, sub], in_column(near[k]),
        )

    @pl.when(inner)
    def _():
        slice_copy(0, edge).start()
        slice_copy(0, middle).start()
        slice_copy(0, far).start()

    @pl.when(outer)
    def _():
        slice_copy(0, middle).start()
        slice_copy(0, far).start()
        slice_copy(0, edge).start()

    for copy in later[1:3]:
        copy.wait()

    @pl.when(inner)
    def _():
        slice_copy(1, edge).start()
        slice_copy(2, edge).start()
        slice_copy(1, far).start()
        slice_copy(1, middle).start()
        slice_copy(2, far).start()
        slice_copy(2, middle).start()

    @pl.when(outer)
    def _():
        slice_copy(1, edge).start()
        slice_copy(1, middle).start()

    for i in range(3):
        unsent.append((slice_copy(i, far), inner if i else None))
        unsent.append((slice_copy(i, middle), None))
        unsent.append((slice_copy(i, edge), None))

    for copy in first:
        copy.wait()
    low, high = encoded(ev[...], off[...])
    xall[mine, : width // 2] = low
    xall[mine, width // 2 :] = high
    xcopies = {}
    for d in range(1, chips):
        xcopies[d] = send(xall.at[mine], xall.at[mine], xs.at[d], xr.at[d], in_row(seat(d, core)))
    xcopies[0] = send(xall.at[mine], xall.at[mine], xs.at[0], xr.at[0], in_row(mate))
    ccopies = []
    for d in range(1, n_seq):
        to = (seq + d) % n_seq
        ccopies.append(send(
            cot_ref.at[:, rows_of(to, span)], call.at[mine], cs.at[d - 1], cr.at[d - 1], in_row(to)
        ))
    xforward = []

    def forward_inputs():
        for d in range(1, chips):
            arrive(xcopies[d])
            at = rows_of((seq - 2 * d + n_seq) % n_seq, block)
            xforward.append(send(xall.at[at], xall.at[at], xs.at[chips + d - 1], xr.at[chips + d - 1], in_row(mate)))

    def relay_copy(i):
        at = slot(near[far], i)
        return remote(at, at, hs.at[i], wr.at[i, near[far]], in_column(near[edge]))

    def group_copies(i, k):
        at = slot(near[k], i)
        return [
            remote(at, at, ys.at[i, k, e - 1], yr.at[i, k, e - 1], in_group((grp + e) % n_grp))
            for e in range(1, n_grp)
        ]

    for i in range(3):
        if i:
            unsent.append((relay_copy(i), inner))
        for k in range(n_sub - 1):
            unsent.extend((copy, None) for copy in group_copies(i, k))

    def landed(i, k):
        at = slot(near[k], i)
        remote(at, at, ws.at[i, k], wr.at[i, near[k]], in_column(near[k])).wait_recv()

    def share_out(i, k):
        for copy in group_copies(i, k):
            copy.start()

    def pass_on(i, k):
        landed(i, k)
        share_out(i, k)

    def steps(inside, outside):
        pl.when(inner)(inside)
        pl.when(outer)(outside)

    def group_done(i):
        for k in range(n_sub - 1):
            for copy in group_copies(i, k):
                copy.wait_recv()

    def relay_on(i):
        landed(i, far)
        relay_copy(i).start()

    def first_inner():
        pass_on(0, far)
        pass_on(0, edge)
        pass_on(0, middle)
        pass_on(1, edge)
        relay_on(1)
        share_out(1, far)

    def first_outer():
        pass_on(0, edge)
        pass_on(0, far)
        pass_on(1, edge)
        pass_on(0, middle)
        slice_copy(2, edge).start()
        slice_copy(2, middle).start()
        pass_on(2, edge)

    def second_outer():
        pass_on(1, middle)

    def third_inner():
        relay_on(2)
        pass_on(1, middle)
        pass_on(2, edge)
        share_out(2, far)

    def third_outer():
        pass_on(1, far)

    def fourth_inner():
        pass_on(2, middle)

    def fourth_outer():
        pass_on(2, middle)
        pass_on(2, far)

    def project(i, target):
        target[...] = mul(xall[...], wall[:, i * span : (i + 1) * span], NN).astype(BF16)

    def featurize(feature, sigmoid, some):
        def step(b, carry):
            at = rows_of(b, block)
            for h in some:
                pre = mul(act[at, h * head : (h + 1) * head], om[h], NN)
                feature[h, at, :], sigmoid[h, at, :] = activations(pre)
            return carry

        lax.fori_loop(0, n_seq, step, 0, unroll=True)

    def start_total(a):
        copies = []
        for d in range(1, n_sub):
            copies.append(send(
                tot.at[a], totin.at[a, d - 1], ts.at[a, d - 1], tr.at[a, d - 1], in_column((sub + d) % n_sub)
            ))
        return copies

    def finish_total(a, copies):
        total = tot[a]
        for d in range(1, n_sub):
            arrive(copies[d - 1])
            total = total + totin[a, d - 1]
        return total

    def start_sum(a):
        part[a] = acc[a].astype(BF16)
        for k in reversed(range(n_sub - 1)):
            send_some(
                None, part.at[a, :, rows_of(near[k], piece)], rsin.at[a, sub],
                ss.at[a, 0, k], sr.at[a, 0, sub], in_column(near[k]),
            )
        pending[a, 0] = [rsin.at[a, source] for source in near]

    def middle_sum(a):
        own = rows_of(sub, piece)
        settle(a, 0)
        summed = acc[a, :, own, :]
        for source in near:
            summed = summed + rsin[a, source].astype(F32)
        half[a, :, own, :] = summed.astype(BF16)
        for k in reversed(range(n_sub - 1)):
            send_some(
                None, half.at[a, :, own], half.at[a, :, own],
                ss.at[a, 1, k], sr.at[a, 1, sub], in_column(near[k]),
            )
        pending[a, 1] = [half.at[a, :, rows_of(source, piece)] for source in near]

    def settle(a, stage):
        for k, dst in enumerate(pending.pop((a, stage))):
            remote(dst, dst, ss.at[a, stage, k], sr.at[a, stage, near[k]], in_column(near[k])).wait_recv()

    def summed_half(a, h):
        return half[a, h]

    def body():
        steps(first_inner, first_outer)
        forward_inputs()
        for copy in later[3:]:
            copy.wait()
        pl.when(outer)(second_outer)
        group_done(0)
        for copy in xforward:
            arrive(copy)
        arrive(xcopies[0])
        pl.when(inner)(third_inner)
        project(0, act)
        pl.when(outer)(third_outer)
        featurize(kf, ks, range(pair))
        steps(fourth_inner, fourth_outer)
        tot[...] = jnp.zeros_like(tot)
        for h in range(pair):
            tot[0, pl.ds(h, 1), :] = jnp.sum(kf[h].astype(F32), axis=0, keepdims=True)
        totals = start_total(0)
        group_done(1)
        if stop == 2:
            return
        project(1, va)
        for h in range(pair):
            acc[0, h] = mul(va[:, h * head : (h + 1) * head], kf[h], TN)
        start_sum(0)
        group_done(2)
        if stop == 3:
            return
        project(2, act)
        total_half = finish_total(0, totals).astype(BF16)
        for copy in ccopies:
            arrive(copy)
        for h in range(pair):
            featurize(qf, qs, [h])
            wide = jnp.broadcast_to(total_half[h : h + 1], (head, features))
            lanes = pl.ds(h * head, head)

            def scale(b, carry, h=h, wide=wide, lanes=lanes):
                at = rows_of(b, block)
                inverse = 1.0 / mul(qf[h, at, :], wide, NT)
                inv[h, at, :] = inverse
                sc[at, lanes] = (call[at, lanes].astype(F32) * loss_scale * inverse).astype(BF16)
                return carry

            lax.fori_loop(0, n_seq, scale, 0, unroll=True)
            acc[1, h] = mul(sc[:, lanes], qf[h], TN)
        start_sum(1)
        middle_sum(0)
        middle_sum(1)
        if stop == 5:
            return
        settle(0, 1)
        for h in range(pair):
            lanes = pl.ds(h * head, head)
            summary = half[0, h]

            def norms(b, carry, h=h, lanes=lanes, summary=summary):
                at = rows_of(b, block)
                inverse = inv[h, at, :]
                attended = mul(qf[h, at, :], summary, NT) * inverse
                scaled = call[at, lanes].astype(F32) * loss_scale * inverse
                nrm[h, at, :] = -jnp.sum(scaled * attended, axis=-1, keepdims=True)
                return carry

            lax.fori_loop(0, n_seq, norms, 0, unroll=True)
            tot[1, pl.ds(h, 1), :] = jnp.sum(
                qf[h].astype(F32) * nrm[h].astype(BF16).astype(F32), axis=0, keepdims=True
            )
        grads = start_total(1)
        if stop == 6:
            return
        for h in range(pair):
            lanes = pl.ds(h * head, head)
            summary = half[0, h]
            weight = total_half[h : h + 1].astype(F32)

            def query_grads(b, carry, h=h, lanes=lanes, summary=summary, weight=weight):
                at = rows_of(b, block)
                grad = mul(sc[at, lanes], summary, NN) + nrm[h, at, :] * weight
                grad = (grad * qs[h, at, :]).astype(BF16)
                gr[at, pl.ds(2 * span + h * head, head)] = mul(grad, om[h], NT).astype(BF16)
                return carry

            lax.fori_loop(0, n_seq, query_grads, 0, unroll=True)
        def chip_rows(d):
            return pl.ds(pl.multiple_of((chip + d) % chips * 2 * block, 2 * block), 2 * block)

        for d in range(1, chips):
            for c in range(cuts):
                keep[d, c] = mul(
                    gr[chip_rows(d), 2 * span :], wall[c * slab : (c + 1) * slab, 2 * span :], NT
                )
        def value_grads(d, h):
            at = chip_rows(d)
            gr[at, pl.ds(span + h * head, head)] = mul(kf[h, at, :], summed_half(1, h), NT).astype(BF16)

        def key_grads(d, h):
            at = chip_rows(d)
            lanes = pl.ds(h * head, head)
            grad = mul(va[at, lanes], summed_half(1, h), NN) + total_grad[h : h + 1]
            grad = (grad * ks[h, at, :]).astype(BF16)
            gr[at, pl.ds(h * head, head)] = mul(grad, om[h], NT).astype(BF16)

        settle(1, 1)
        for h in range(pair):
            for d in range(1, chips):
                value_grads(d, h)
        for d in range(1, chips):
            for c in range(cuts):
                keep[d, c] = keep[d, c] + mul(
                    gr[chip_rows(d), span : 2 * span], wall[c * slab : (c + 1) * slab, span : 2 * span], NT
                )
        total_grad = finish_total(1, grads)
        for h in range(pair):
            for d in range(1, chips):
                key_grads(d, h)
        if stop in (7, 8):
            return

        def to_mate(d):
            copies = []
            for c in range(cuts):
                at = pl.ds(c * slab, slab)
                columns_of = slice(0, span if d else 3 * span)
                grads = mul(gr[chip_rows(d), columns_of], wall[c * slab : (c + 1) * slab, columns_of], NT)
                keep[d, c] = keep[d, c] + grads if d else grads
                mo[d, :, at] = keep[d, c, rows_of(1 - core, block), :].astype(BF16)
                copies.append(send(
                    mo.at[d, :, at], mi.at[d, :, at], ms.at[d, c], mr.at[d, c], in_row(mate)
                ))
            return copies

        for_mate = {d: to_mate(d) for d in range(1, chips)}
        outward = {}
        for d in range(1, chips):
            for c in range(cuts):
                at = pl.ds(c * slab, slab)
                arrive(for_mate[d][c])
                ro[d - 1, :, at] = (
                    keep[d, c, rows_of(core, block), :] + mi[d, :, at].astype(F32)
                ).astype(BF16)
                outward[d, c] = send(
                    ro.at[d - 1, :, at], ri.at[d - 1, :, at], os_.at[d - 1, c], or_.at[d - 1, c],
                    in_row(seat(d, core)),
                )
        for h in range(pair):
            value_grads(0, h)
            key_grads(0, h)
        for_mate[0] = to_mate(0)
        for c in range(cuts):
            at = pl.ds(c * slab, slab)
            arrive(for_mate[0][c])
            summed = keep[0, c, rows_of(core, block), :] + mi[0, :, at].astype(F32)
            for d in range(1, chips):
                arrive(outward[d, c])
                summed = summed + ri[d - 1, :, at].astype(F32)
            out_ref[:, at] = summed.astype(BF16)

    body()
    drain()


def fits(n_grp, n_seq, n_sub, events, offsets, cotangent, query_weight, key_weight, value_weight, omega):
    heads, head, features = omega.shape
    block, width = events.shape
    pair = heads // n_seq
    rows = query_weight.shape[0]
    return (
        n_seq >= 4 and n_seq % 2 == 0 and n_grp > 1 and n_sub == 4 and heads % n_seq == 0 and pair <= 8
        and head % 128 == 0 and features % 128 == 0 and block % 128 == 0 and width % 512 == 0
        and head % (16 * n_sub) == 0 and rows % (16 * n_grp) == 0
        and n_seq * block <= 1024 and pair * features <= 512 and width <= 1024
    )


STOP = 99


def fused(n_grp, n_seq, n_sub, events, offsets, cotangent, query_weight, key_weight, value_weight, omega):
    block, width = events.shape
    heads, head, features = omega.shape
    tokens = n_seq * block
    pair = heads // n_seq
    span = pair * head
    piece = head // n_sub
    chips = n_seq // 2
    cuts = 2
    vm = pltpu.VMEM
    dma = pltpu.SemaphoreType.DMA
    scratch = [
        vm((block, width), BF16),
        vm((1, block), jnp.int32),
        vm((tokens, width), BF16),
        vm((tokens, span), BF16),
        vm((width, 3 * span), BF16),
        vm((pair, head, features), BF16),
        vm((tokens, span), BF16),
        vm((tokens, span), BF16),
        vm((pair, tokens, features), BF16),
        vm((pair, tokens, features), BF16),
        vm((pair, tokens, features), F32),
        vm((pair, tokens, features), F32),
        vm((tokens, span), BF16),
        vm((pair, tokens, head), F32),
        vm((pair, tokens, 1), F32),
        vm((tokens, 3 * span), BF16),
        vm((2, pair, head, features), F32),
        vm((2, pair, head, features), BF16),
        vm((2, n_sub, pair, piece, features), BF16),
        vm((2, pair, head, features), BF16),
        vm((2, 8, features), F32),
        vm((2, n_sub - 1, 8, features), F32),
        vm((chips, cuts, 2 * block, width // cuts), F32),
        vm((chips, block, width), BF16),
        vm((chips, block, width), BF16),
        vm((chips - 1, block, width), BF16),
        vm((chips - 1, block, width), BF16),
        dma((7,)),
        dma((2 * chips - 1,)), dma((2 * chips - 1,)),
        dma((n_seq - 1,)), dma((n_seq - 1,)),
        dma((3, n_sub - 1)), dma((3, n_sub)), dma((3,)),
        dma((3, n_sub - 1, n_grp - 1)), dma((3, n_sub - 1, n_grp - 1)),
        dma((2, 2, n_sub - 1)), dma((2, 2, n_sub)),
        dma((2, n_sub - 1)), dma((2, n_sub - 1)),
        dma((chips, cuts)), dma((chips, cuts)),
        dma((chips - 1, cuts)), dma((chips - 1, cuts)),
    ]
    loss_scale = math.sqrt(block * n_seq * n_sub)
    return pl.pallas_call(
        functools.partial(kernel, n_grp, n_seq, n_sub, loss_scale, cuts, STOP),
        out_shape=jax.ShapeDtypeStruct((block, width), BF16),
        in_specs=[pl.BlockSpec(memory_space=pl.ANY)] * 7,
        out_specs=pl.BlockSpec(memory_space=pltpu.VMEM),
        scratch_shapes=scratch,
        compiler_params=pltpu.CompilerParams(
            collective_id=0, has_side_effects=True, vmem_limit_bytes=48 * 1024 * 1024
        ),
    )(*[
        pltpu.with_memory_space_constraint(array, pltpu.HBM)
        for array in (
            events, offsets.reshape(1, block), cotangent, query_weight, key_weight, value_weight, omega
        )
    ])


def solution(mesh):
    in_specs = (
        P(("grp", "seq", "sub"), None),
        P(("grp", "seq", "sub")),
        P(("grp", "seq", "sub"), None),
        P("sub", None),
        P("sub", None),
        P("sub", None),
        P(),
    )
    out_specs = P(("grp", "seq", "sub"), None)
    n_grp, n_seq, n_sub = (mesh.shape[name] for name in ("grp", "seq", "sub"))

    def body(*args):
        if fits(n_grp, n_seq, n_sub, *args):
            return fused(n_grp, n_seq, n_sub, *args)
        return local(*args)

    return jax.shard_map(body, mesh=mesh, in_specs=in_specs, out_specs=out_specs, check_vma=False)
```

```python
import functools
import math

import jax
import jax.numpy as jnp
from jax import lax
from jax.experimental import pallas as pl
from jax.experimental.pallas import tpu as pltpu
from jax.sharding import PartitionSpec as P


def encode(events, offsets):
    half_width = events.shape[1] // 2
    indices = jnp.arange(half_width, dtype=jnp.float32)
    frequency = jnp.exp(indices * (-2.0 * math.log(10000.0) / events.shape[1]))
    angles = offsets.astype(jnp.float32)[:, None] * frequency[None, :]
    encoding = jnp.concatenate([jnp.sin(angles), jnp.cos(angles)], axis=1)
    return (events.astype(jnp.float32) + encoding).astype(jnp.bfloat16)


def split_heads(matrix, head_count):
    return matrix.reshape(matrix.shape[0], head_count, matrix.shape[1] // head_count)


def transposed(left, weight):
    return lax.dot_general(
        left, weight, (((1,), (1,)), ((), ())), preferred_element_type=jnp.float32
    )


def local(events, offsets, cotangent, query_weight, key_weight, value_weight, omega):
    widened_rows = jnp.float32
    head_count = omega.shape[0]
    local_rows = events.shape[0]
    model_width = events.shape[1]
    all_tokens = local_rows * lax.axis_size("seq") * lax.axis_size("sub")
    loss_scale = math.sqrt(all_tokens)
    inputs = encode(events, offsets)
    gathered = (
        lax.all_gather(query_weight, "sub", axis=0, tiled=True),
        lax.all_gather(key_weight, "sub", axis=0, tiled=True),
        lax.all_gather(value_weight, "sub", axis=0, tiled=True),
    )
    queries, key_act, value_act = [
        jnp.dot(inputs, weight, preferred_element_type=widened_rows).astype(jnp.bfloat16)
        for weight in gathered
    ]
    query_pre = jnp.einsum(
        "thd,hdm->thm", split_heads(queries, head_count), omega, preferred_element_type=widened_rows
    )
    key_pre = jnp.einsum(
        "thd,hdm->thm", split_heads(key_act, head_count), omega, preferred_element_type=widened_rows
    )
    query_feature_map = jax.nn.softplus(query_pre).astype(jnp.bfloat16)
    key_feature_map = jax.nn.softplus(key_pre).astype(jnp.bfloat16)
    value_per_head = split_heads(value_act, head_count)
    local_digest = jnp.einsum(
        "reb,rec->ebc", key_feature_map, value_per_head, preferred_element_type=widened_rows
    )
    local_total = jnp.sum(key_feature_map, axis=0, dtype=widened_rows)
    state_digest, key_total = lax.psum((local_digest, local_total), ("seq", "sub"))
    digest_halves = state_digest.astype(jnp.bfloat16)
    total_half = key_total.astype(jnp.bfloat16)
    numerator = jnp.einsum(
        "xls,lsk->xlk", query_feature_map, digest_halves, preferred_element_type=widened_rows
    )
    denom = jnp.einsum(
        "thm,hm->th", query_feature_map, total_half, preferred_element_type=widened_rows
    )
    attended = numerator / denom[..., None]
    upstream = split_heads(cotangent, head_count).astype(widened_rows) * loss_scale
    scaled_grad = upstream / denom[..., None]
    norm_grad = -jnp.sum(scaled_grad * attended, axis=-1)
    scaled_halves = scaled_grad.astype(jnp.bfloat16)
    norm_half = norm_grad.astype(jnp.bfloat16)
    local_gradient = jnp.einsum(
        "reb,rec->ebc", query_feature_map, scaled_halves, preferred_element_type=widened_rows
    )
    local_norm = jnp.einsum(
        "thm,th->hm", query_feature_map, norm_half, preferred_element_type=widened_rows
    )
    summary_grad, overall_gradient = lax.psum((local_gradient, local_norm), ("seq", "sub"))
    gradient_halves = summary_grad.astype(jnp.bfloat16)
    query_feature_gradient = jnp.einsum(
        "pfy,fly->pfl", scaled_halves, digest_halves, preferred_element_type=widened_rows
    )
    query_feature_gradient = (
        query_feature_gradient + norm_grad[..., None] * total_half.astype(widened_rows)[None]
    )
    key_feature_gradient = (
        jnp.einsum(
            "pfy,fly->pfl", value_per_head, gradient_halves, preferred_element_type=widened_rows
        )
        + overall_gradient[None]
    )
    value_gradient = jnp.einsum(
        "xls,lsk->xlk", key_feature_map, gradient_halves, preferred_element_type=widened_rows
    ).astype(jnp.bfloat16)
    query_pre_grad = (query_feature_gradient * jax.nn.sigmoid(query_pre)).astype(jnp.bfloat16)
    key_pre_grad = (key_feature_gradient * jax.nn.sigmoid(key_pre)).astype(jnp.bfloat16)
    query_grad = jnp.einsum(
        "thm,hdm->thd", query_pre_grad, omega, preferred_element_type=widened_rows
    ).astype(jnp.bfloat16)
    key_grad = jnp.einsum(
        "thm,hdm->thd", key_pre_grad, omega, preferred_element_type=widened_rows
    ).astype(jnp.bfloat16)
    query_flat = query_grad.reshape(local_rows, model_width)
    key_flat = key_grad.reshape(local_rows, model_width)
    value_flat = value_gradient.reshape(local_rows, model_width)
    summed = transposed(query_flat, gathered[0])
    summed = summed + transposed(key_flat, gathered[1])
    summed = summed + transposed(value_flat, gathered[2])
    return summed.astype(jnp.bfloat16)


F32, BF16 = jnp.float32, jnp.bfloat16
MESH = pl.DeviceIdType.MESH
NN = (((1,), (0,)), ((), ()))
NT = (((1,), (1,)), ((), ()))
TN = (((0,), (0,)), ((), ()))


def mul(left, right, dims):
    return lax.dot_general(left, right, dims, preferred_element_type=F32)


def activations(pre):
    small = jnp.exp(-jnp.abs(pre))
    feature = jnp.maximum(pre, 0.0) + jnp.log1p(small)
    sigmoid = jnp.where(pre >= 0.0, 1.0, small) / (1.0 + small)
    return feature.astype(BF16), sigmoid


def encoded(events, offsets):
    block, width = events.shape
    row = lax.broadcasted_iota(jnp.int32, (block, block), 0)
    lane = lax.broadcasted_iota(jnp.int32, (block, block), 1)
    spread = jnp.broadcast_to(offsets.astype(F32), (block, block))
    column = jnp.sum(jnp.where(row == lane, spread, 0.0), axis=1, keepdims=True)
    indices = lax.broadcasted_iota(jnp.int32, (1, width // 2), 1).astype(F32)
    frequency = jnp.exp(indices * (-2.0 * math.log(10000.0) / width))
    angles = column * frequency
    turns = jnp.floor(angles * (2.0 / math.pi) + 0.5)
    rest = angles - turns * 1.5703125
    rest = rest - turns * 4.837512969970703125e-4
    rest = rest - turns * 7.54978994e-8
    square = rest * rest
    sine = ((-1.9515295891e-4 * square + 8.3321608736e-3) * square - 1.6666654611e-1) * square * rest + rest
    cosine = ((2.443315711809948e-5 * square - 1.388731625493765e-3) * square + 4.166664568298827e-2)
    cosine = cosine * square * square - 0.5 * square + 1.0
    halves = jnp.floor(turns * 0.5)
    odd = turns - 2.0 * halves
    sign = 1.0 - 2.0 * (halves - 2.0 * jnp.floor(halves * 0.5))
    swap = odd > 0.5
    sines = jnp.where(swap, cosine, sine) * sign
    cosines = jnp.where(swap, -sine, cosine) * sign
    wide = events.astype(F32)
    return (
        (wide[:, : width // 2] + sines).astype(BF16),
        (wide[:, width // 2 :] + cosines).astype(BF16),
    )


def kernel(
    n_grp, n_seq, n_sub, loss_scale, cuts, stop,
    ev_ref, off_ref, cot_ref, wq_ref, wk_ref, wv_ref, omega_ref, out_ref,
    ev, off, xall, call, wall, om, act, va, qf, kf, qs, ks, sc, inv, nrm, gr,
    acc, part, rsin, half, tot, totin, keep, mo, mi, ro, ri,
    local_sem, xs, xr, cs, cr, ws, wr, hs, ys, yr, ss, sr, ts, tr, ms, mr, os_, or_,
):
    grp, seq, sub = lax.axis_index("grp"), lax.axis_index("seq"), lax.axis_index("sub")
    chips = n_seq // 2
    chip, core = seq // 2, seq % 2
    mate = 2 * chip + 1 - core
    block, width = ev_ref.shape
    pair, head, features = om.shape
    span = pair * head
    rows = wq_ref.shape[0]
    share = rows // n_grp
    piece = head // n_sub
    slab = width // cuts
    edge, middle, far = range(n_sub - 1)

    def in_row(index):
        return {"grp": grp, "seq": index, "sub": sub}

    def in_column(index):
        return {"grp": grp, "seq": seq, "sub": index}

    def in_group(index):
        return {"grp": index, "seq": seq, "sub": sub}

    def seat(d, which):
        return 2 * ((chip + d) % chips) + which

    def rows_of(index, size):
        return pl.ds(pl.multiple_of(index * size, size), size)

    def nearest(k):
        found = 0
        for s in range(n_sub):
            others = sorted((abs(s - t), -abs(2 * t - n_sub + 1), t) for t in range(n_sub) if t != s)
            found = found + jnp.where(sub == s, others[k][2], 0)
        return found

    near = [nearest(k) for k in range(n_sub - 1)]
    unsent, unread, pending = [], [], {}

    def remote(src, dst, send_sem, recv_sem, device):
        return pltpu.make_async_remote_copy(
            src_ref=src, dst_ref=dst, send_sem=send_sem, recv_sem=recv_sem,
            device_id=device, device_id_type=MESH,
        )

    def send(src, dst, send_sem, recv_sem, device):
        copy = remote(src, dst, send_sem, recv_sem, device)
        copy.start()
        unsent.append((copy, None))
        unread.append(copy)
        return copy

    def send_some(condition, src, dst, send_sem, recv_sem, device):
        copy = remote(src, dst, send_sem, recv_sem, device)
        if condition is None:
            copy.start()
        else:
            pl.when(condition)(copy.start)
        unsent.append((copy, condition))

    def arrive(copy):
        copy.wait_recv()
        unread[:] = [other for other in unread if other is not copy]

    def drain():
        for key in list(pending):
            settle(*key)
        for copy in unread:
            copy.wait_recv()
        for copy, condition in unsent:
            if condition is None:
                copy.wait_send()
            else:
                pl.when(condition)(copy.wait_send)

    barrier = pltpu.get_barrier_semaphore()
    for d in range(1, n_seq):
        pl.semaphore_signal(barrier, inc=1, device_id=in_row((seq + d) % n_seq), device_id_type=MESH)
    for d in range(1, n_sub):
        pl.semaphore_signal(barrier, inc=1, device_id=in_column((sub + d) % n_sub), device_id_type=MESH)
    for d in range(1, n_grp):
        pl.semaphore_signal(barrier, inc=1, device_id=in_group((grp + d) % n_grp), device_id_type=MESH)

    weights = (wk_ref, wv_ref, wq_ref)
    mine = rows_of(seq, block)
    columns = rows_of(seq, span)

    def local(src, dst, index):
        copy = pltpu.make_async_copy(src, dst, local_sem.at[index])
        copy.start()
        return copy

    later = [
        local(w.at[:, columns], wall.at[rows_of(sub, rows), pl.ds(i * span, span)], 2 + i)
        for i, w in enumerate(weights)
    ]
    first = [local(ev_ref, ev, 0), local(off_ref, off, 1)]
    later.append(local(omega_ref.at[rows_of(seq, pair)], om, 5))
    later.append(local(cot_ref.at[:, columns], call.at[mine], 6))
    later[0].wait()
    pl.semaphore_wait(barrier, n_seq + n_sub + n_grp - 3)

    def slot(source, i):
        return wall.at[
            pl.ds(pl.multiple_of(source * rows + grp * share, share), share), pl.ds(i * span, span)
        ]

    inner = (sub > 0) & (sub < n_sub - 1)
    outer = jnp.logical_not(inner)

    def slice_copy(i, k):
        return remote(
            slot(sub, i), slot(sub, i),
            ws.at[i, k], wr.at[i, sub], in_column(near[k]),
        )

    @pl.when(inner)
    def _():
        slice_copy(0, edge).start()
        slice_copy(0, middle).start()
        slice_copy(0, far).start()

    @pl.when(outer)
    def _():
        slice_copy(0, middle).start()
        slice_copy(0, far).start()
        slice_copy(0, edge).start()

    for copy in later[1:3]:
        copy.wait()

    @pl.when(inner)
    def _():
        slice_copy(1, edge).start()
        slice_copy(2, edge).start()
        slice_copy(1, far).start()
        slice_copy(1, middle).start()
        slice_copy(2, far).start()
        slice_copy(2, middle).start()

    @pl.when(outer)
    def _():
        slice_copy(1, edge).start()
        slice_copy(1, middle).start()

    for i in range(3):
        unsent.append((slice_copy(i, far), inner if i else None))
        unsent.append((slice_copy(i, middle), None))
        unsent.append((slice_copy(i, edge), None))

    for copy in first:
        copy.wait()
    low, high = encoded(ev[...], off[...])
    xall[mine, : width // 2] = low
    xall[mine, width // 2 :] = high
    xcopies = {}
    for d in range(1, chips):
        xcopies[d] = send(xall.at[mine], xall.at[mine], xs.at[d], xr.at[d], in_row(seat(d, core)))
    xcopies[0] = send(xall.at[mine], xall.at[mine], xs.at[0], xr.at[0], in_row(mate))
    ccopies = []
    for d in range(1, n_seq):
        to = (seq + d) % n_seq
        ccopies.append(send(
            cot_ref.at[:, rows_of(to, span)], call.at[mine], cs.at[d - 1], cr.at[d - 1], in_row(to)
        ))
    xforward = []

    def forward_inputs():
        for d in range(1, chips):
            arrive(xcopies[d])
            at = rows_of((seq - 2 * d + n_seq) % n_seq, block)
            xforward.append(send(xall.at[at], xall.at[at], xs.at[chips + d - 1], xr.at[chips + d - 1], in_row(mate)))

    def relay_copy(i):
        at = slot(near[far], i)
        return remote(at, at, hs.at[i], wr.at[i, near[far]], in_column(near[edge]))

    def group_copies(i, k):
        at = slot(near[k], i)
        return [
            remote(at, at, ys.at[i, k, e - 1], yr.at[i, k, e - 1], in_group((grp + e) % n_grp))
            for e in range(1, n_grp)
        ]

    for i in range(3):
        if i:
            unsent.append((relay_copy(i), inner))
        for k in range(n_sub - 1):
            unsent.extend((copy, None) for copy in group_copies(i, k))

    def landed(i, k):
        at = slot(near[k], i)
        remote(at, at, ws.at[i, k], wr.at[i, near[k]], in_column(near[k])).wait_recv()

    def share_out(i, k):
        for copy in group_copies(i, k):
            copy.start()

    def pass_on(i, k):
        landed(i, k)
        share_out(i, k)

    def steps(inside, outside):
        pl.when(inner)(inside)
        pl.when(outer)(outside)

    def group_done(i):
        for k in range(n_sub - 1):
            for copy in group_copies(i, k):
                copy.wait_recv()

    def relay_on(i):
        landed(i, far)
        relay_copy(i).start()

    def first_inner():
        pass_on(0, far)
        pass_on(0, edge)
        pass_on(0, middle)
        pass_on(1, edge)
        relay_on(1)
        share_out(1, far)

    def first_outer():
        pass_on(0, edge)
        pass_on(0, far)
        pass_on(1, edge)
        pass_on(0, middle)
        slice_copy(2, edge).start()
        slice_copy(2, middle).start()
        pass_on(2, edge)

    def second_outer():
        pass_on(1, middle)

    def third_inner():
        relay_on(2)
        pass_on(1, middle)
        pass_on(2, edge)
        share_out(2, far)

    def third_outer():
        pass_on(1, far)

    def fourth_inner():
        pass_on(2, middle)

    def fourth_outer():
        pass_on(2, middle)
        pass_on(2, far)

    def project(i, target):
        target[...] = mul(xall[...], wall[:, i * span : (i + 1) * span], NN).astype(BF16)

    def featurize(feature, sigmoid, some):
        def step(b, carry):
            at = rows_of(b, block)
            for h in some:
                pre = mul(act[at, h * head : (h + 1) * head], om[h], NN)
                feature[h, at, :], sigmoid[h, at, :] = activations(pre)
            return carry

        lax.fori_loop(0, n_seq, step, 0, unroll=True)

    def start_total(a):
        copies = []
        for d in range(1, n_sub):
            copies.append(send(
                tot.at[a], totin.at[a, d - 1], ts.at[a, d - 1], tr.at[a, d - 1], in_column((sub + d) % n_sub)
            ))
        return copies

    def finish_total(a, copies):
        total = tot[a]
        for d in range(1, n_sub):
            arrive(copies[d - 1])
            total = total + totin[a, d - 1]
        return total

    def start_sum(a):
        part[a] = acc[a].astype(BF16)
        for k in reversed(range(n_sub - 1)):
            send_some(
                None, part.at[a, :, rows_of(near[k], piece)], rsin.at[a, sub],
                ss.at[a, 0, k], sr.at[a, 0, sub], in_column(near[k]),
            )
        pending[a, 0] = [rsin.at[a, source] for source in near]

    def middle_sum(a):
        own = rows_of(sub, piece)
        settle(a, 0)
        summed = acc[a, :, own, :]
        for source in near:
            summed = summed + rsin[a, source].astype(F32)
        half[a, :, own, :] = summed.astype(BF16)
        for k in reversed(range(n_sub - 1)):
            send_some(
                None, half.at[a, :, own], half.at[a, :, own],
                ss.at[a, 1, k], sr.at[a, 1, sub], in_column(near[k]),
            )
        pending[a, 1] = [half.at[a, :, rows_of(source, piece)] for source in near]

    def settle(a, stage):
        for k, dst in enumerate(pending.pop((a, stage))):
            remote(dst, dst, ss.at[a, stage, k], sr.at[a, stage, near[k]], in_column(near[k])).wait_recv()

    def summed_half(a, h):
        return half[a, h]

    def body():
        steps(first_inner, first_outer)
        forward_inputs()
        for copy in later[3:]:
            copy.wait()
        pl.when(outer)(second_outer)
        group_done(0)
        for copy in xforward:
            arrive(copy)
        arrive(xcopies[0])
        pl.when(inner)(third_inner)
        project(0, act)
        pl.when(outer)(third_outer)
        featurize(kf, ks, range(pair))
        steps(fourth_inner, fourth_outer)
        tot[...] = jnp.zeros_like(tot)
        for h in range(pair):
            tot[0, pl.ds(h, 1), :] = jnp.sum(kf[h].astype(F32), axis=0, keepdims=True)
        totals = start_total(0)
        group_done(1)
        if stop == 2:
            return
        project(1, va)
        for h in range(pair):
            acc[0, h] = mul(va[:, h * head : (h + 1) * head], kf[h], TN)
        start_sum(0)
        group_done(2)
        if stop == 3:
            return
        project(2, act)
        total_half = finish_total(0, totals).astype(BF16)
        for copy in ccopies:
            arrive(copy)
        for h in range(pair):
            featurize(qf, qs, [h])
            wide = jnp.broadcast_to(total_half[h : h + 1], (head, features))
            lanes = pl.ds(h * head, head)

            def scale(b, carry, h=h, wide=wide, lanes=lanes):
                at = rows_of(b, block)
                inverse = 1.0 / mul(qf[h, at, :], wide, NT)
                inv[h, at, :] = inverse
                sc[at, lanes] = (call[at, lanes].astype(F32) * loss_scale * inverse).astype(BF16)
                return carry

            lax.fori_loop(0, n_seq, scale, 0, unroll=True)
            acc[1, h] = mul(sc[:, lanes], qf[h], TN)
        start_sum(1)
        middle_sum(0)
        middle_sum(1)
        if stop == 5:
            return
        settle(0, 1)
        for h in range(pair):
            lanes = pl.ds(h * head, head)
            summary = half[0, h]

            def norms(b, carry, h=h, lanes=lanes, summary=summary):
                at = rows_of(b, block)
                inverse = inv[h, at, :]
                attended = mul(qf[h, at, :], summary, NT) * inverse
                scaled = call[at, lanes].astype(F32) * loss_scale * inverse
                nrm[h, at, :] = -jnp.sum(scaled * attended, axis=-1, keepdims=True)
                return carry

            lax.fori_loop(0, n_seq, norms, 0, unroll=True)
            tot[1, pl.ds(h, 1), :] = jnp.sum(
                qf[h].astype(F32) * nrm[h].astype(BF16).astype(F32), axis=0, keepdims=True
            )
        grads = start_total(1)
        if stop == 6:
            return
        for h in range(pair):
            lanes = pl.ds(h * head, head)
            summary = half[0, h]
            weight = total_half[h : h + 1].astype(F32)

            def query_grads(b, carry, h=h, lanes=lanes, summary=summary, weight=weight):
                at = rows_of(b, block)
                grad = mul(sc[at, lanes], summary, NN) + nrm[h, at, :] * weight
                grad = (grad * qs[h, at, :]).astype(BF16)
                gr[at, pl.ds(2 * span + h * head, head)] = mul(grad, om[h], NT).astype(BF16)
                return carry

            lax.fori_loop(0, n_seq, query_grads, 0, unroll=True)
        def chip_rows(d):
            return pl.ds(pl.multiple_of((chip + d) % chips * 2 * block, 2 * block), 2 * block)

        for d in range(1, chips):
            for c in range(cuts):
                keep[d, c] = mul(
                    gr[chip_rows(d), 2 * span :], wall[c * slab : (c + 1) * slab, 2 * span :], NT
                )
        def value_grads(d, h):
            at = chip_rows(d)
            gr[at, pl.ds(span + h * head, head)] = mul(kf[h, at, :], summed_half(1, h), NT).astype(BF16)

        def key_grads(d, h):
            at = chip_rows(d)
            lanes = pl.ds(h * head, head)
            grad = mul(va[at, lanes], summed_half(1, h), NN) + total_grad[h : h + 1]
            grad = (grad * ks[h, at, :]).astype(BF16)
            gr[at, pl.ds(h * head, head)] = mul(grad, om[h], NT).astype(BF16)

        settle(1, 1)
        for h in range(pair):
            for d in range(1, chips):
                value_grads(d, h)
        for d in range(1, chips):
            for c in range(cuts):
                keep[d, c] = keep[d, c] + mul(
                    gr[chip_rows(d), span : 2 * span], wall[c * slab : (c + 1) * slab, span : 2 * span], NT
                )
        total_grad = finish_total(1, grads)
        for h in range(pair):
            for d in range(1, chips):
                key_grads(d, h)
        if stop in (7, 8):
            return

        def to_mate(d):
            copies = []
            for c in range(cuts):
                at = pl.ds(c * slab, slab)
                columns_of = slice(0, span if d else 3 * span)
                grads = mul(gr[chip_rows(d), columns_of], wall[c * slab : (c + 1) * slab, columns_of], NT)
                keep[d, c] = keep[d, c] + grads if d else grads
                mo[d, :, at] = keep[d, c, rows_of(1 - core, block), :].astype(BF16)
                copies.append(send(
                    mo.at[d, :, at], mi.at[d, :, at], ms.at[d, c], mr.at[d, c], in_row(mate)
                ))
            return copies

        for_mate = {d: to_mate(d) for d in range(1, chips)}
        outward = {}
        for d in range(1, chips):
            for c in range(cuts):
                at = pl.ds(c * slab, slab)
                arrive(for_mate[d][c])
                ro[d - 1, :, at] = (
                    keep[d, c, rows_of(core, block), :] + mi[d, :, at].astype(F32)
                ).astype(BF16)
                outward[d, c] = send(
                    ro.at[d - 1, :, at], ri.at[d - 1, :, at], os_.at[d - 1, c], or_.at[d - 1, c],
                    in_row(seat(d, core)),
                )
        for h in range(pair):
            value_grads(0, h)
            key_grads(0, h)
        for_mate[0] = to_mate(0)
        for c in range(cuts):
            at = pl.ds(c * slab, slab)
            arrive(for_mate[0][c])
            summed = keep[0, c, rows_of(core, block), :] + mi[0, :, at].astype(F32)
            for d in range(1, chips):
                arrive(outward[d, c])
                summed = summed + ri[d - 1, :, at].astype(F32)
            out_ref[:, at] = summed.astype(BF16)

    body()
    drain()


def fits(n_grp, n_seq, n_sub, events, offsets, cotangent, query_weight, key_weight, value_weight, omega):
    heads, head, features = omega.shape
    block, width = events.shape
    pair = heads // n_seq
    rows = query_weight.shape[0]
    return (
        n_seq >= 4 and n_seq % 2 == 0 and n_grp > 1 and n_sub == 4 and heads % n_seq == 0 and pair <= 8
        and head % 128 == 0 and features % 128 == 0 and block % 128 == 0 and width % 512 == 0
        and head % (16 * n_sub) == 0 and rows % (16 * n_grp) == 0
        and n_seq * block <= 1024 and pair * features <= 512 and width <= 1024
    )


STOP = 99


def fused(n_grp, n_seq, n_sub, events, offsets, cotangent, query_weight, key_weight, value_weight, omega):
    block, width = events.shape
    heads, head, features = omega.shape
    tokens = n_seq * block
    pair = heads // n_seq
    span = pair * head
    piece = head // n_sub
    chips = n_seq // 2
    cuts = 1
    vm = pltpu.VMEM
    dma = pltpu.SemaphoreType.DMA
    scratch = [
        vm((block, width), BF16),
        vm((1, block), jnp.int32),
        vm((tokens, width), BF16),
        vm((tokens, span), BF16),
        vm((width, 3 * span), BF16),
        vm((pair, head, features), BF16),
        vm((tokens, span), BF16),
        vm((tokens, span), BF16),
        vm((pair, tokens, features), BF16),
        vm((pair, tokens, features), BF16),
        vm((pair, tokens, features), F32),
        vm((pair, tokens, features), F32),
        vm((tokens, span), BF16),
        vm((pair, tokens, head), F32),
        vm((pair, tokens, 1), F32),
        vm((tokens, 3 * span), BF16),
        vm((2, pair, head, features), F32),
        vm((2, pair, head, features), BF16),
        vm((2, n_sub, pair, piece, features), BF16),
        vm((2, pair, head, features), BF16),
        vm((2, 8, features), F32),
        vm((2, n_sub - 1, 8, features), F32),
        vm((chips, cuts, 2 * block, width // cuts), F32),
        vm((chips, block, width), BF16),
        vm((chips, block, width), BF16),
        vm((chips - 1, block, width), BF16),
        vm((chips - 1, block, width), BF16),
        dma((7,)),
        dma((2 * chips - 1,)), dma((2 * chips - 1,)),
        dma((n_seq - 1,)), dma((n_seq - 1,)),
        dma((3, n_sub - 1)), dma((3, n_sub)), dma((3,)),
        dma((3, n_sub - 1, n_grp - 1)), dma((3, n_sub - 1, n_grp - 1)),
        dma((2, 2, n_sub - 1)), dma((2, 2, n_sub)),
        dma((2, n_sub - 1)), dma((2, n_sub - 1)),
        dma((chips, cuts)), dma((chips, cuts)),
        dma((chips - 1, cuts)), dma((chips - 1, cuts)),
    ]
    loss_scale = math.sqrt(block * n_seq * n_sub)
    return pl.pallas_call(
        functools.partial(kernel, n_grp, n_seq, n_sub, loss_scale, cuts, STOP),
        out_shape=jax.ShapeDtypeStruct((block, width), BF16),
        in_specs=[pl.BlockSpec(memory_space=pl.ANY)] * 7,
        out_specs=pl.BlockSpec(memory_space=pltpu.VMEM),
        scratch_shapes=scratch,
        compiler_params=pltpu.CompilerParams(
            collective_id=0, has_side_effects=True, vmem_limit_bytes=48 * 1024 * 1024
        ),
    )(*[
        pltpu.with_memory_space_constraint(array, pltpu.HBM)
        for array in (
            events, offsets.reshape(1, block), cotangent, query_weight, key_weight, value_weight, omega
        )
    ])


def solution(mesh):
    in_specs = (
        P(("grp", "seq", "sub"), None),
        P(("grp", "seq", "sub")),
        P(("grp", "seq", "sub"), None),
        P("sub", None),
        P("sub", None),
        P("sub", None),
        P(),
    )
    out_specs = P(("grp", "seq", "sub"), None)
    n_grp, n_seq, n_sub = (mesh.shape[name] for name in ("grp", "seq", "sub"))

    def body(*args):
        if fits(n_grp, n_seq, n_sub, *args):
            return fused(n_grp, n_seq, n_sub, *args)
        return local(*args)

    return jax.shard_map(body, mesh=mesh, in_specs=in_specs, out_specs=out_specs, check_vma=False)
```
